32 devices in a mesh: groups: 2 (over x), gx: 16 (over z, y, core).
Axes of the slice: x: 2, y: 2, z: 4, core: 2. Of those that a mesh axis runs over, the one named last changes fastest.
Arguments:
- features: bfloat16 [128, 8, 8, 8, 128], P(('groups', 'gx')), parts along dimension 0, may hold values from -6 to 6
- fine_nbr: int32 [128, 27], P(('groups', 'gx')), parts along dimension 0, may hold values from -1 to 3, as said below
- fine_send: int32 [32, 2, 4], P(('groups', 'gx')), parts along dimension 0, may hold values from -1 to 3, as said below
- fine_parent: int32 [128], P(('groups', 'gx')), parts along dimension 0, may hold values from -1 to 127, as said below
- coarse_child: int32 [32, 8], P(('groups', 'gx')), parts along dimension 0, may hold values from -1 to 63, as said below
- coarse_nbr: int32 [32, 27], P(('groups', 'gx')), parts along dimension 0, may hold values from -1 to 15, as said below
- enc_fine_w: bfloat16 [27, 128, 128], replicated, may hold values from -0.15625 to 0.15625
- enc_coarse_w: bfloat16 [27, 128, 128], replicated, may hold values from -0.15625 to 0.15625
- dec_coarse_w: bfloat16 [27, 128, 128], replicated, may hold values from -0.15625 to 0.15625
- dec_fine_w: bfloat16 [27, 128, 128], replicated, may hold values from -0.15625 to 0.15625
Outputs:
- fine_out: bfloat16 [128, 8, 8, 8, 128], P(('groups', 'gx')), parts along dimension 0
The draws below stay inside these ranges and needn't reach their ends.
There are 2 independent parts, one for each index of `groups`. The reference program is written for one: setup_inputs(seed, part) draws one part's arguments, and reference() takes and returns one part's arrays. A program takes and returns all parts, laid end to end along the dimension named above; an argument that names none is the same for every part. Nothing has to cross between parts.
Inputs may be any that keep to these rules, and one draw needn't show every extreme that they name: `fine_nbr`: entry t of a fine slot on gx device d names the slot, on device d + dx, of the brick at brick offset (dx, dy, dz), or is -1 where there is none. A slot whose entry 13 is -1 holds no brick and all its entries are -1; entry 13 of a brick is its own slot. Adjacency is symmetric. `fine_send`: on device d, entry s of row 0 is s when slot s holds a brick with a neighbour on device d + 1, else -1; row 1 likewise for device d - 1. `fine_parent`: 8 g + o for a brick whose parent is coarse slot g at octant o, -1 for slots without a brick. Coarse slot g is held by gx device g, which lies in the same aligned group of four gx devices as the child's device. `coarse_child`: entry o of coarse slot g is the fine slot f with fine_parent[f] = 8 g + o, or -1 where there is none. `coarse_nbr`: entry t (taps ordered as for fine_nbr) is the coarse slot of the neighbouring coarse brick, or -1 where there is none; entry 13 is the brick's own slot; every neighbour is held by a gx device of the same or an adjacent aligned group of four, and neighbours with dx = 0 by a device of the same aligned group of four.
All inputs are finite; a program needn't handle non-finite values.
Results may differ from the reference program's by a relative error of at most 0.01.
Values may be sent and summed in bfloat16 or wider, within the bound.
A program may use at most 128 MiB of HBM per device.

```python
import jax
import jax.numpy as jnp
import numpy as np
from jax import lax

C = 128
EDGE = 8
FB = 4
CB = 1
NF = 64
NC = 16
N_GX = 16


OFFSETS = (-1, 0, 1)


def geometry(key):
    keys = jax.random.split(jax.random.fold_in(key, 7), 6)
    columns = N_GX
    depth = FB // 2
    places = 2 * FB
    tap_x = jnp.asarray(np.repeat(np.array(OFFSETS), 9), jnp.int32)
    tap_y = jnp.asarray(np.tile(np.repeat(np.array(OFFSETS), 3), 3), jnp.int32)
    tap_z = jnp.asarray(np.tile(np.array(OFFSETS), 9), jnp.int32)
    counts = jax.random.randint(keys[0], (columns,), FB // 2, FB + 1)
    busiest = jax.random.randint(keys[1], (), 0, columns)
    counts = jnp.where(jnp.arange(columns) == busiest, FB, counts)
    place_order = jax.vmap(lambda sub: jax.random.permutation(sub, places))(jax.random.split(keys[2], columns))
    slot_order = jax.vmap(lambda sub: jax.random.permutation(sub, FB))(jax.random.split(keys[3], columns))
    rank = jnp.arange(FB, dtype=jnp.int32)
    live_place = jnp.where(rank[None, :] < counts[:, None], place_order[:, :FB], -1).astype(jnp.int32)
    column_ids = jnp.arange(columns, dtype=jnp.int32)[:, None]
    slot_place = jnp.full((columns, FB), -1, jnp.int32).at[column_ids, slot_order].set(live_place)
    target = jnp.where(slot_place >= 0, slot_place, places)
    place_slot = jnp.full((columns, places + 1), -1, jnp.int32).at[column_ids, target].set(jnp.broadcast_to(rank, (columns, FB)))[:, :places]
    live = slot_place >= 0
    fine_y = jnp.where(live, slot_place // depth, 0)
    fine_z = jnp.where(live, slot_place % depth, 0)
    near_x = column_ids[:, :, None] + tap_x
    near_y = fine_y[:, :, None] + tap_y
    near_z = fine_z[:, :, None] + tap_z
    inside = live[:, :, None] & (near_x >= 0) & (near_x < columns) & (near_y >= 0) & (near_y < 4)
    inside = inside & (near_z >= 0) & (near_z < depth)
    found = place_slot[jnp.clip(near_x, 0, columns - 1), jnp.clip(near_y, 0, 3) * depth + jnp.clip(near_z, 0, depth - 1)]
    fine_nbr = jnp.where(inside, found, -1).astype(jnp.int32)
    upward = jnp.any(fine_nbr[:, :, 18:] >= 0, axis=-1)
    downward = jnp.any(fine_nbr[:, :, :9] >= 0, axis=-1)
    fine_send = jnp.stack([jnp.where(upward, rank, -1), jnp.where(downward, rank, -1)], axis=1).astype(jnp.int32)
    quads = columns // 4
    coarse_depth = FB // 4
    coarse_order = jax.vmap(lambda sub: jax.random.permutation(sub, FB))(jax.random.split(keys[4], quads))

    def coarse_slot(coarse_x, coarse_y, coarse_z):
        local = coarse_x % 2 * (FB // 2) + coarse_y * coarse_depth + coarse_z
        return coarse_x // 2 * FB + coarse_order[coarse_x // 2, local]
    parent_x = column_ids // 2
    parent = coarse_slot(jnp.broadcast_to(parent_x, (columns, FB)), fine_y // 2, fine_z // 2)
    octant = column_ids % 2 * 4 + fine_y % 2 * 2 + fine_z % 2
    fine_parent = jnp.where(live, parent * 8 + octant, -1).astype(jnp.int32).reshape(NF)
    dump = NC * 8
    coarse_child = jnp.full((NC * 8 + 1,), -1, jnp.int32).at[jnp.where(fine_parent >= 0, fine_parent, dump)].set(jnp.arange(NF, dtype=jnp.int32))[:NC * 8].reshape(NC, 8)
    width_x = columns // 2
    grid_x = jnp.broadcast_to(jnp.arange(width_x, dtype=jnp.int32)[:, None, None], (width_x, 2, coarse_depth))
    grid_y = jnp.broadcast_to(jnp.arange(2, dtype=jnp.int32)[None, :, None], (width_x, 2, coarse_depth))
    grid_z = jnp.broadcast_to(jnp.arange(coarse_depth, dtype=jnp.int32)[None, None, :], (width_x, 2, coarse_depth))
    step_x = grid_x[..., None] + tap_x
    step_y = grid_y[..., None] + tap_y
    step_z = grid_z[..., None] + tap_z
    within = (step_x >= 0) & (step_x < width_x) & (step_y >= 0) & (step_y < 2) & (step_z >= 0) & (step_z < coarse_depth)
    neighbour = coarse_slot(jnp.clip(step_x, 0, width_x - 1), jnp.clip(step_y, 0, 1), jnp.clip(step_z, 0, coarse_depth - 1))
    neighbour = jnp.where(within, neighbour, -1).astype(jnp.int32).reshape(-1, 27)
    owners = coarse_slot(grid_x, grid_y, grid_z).reshape(-1)
    coarse_nbr = jnp.zeros((NC, 27), jnp.int32).at[owners].set(neighbour)
    return (fine_nbr.reshape(NF, 27), fine_send, fine_parent, coarse_child, coarse_nbr)


def draw_fine_nbr(key, part):
    return geometry(key)[0]


def draw_fine_send(key, part):
    return geometry(key)[1]


def draw_fine_parent(key, part):
    return geometry(key)[2]


def draw_coarse_child(key, part):
    return geometry(key)[3]


def draw_coarse_nbr(key, part):
    return geometry(key)[4]


def block_levels(key, extent, pieces, least, top_value):
    level, own = 1.0, jax.random.fold_in(key, 6)
    for axis_at, blocks in pieces:
        steps = jnp.exp(jax.random.uniform(jax.random.fold_in(own, axis_at), (blocks,), jnp.float32, least / len(pieces), top_value / len(pieces)))
        level = level * jnp.repeat(steps, extent[axis_at] // blocks).reshape([-1 if axis == axis_at else 1 for axis in range(len(extent))])
    return level


def scatter_about(stream_key, shape, scale, most, cuts=(), kind=jnp.bfloat16):
    values = jax.random.normal(stream_key, shape, jnp.float32) * scale
    if len(cuts) > 0:
        values = block_levels(stream_key, shape, cuts, -0.22, 0.18) * values
    return jnp.clip(values, min=-most, max=most).astype(kind)


def setup_inputs(seed: int = 0, part: int = 0) -> dict:
    seeds = jax.random.split(jax.random.key(seed), 11)
    part_keys = jax.random.split(jax.random.fold_in(seeds[10], part), 11)
    features = scatter_about(part_keys[0], (NF, EDGE, EDGE, EDGE, C), 1.0, 6.0, ((0, 16),))
    fine_nbr = draw_fine_nbr(jax.random.fold_in(jax.random.fold_in(seeds[10], part), 71), part)
    fine_send = draw_fine_send(jax.random.fold_in(jax.random.fold_in(seeds[10], part), 71), part)
    fine_parent = draw_fine_parent(jax.random.fold_in(jax.random.fold_in(seeds[10], part), 71), part)
    coarse_child = draw_coarse_child(jax.random.fold_in(jax.random.fold_in(seeds[10], part), 71), part)
    coarse_nbr = draw_coarse_nbr(jax.random.fold_in(jax.random.fold_in(seeds[10], part), 71), part)
    enc_fine_w = scatter_about(seeds[6], (27, C, C), (27 * C // 2) ** -0.5, 0.15625)
    enc_coarse_w = scatter_about(seeds[7], (27, C, C), (27 * C // 2) ** -0.5, 0.15625)
    dec_coarse_w = scatter_about(seeds[8], (27, C, C), (27 * C // 2) ** -0.5, 0.15625)
    dec_fine_w = scatter_about(seeds[9], (27, C, C), (27 * C // 2) ** -0.5, 0.15625)
    return dict(features=features, fine_nbr=fine_nbr, fine_send=fine_send, fine_parent=fine_parent, coarse_child=coarse_child, coarse_nbr=coarse_nbr, enc_fine_w=enc_fine_w, enc_coarse_w=enc_coarse_w, dec_coarse_w=dec_coarse_w, dec_fine_w=dec_fine_w)


OFFSETS = (-1, 0, 1)


def region(offset, edge):
    if offset < 0:
        return slice(edge - 1, edge)
    if offset == 0:
        return slice(0, edge)
    return slice(0, 1)


def assemble(tables, index, edge):
    layers = []
    for offset_x in OFFSETS:
        table = tables[offset_x + 1]
        rows = []
        for offset_y in OFFSETS:
            cells = []
            for offset_z in OFFSETS:
                tap = 9 * (offset_x + 1) + 3 * (offset_y + 1) + offset_z + 1
                piece = table[:, :, region(offset_y, edge), region(offset_z, edge), :]
                cells.append(jnp.take(piece, index[:, tap], axis=0))
            rows.append(jnp.concatenate(cells, axis=3))
        layers.append(jnp.concatenate(rows, axis=2))
    return jnp.concatenate(layers, axis=1)


def convolve(padded, weights, edge):
    count = padded.shape[0]
    width = padded.shape[-1]
    total = jnp.zeros((count * edge ** 3, width), jnp.float32)
    for first in range(3):
        columns = jnp.concatenate([padded[:, first:first + edge, second:second + edge, third:third + edge, :]
                                   for second in range(3) for third in range(3)], axis=-1)
        columns = columns.reshape(count * edge ** 3, 9 * width).astype(jnp.float32)
        kernel = weights[9 * first:9 * first + 9].reshape(9 * width, width).astype(jnp.float32)
        total = total + jnp.dot(columns, kernel, preferred_element_type=jnp.float32)
    return jax.nn.relu(total).astype(jnp.bfloat16).reshape(count, edge, edge, edge, width)


def layer(bricks, index, weights, block):
    edge = bricks.shape[1]
    width = bricks.shape[-1]
    table = jnp.concatenate([bricks, jnp.zeros((1,) + bricks.shape[1:], jnp.bfloat16)], axis=0)
    tables = [table[:, edge - 1:], table, table[:, :1]]
    blocks = index.reshape(-1, block, 27)
    result = lax.map(lambda part_index: convolve(assemble(tables, part_index, edge), weights, edge), blocks)
    return result.reshape(-1, edge, edge, edge, width)


def from_octants(blocks, half):
    count = blocks.shape[0]
    width = blocks.shape[-1]
    shaped = blocks.reshape(count, 2, 2, 2, half, half, half, width).transpose(0, 1, 4, 2, 5, 3, 6, 7)
    return shaped.reshape(count, 2 * half, 2 * half, 2 * half, width)


def to_octants(bricks, half):
    count = bricks.shape[0]
    width = bricks.shape[-1]
    shaped = bricks.reshape(count, 2, half, 2, half, 2, half, width).transpose(0, 1, 3, 5, 2, 4, 6, 7)
    return shaped.reshape(count * 8, half, half, half, width)


def reference(features, fine_nbr, fine_send, fine_parent, coarse_child, coarse_nbr,
              enc_fine_w, enc_coarse_w, dec_coarse_w, dec_fine_w):
    edge = features.shape[1]
    width = features.shape[-1]
    half = edge // 2
    tap_x = jnp.asarray(np.repeat(np.array(OFFSETS), 9), jnp.int32)
    slot = jnp.arange(NF, dtype=jnp.int32)
    device = slot // FB
    neighbour_device = device[:, None] + tap_x[None, :]
    target = neighbour_device * FB + fine_nbr
    row = jnp.where(tap_x > 0, 1, 0).astype(jnp.int32)[None, :]
    flat_send = fine_send.reshape(-1)
    listed = jnp.clip((neighbour_device * 2 + row) * FB + fine_nbr, 0, N_GX * 2 * FB - 1).astype(jnp.int32)
    valid = (fine_nbr >= 0) & ((tap_x[None, :] == 0) | (flat_send[listed] == fine_nbr))
    src_fine = jnp.where(valid, target, NF).astype(jnp.int32)

    enc_fine = layer(features, src_fine, enc_fine_w, FB)
    pooled = enc_fine.astype(jnp.float32).reshape(NF, half, 2, half, 2, half, 2, width).mean(axis=(2, 4, 6))
    pooled = pooled.astype(jnp.bfloat16)
    pooled_table = jnp.concatenate([pooled, jnp.zeros((1, half, half, half, width), jnp.bfloat16)], axis=0)
    child_index = jnp.where(coarse_child >= 0, coarse_child, NF).astype(jnp.int32)
    coarse_in = from_octants(pooled_table[child_index], half)

    src_coarse = jnp.where(coarse_nbr >= 0, coarse_nbr, NC).astype(jnp.int32)
    enc_coarse = layer(coarse_in, src_coarse, enc_coarse_w, CB)
    dec_coarse = layer(enc_coarse, src_coarse, dec_coarse_w, CB)

    octants = to_octants(dec_coarse, half)
    octant_table = jnp.concatenate([octants, jnp.zeros((1, half, half, half, width), jnp.bfloat16)], axis=0)
    parent_index = jnp.where(fine_parent >= 0, fine_parent, NC * 8).astype(jnp.int32)
    upsampled = octant_table[parent_index]
    upsampled = jnp.repeat(jnp.repeat(jnp.repeat(upsampled, 2, axis=1), 2, axis=2), 2, axis=3)
    dec_in = (enc_fine.astype(jnp.float32) + upsampled.astype(jnp.float32)).astype(jnp.bfloat16)
    return layer(dec_in, src_fine, dec_fine_w, FB)
```

```python
import functools

import jax
import jax.numpy as jnp
from jax import lax
from jax.experimental import pallas as pl
from jax.experimental.pallas import tpu as pltpu
from jax.sharding import PartitionSpec as P

F32 = jnp.float32
BF16 = jnp.bfloat16
LANES = 4
MESH = pl.DeviceIdType.MESH


def pick(offset, edge):
    if offset < 0:
        return slice(edge - 1, edge)
    if offset == 0:
        return slice(0, edge)
    return slice(0, 1)


def place(offset, edge, base):
    if offset < 0:
        return slice(base - 1, base)
    if offset == 0:
        return slice(base, base + edge)
    return slice(base + edge, base + edge + 1)


def kernel(
    n,
    fine_nbr_hbm,
    fine_send_hbm,
    fine_parent_hbm,
    child_hbm,
    nbr_hbm,
    feat_hbm,
    w1_hbm,
    w2_hbm,
    w3_hbm,
    w4_hbm,
    out_ref,
    fine_nbr,
    fine_send,
    fine_parent,
    child_ref,
    nbr_ref,
    feat,
    w1,
    w2,
    w3,
    w4,
    pad,
    cols,
    opened,
    table,
    enc,
    below,
    above,
    face_out,
    face_in,
    face_out2,
    face_in2,
    half_z,
    pooled,
    pooled_out,
    children,
    meta,
    meta_s,
    coarse,
    coarse2,
    low_x,
    high_x,
    side_out,
    side_in,
    side_out2,
    side_in2,
    spread,
    lifted,
    load_sem,
    small_sem,
    face_send_sem,
    face_recv_sem,
    pool_send_sem,
    pool_recv_sem,
    meta_send_sem,
    meta_recv_sem,
    side_send_sem,
    side_recv_sem,
    meta_sem,
):
    slots, edge = out_ref.shape[0], enc.shape[1]
    plane = edge * edge
    width = out_ref.shape[-1]
    half = edge // 2
    block = half**3
    per = child_ref.shape[0]
    bricks = LANES * per
    me = lax.axis_index("gx")
    member = lax.rem(me, LANES)
    group = lax.div(me, LANES)

    def peer(k):
        return me - member + (member ^ k)

    width = out_ref.shape[-1]
    loads = [[pltpu.make_async_copy(feat_hbm, feat, load_sem.at[0, 0])]]
    for i, (src, dst) in enumerate(
        ((w1_hbm, w1), (w2_hbm, w2), (w3_hbm, w3), (w4_hbm, w4))
    ):
        loads.append(
            [
                pltpu.make_async_copy(
                    src.at[dx], dst.at[:, dx * width : (dx + 1) * width], load_sem.at[i + 1, dx]
                )
                for dx in range(3)
            ]
        )
    small = [
        pltpu.make_async_copy(src, dst, small_sem.at[i])
        for i, (src, dst) in enumerate(
            (
                (fine_nbr_hbm, fine_nbr),
                (fine_send_hbm, fine_send),
                (fine_parent_hbm, fine_parent),
                (child_hbm, child_ref),
                (nbr_hbm, nbr_ref),
            )
        )
    ]
    for copy in loads[0]:
        copy.start()
    for copy in small:
        copy.start()
    for copies in loads[1:]:
        for copy in copies:
            copy.start()

    def loaded(i):
        for copy in loads[i]:
            copy.wait()

    has_prev, has_next = me > 0, me < n - 1
    has_down, has_up = me >= LANES, me < n - LANES
    barrier = pltpu.get_barrier_semaphore()

    def greet(other):
        pl.semaphore_signal(barrier, inc=1, device_id={"gx": other}, device_id_type=MESH)

    sides = (
        (has_prev & (member == 0), me - 1),
        (has_next & (member == LANES - 1), me + 1),
        (has_down, me - LANES),
        (has_up, me + LANES),
    )
    for k in range(1, LANES):
        greet(peer(k))
    peers = LANES - 1
    for there, other in sides:
        pl.when(there)(functools.partial(greet, other))
        peers = peers + jnp.where(there, 1, 0)

    def remote(src, dst, send, recv, other):
        return pltpu.make_async_remote_copy(
            src_ref=src,
            dst_ref=dst,
            send_sem=send,
            recv_sem=recv,
            device_id={"gx": other},
            device_id_type=MESH,
        )

    def face_copies(outgoing, incoming, phase):
        up = remote(
            outgoing.at[0],
            incoming.at[0],
            face_send_sem.at[phase, 0],
            face_recv_sem.at[phase, 0],
            me + 1,
        )
        down = remote(
            outgoing.at[1],
            incoming.at[1],
            face_send_sem.at[phase, 1],
            face_recv_sem.at[phase, 1],
            me - 1,
        )
        return up, down

    def start_pair(up, up_there, down, down_there):
        pl.when(up_there)(up.start)
        pl.when(down_there)(down.start)

    def finish_pair(up, up_there, down, down_there):
        @pl.when(down_there)
        def _():
            up.wait_recv()
            down.wait_send()

        @pl.when(up_there)
        def _():
            down.wait_recv()
            up.wait_send()


    cube = (edge, edge, edge, width)
    zero_brick = jnp.zeros(cube, F32)
    zero_plane = jnp.zeros((edge, edge, width), F32)
    table[slots] = zero_brick

    def stage_faces(outgoing, s):
        up_from = jnp.where(fine_send[0, s] >= 0, s, slots)
        down_from = jnp.where(fine_send[1, s] >= 0, s, slots)
        outgoing[0, s] = table[up_from, edge - 1].reshape(plane, width).astype(BF16)
        outgoing[1, s] = table[down_from, 0].reshape(plane, width).astype(BF16)

    for copy in small:
        copy.wait()
    meta[member, 0:per, 0 : child_ref.shape[1]] = child_ref[...]
    meta[member, per : 2 * per, 0 : nbr_ref.shape[1]] = nbr_ref[...]
    loaded(0)
    for s in range(slots):
        table[s] = feat[s].astype(F32).reshape(cube)
    for s in range(slots):
        stage_faces(face_out, s)
    halo1 = face_copies(face_out, face_in, 0)
    meta_copies = [
        remote(
            meta.at[member],
            meta.at[member],
            meta_send_sem.at[k - 1],
            meta_recv_sem.at[k - 1],
            peer(k),
        )
        for k in range(1, LANES)
    ]

    below[slots] = zero_plane
    above[slots] = zero_plane
    coarse[bricks] = zero_brick
    coarse2[bricks] = zero_brick
    low_x[3 * bricks] = zero_plane
    high_x[3 * bricks] = zero_plane
    children[LANES * slots] = jnp.zeros((block, width), F32)

    base = edge

    def assemble(centre, lower, upper, index, taps=range(27)):
        for t in taps:
            dx, dy, dz = t // 9 - 1, t // 3 % 3 - 1, t % 3 - 1
            at = index(t)
            ys, zs = pick(dy, edge), pick(dz, edge)
            if dx == 0:
                piece = centre[at, :, ys, zs, :]
            elif dx < 0:
                piece = lower[at, ys, zs, :][None]
            else:
                piece = upper[at, ys, zs, :][None]
            pad[place(dx, edge, 1), place(dy, edge, 1), place(dz, edge, base), :] = piece

    def product(weights, planes, rows):
        two = jnp.dot(
            cols[0 : (planes + 1) * rows, :],
            weights[:, 0 : 2 * width],
            preferred_element_type=F32,
        )
        third = jnp.dot(
            cols[2 * rows : (planes + 2) * rows, :],
            weights[:, 2 * width : 3 * width],
            preferred_element_type=F32,
        )
        total = third + two[0 : planes * rows, 0:width] + two[rows:, width : 2 * width]
        return jnp.maximum(total, 0.0).astype(BF16)

    own_taps = range(9, 18)
    far_taps = (*range(9), *range(18, 27))

    def gather_columns(x, row):
        for k in range(9):
            dy, dz = k // 3, k % 3 - 1
            piece = pad[x, dy : dy + edge, base + dz : base + dz + edge, :]
            cols[pl.ds(row, plane), k * width : (k + 1) * width] = piece.reshape(
                plane, width
            ).astype(BF16)

    def local_product(centre, j, index, weights):
        assemble(centre, None, None, index, own_taps)
        for x in range(edge):
            gather_columns(x + 1, x * plane)
        two = jnp.dot(
            cols[0 : edge * plane, :], weights[:, 0 : 2 * width], preferred_element_type=F32
        )
        third = jnp.dot(
            cols[plane : edge * plane, :],
            weights[:, 2 * width : 3 * width],
            preferred_element_type=F32,
        )
        inner = slice(plane, (edge - 1) * plane)
        middle = two[:, width : 2 * width]
        opened[j, 0] = middle[0:plane] + third[0:plane]
        opened[j, 1] = middle[(edge - 1) * plane :] + two[(edge - 2) * plane : (edge - 1) * plane, 0:width]
        total = middle[inner] + third[inner] + two[0 : (edge - 2) * plane, 0:width]
        return jnp.maximum(total, 0.0).astype(BF16)

    def outer_planes(count, lower, upper, index_of, weights, store):
        @pl.loop(0, count)
        def _(j):
            assemble(None, lower, upper, index_of(j), far_taps)
            gather_columns(0, pl.multiple_of(j * plane, plane))
            gather_columns(edge + 1, pl.multiple_of((count + j) * plane, plane))

        for side in range(2):
            added = jnp.dot(
                cols[side * count * plane : (side + 1) * count * plane, :],
                weights[:, 2 * side * width : (2 * side + 1) * width],
                preferred_element_type=F32,
            )
            for j in range(count):
                total = opened[j, side] + added[j * plane : (j + 1) * plane]
                store(j, side * (edge - 1), jnp.maximum(total, 0.0).astype(BF16))

    def fine_index(b):
        def index(t):
            at = fine_nbr[b, t]
            return jnp.where(at >= 0, at, slots)

        return index

    def take_faces(incoming):
        for s in range(slots):
            below[s] = incoming[0, s].astype(F32).reshape(edge, edge, width)
            above[s] = incoming[1, s].astype(F32).reshape(edge, edge, width)

    loaded(1)
    face = (edge, edge, width)
    cells = half * half

    def pool_copy(k, b):
        if b is None:
            source, at = pooled_out.at[member], slots
        else:
            source, at = pooled.at[member, b], b
        return remote(
            source, source, pool_send_sem.at[k - 1, at], pool_recv_sem.at[k - 1, at], peer(k)
        )

    def pool(value, count):
        pairs = value.reshape(count, 2, half, 2, edge, width)
        summed = (pairs[:, 0, :, 0] + pairs[:, 0, :, 1]) + (pairs[:, 1, :, 0] + pairs[:, 1, :, 1])
        half_z[0 : count * half * edge, :] = summed.reshape(count * half * edge, width)
        even = half_z[pl.ds(0, count * cells, stride=2), :]
        odd = half_z[pl.ds(1, count * cells, stride=2), :]
        return ((even + odd) * 0.125).astype(BF16)

    def encode(b):
        value = local_product(table, b, fine_index(b), w1).astype(F32)
        value = value.reshape((edge - 2,) + face)
        enc[b, 1 : edge - 1] = value
        pooled[member, b] = pool(value[1 : edge - 3], half - 2)

    def send_pooled(b):
        for k in range(1, LANES):
            pool_copy(k, b).start()

    encode(0)
    pl.semaphore_wait(barrier, peers)
    start_pair(halo1[0], has_next, halo1[1], has_prev)
    for copy in meta_copies:
        copy.start()
    send_pooled(0)

    @pl.loop(1, slots)
    def _(b):
        encode(b)
        send_pooled(b)

    finish_pair(halo1[0], has_next, halo1[1], has_prev)
    take_faces(face_in)

    def store_enc(b, x, value):
        enc[b, x] = value.astype(F32).reshape(face)

    outer_planes(slots, below, above, fine_index, w1, store_enc)
    for b in range(slots):
        pooled_out[member, b, 0:cells] = pool(enc[b, 0:2], 1)
        pooled_out[member, b, cells : 2 * cells] = pool(enc[b, edge - 2 : edge], 1)
    for k in range(1, LANES):
        pool_copy(k, None).start()

    for copy in meta_copies:
        copy.wait()
    to_smem = pltpu.make_async_copy(meta, meta_s, meta_sem)
    to_smem.start()
    for k in range(1, LANES):
        for b in (*range(slots), None):
            pool_copy(k, b).wait()
    to_smem.wait()
    for lane in range(LANES):
        for s in range(slots):
            at = lane * slots + s
            children[at, cells : block - cells] = pooled[lane, s].astype(F32)
            children[at, 0:cells] = pooled_out[lane, s, 0:cells].astype(F32)
            children[at, block - cells : block] = pooled_out[lane, s, cells : 2 * cells].astype(F32)

    def owner_of(value):
        value = jnp.maximum(value, 0)
        return lax.div(value, per), lax.rem(value, per)

    @pl.loop(0, bricks)
    def _(j):
        lane, slot = lax.div(j, per), lax.rem(j, per)
        for o in range(8):
            child = meta_s[lane, slot, o]
            safe = jnp.maximum(child, 0)
            at = lax.rem(lax.div(safe, slots), LANES) * slots + lax.rem(safe, slots)
            at = jnp.where(child >= 0, at, LANES * slots)
            ox, oy, oz = o // 4 * half, o // 2 % 2 * half, o % 2 * half
            for x in range(half):
                for y in range(half):
                    row = (x * half + y) * half
                    coarse[j, ox + x, oy + y, oz : oz + half, :] = children[
                        at, row : row + half, :
                    ]

    def side_copies(outgoing, incoming, phase):
        up = remote(
            outgoing,
            incoming.at[0],
            side_send_sem.at[phase, 0],
            side_recv_sem.at[phase, 0],
            me + LANES,
        )
        down = remote(
            outgoing,
            incoming.at[1],
            side_send_sem.at[phase, 1],
            side_recv_sem.at[phase, 1],
            me - LANES,
        )
        return up, down

    def coarse_index(lane, slot, live):
        def index(t):
            value = meta_s[lane, per + slot, t]
            there = (value >= 0) & live
            device, at = owner_of(value)
            at = lax.rem(device, LANES) * per + at
            if t // 9 == 1:
                return jnp.where(there, at, bricks)
            at = at + (lax.div(device, LANES) - group + 1) * bricks
            at = jnp.minimum(jnp.maximum(at, 0), 3 * bricks)
            return jnp.where(there, at, 3 * bricks)

        return index

    def send_sides(source, outgoing, incoming, phase):
        for j in range(bricks):
            first, last = source[j, 0], source[j, edge - 1]
            low_x[bricks + j] = first
            high_x[bricks + j] = last
            outgoing[j, 0] = first.reshape(plane, width).astype(BF16)
            outgoing[j, 1] = last.reshape(plane, width).astype(BF16)
        up, down = side_copies(outgoing, incoming, phase)
        start_pair(up, has_up, down, has_down)
        return up, down

    def take_sides(copies, incoming):
        finish_pair(copies[0], has_up, copies[1], has_down)
        for side, start in ((0, 0), (1, 2 * bricks)):
            for j in range(bricks):
                low_x[start + j] = incoming[side, j, 0].astype(F32).reshape(edge, edge, width)
                high_x[start + j] = incoming[side, j, 1].astype(F32).reshape(edge, edge, width)

    def group_index(j):
        return coarse_index(lax.div(j, per), lax.rem(j, per), True)

    face = (edge, edge, width)
    copies = send_sides(coarse, side_out, side_in, 0)
    loaded(2)

    @pl.loop(0, bricks)
    def _(j):
        value = local_product(coarse, j, group_index(j), w2).astype(F32)
        coarse2[j, 1 : edge - 1] = value.reshape((edge - 2,) + face)

    take_sides(copies, side_in)

    def store_coarse(j, x, value):
        coarse2[j, x] = value.astype(F32).reshape(face)

    outer_planes(bricks, high_x, low_x, group_index, w2, store_coarse)
    copies = send_sides(coarse2, side_out2, side_in2, 1)
    loaded(3)

    part = half * edge
    strip = slots * part

    def quarter(s, taps, planes):
        parent = fine_parent[s]
        safe = jnp.maximum(parent, 0)
        device, slot = owner_of(lax.div(safe, 8))
        octant = lax.rem(safe, 8)
        ox = lax.div(octant, 4) * half
        oy = lax.rem(lax.div(octant, 2), 2) * half
        index = coarse_index(lax.rem(device, LANES), slot, parent >= 0)
        assemble(coarse2, high_x, low_x, index, taps)
        for x in planes:
            start = pl.multiple_of(x * strip + s * part, part)
            for k in range(9):
                dy, dz = k // 3, k % 3 - 1
                piece = pad[ox + x, pl.ds(oy + dy, half), base + dz : base + dz + edge, :]
                cols[pl.ds(start, part), k * width : (k + 1) * width] = piece.reshape(
                    part, width
                ).astype(BF16)

    @pl.loop(0, slots)
    def _(s):
        quarter(s, own_taps, range(1, half + 1))

    take_sides(copies, side_in2)

    @pl.loop(0, slots)
    def _(s):
        quarter(s, range(27), (0, half + 1))

    parents = product(w3, half, strip).astype(F32).reshape(half, slots, part, width)

    for s in range(slots):
        oz = lax.rem(jnp.maximum(fine_parent[s], 0), 2)
        piece = parents[:, s].reshape(half * half * edge, width)
        spread[pl.ds(0, half * half * edge, stride=2), :] = piece
        spread[pl.ds(1, half * half * edge, stride=2), :] = piece
        for z in range(2):
            for row in range(half * half):
                start = row * 2 * edge + z * edge
                lifted[z, row] = spread[start : start + edge, :]
        for x in range(half):
            for y in range(half):
                up = lifted[oz, x * half + y]
                for xx in range(2):
                    for yy in range(2):
                        value = enc[s, 2 * x + xx, 2 * y + yy] + up
                        table[s, 2 * x + xx, 2 * y + yy] = value.astype(BF16).astype(F32)
        stage_faces(face_out2, s)
    halo2 = face_copies(face_out2, face_in2, 1)
    start_pair(halo2[0], has_next, halo2[1], has_prev)
    loaded(4)

    @pl.loop(0, slots)
    def _(b):
        value = local_product(table, b, fine_index(b), w4)
        out_ref[b, plane : (edge - 1) * plane, :] = value

    finish_pair(halo2[0], has_next, halo2[1], has_prev)
    take_faces(face_in2)

    def store_fine(b, x, value):
        out_ref[b, x * plane : (x + 1) * plane, :] = value

    outer_planes(slots, below, above, fine_index, w4, store_fine)


def per_device(
    n,
    features,
    fine_nbr,
    fine_send,
    fine_parent,
    coarse_child,
    coarse_nbr,
    enc_fine_w,
    enc_coarse_w,
    dec_coarse_w,
    dec_fine_w,
):
    slots, edge, width = features.shape[0], features.shape[1], features.shape[-1]
    per = coarse_nbr.shape[0]
    bricks = LANES * per
    half = edge // 2
    plane = edge * edge
    voxels = edge**3
    strip = slots * half * edge
    rows = -(-2 * per // 8) * 8
    kernels = [
        w.reshape(3, 9 * width, width)
        for w in (enc_fine_w, enc_coarse_w, dec_coarse_w, dec_fine_w)
    ]
    vmem = pltpu.VMEM
    vmem_spec = pl.BlockSpec(memory_space=pltpu.VMEM)
    any_spec = pl.BlockSpec(memory_space=pl.ANY)
    cube = (edge, edge, edge, width)
    face = (edge, edge, width)
    dma = pltpu.SemaphoreType.DMA
    out = pl.pallas_call(
        functools.partial(kernel, n),
        out_shape=pltpu.VMEM((slots, voxels, width), BF16),
        in_specs=[any_spec] * 10,
        out_specs=vmem_spec,
        scratch_shapes=[
            pltpu.SMEM(fine_nbr.shape, jnp.int32),
            pltpu.SMEM(fine_send.shape[1:], jnp.int32),
            pltpu.SMEM(fine_parent.shape, jnp.int32),
            vmem(coarse_child.shape, jnp.int32),
            vmem(coarse_nbr.shape, jnp.int32),
            vmem((slots, voxels, width), BF16),
            *[vmem((9 * width, 3 * width), BF16)] * 4,
            vmem((edge + 2, edge + 2, 3 * edge, width), F32),
            vmem((max((edge + 2) * plane, (half + 2) * strip, 2 * max(slots, bricks) * plane), 9 * width), BF16),
            vmem((max(slots, bricks), 2, plane, width), F32),
            vmem((slots + 1,) + cube, F32),
            vmem((slots,) + cube, F32),
            vmem((slots + 1,) + face, F32),
            vmem((slots + 1,) + face, F32),
            vmem((2, slots, plane, width), BF16),
            vmem((2, slots, plane, width), BF16),
            vmem((2, slots, plane, width), BF16),
            vmem((2, slots, plane, width), BF16),
            vmem((half * half * edge, width), F32),
            vmem((LANES, slots, (half - 2) * half**2, width), BF16),
            vmem((LANES, slots, 2 * half**2, width), BF16),
            vmem((LANES * slots + 1, half**3, width), F32),
            vmem((LANES, rows, 128), jnp.int32),
            pltpu.SMEM((LANES, rows, 128), jnp.int32),
            vmem((bricks + 1,) + cube, F32),
            vmem((bricks + 1,) + cube, F32),
            vmem((3 * bricks + 1,) + face, F32),
            vmem((3 * bricks + 1,) + face, F32),
            vmem((bricks, 2, plane, width), BF16),
            vmem((2, bricks, 2, plane, width), BF16),
            vmem((bricks, 2, plane, width), BF16),
            vmem((2, bricks, 2, plane, width), BF16),
            vmem((half * half * 2 * edge, width), F32),
            vmem((2, half * half, edge, width), F32),
            dma((5, 3)),
            dma((5,)),
            dma((2, 2)),
            dma((2, 2)),
            dma((LANES - 1, slots + 1)),
            dma((LANES - 1, slots + 1)),
            dma((LANES - 1,)),
            dma((LANES - 1,)),
            dma((2, 2)),
            dma((2, 2)),
            dma(()),
        ],
        compiler_params=pltpu.CompilerParams(
            collective_id=0, has_side_effects=True, vmem_limit_bytes=60 * 1024 * 1024
        ),
    )(
        fine_nbr,
        fine_send[0],
        fine_parent,
        coarse_child,
        coarse_nbr,
        features.reshape(slots, voxels, width),
        *kernels,
    )
    return out.reshape(features.shape)


def solution(mesh):
    lead = ("groups", "gx")
    placed = (
        P(lead, None, None, None, None),
        P(lead, None),
        P(lead, None, None),
        P(lead),
        P(lead, None),
        P(lead, None),
        P(),
        P(),
        P(),
        P(),
    )
    return jax.shard_map(
        functools.partial(per_device, mesh.shape["gx"]),
        mesh=mesh,
        in_specs=placed,
        out_specs=P(lead, None, None, None, None),
        check_vma=False,
    )
```

```python
import functools

import jax
import jax.numpy as jnp
from jax import lax
from jax.experimental import pallas as pl
from jax.experimental.pallas import tpu as pltpu
from jax.sharding import PartitionSpec as P

F32 = jnp.float32
BF16 = jnp.bfloat16
LANES = 4
SPLIT = 2
MESH = pl.DeviceIdType.MESH


def pick(offset, edge):
    if offset < 0:
        return slice(edge - 1, edge)
    if offset == 0:
        return slice(0, edge)
    return slice(0, 1)


def place(offset, edge, base):
    if offset < 0:
        return slice(base - 1, base)
    if offset == 0:
        return slice(base, base + edge)
    return slice(base + edge, base + edge + 1)


def kernel(
    n,
    fine_nbr_hbm,
    fine_send_hbm,
    fine_parent_hbm,
    child_hbm,
    nbr_hbm,
    feat_hbm,
    w1_hbm,
    w2_hbm,
    w3_hbm,
    w4_hbm,
    out_ref,
    fine_nbr,
    fine_send,
    fine_parent,
    child_ref,
    nbr_ref,
    feat,
    w1,
    w2,
    w3,
    w4,
    wup,
    pad,
    upad,
    zs,
    zfar,
    zq,
    zu,
    opened,
    acc,
    dacc,
    picks,
    utab,
    ubelow,
    uabove,
    table,
    enc,
    below,
    above,
    face_out,
    face_in,
    face_out2,
    face_in2,
    face_out3,
    face_in3,
    half_z,
    pooled,
    pooled_out,
    children,
    meta,
    meta_s,
    coarse,
    coarse2,
    low_x,
    high_x,
    side_out,
    side_in,
    side_out2,
    side_in2,
    spread,
    load_sem,
    small_sem,
    face_send_sem,
    face_recv_sem,
    pool_send_sem,
    pool_recv_sem,
    meta_send_sem,
    meta_recv_sem,
    side_send_sem,
    side_recv_sem,
    meta_sem,
):
    slots, edge = out_ref.shape[0], enc.shape[1]
    plane = edge * edge
    width = out_ref.shape[-1]
    half = edge // 2
    block = half**3
    per = child_ref.shape[0]
    bricks = LANES * per
    me = lax.axis_index("gx")
    member = lax.rem(me, LANES)
    group = lax.div(me, LANES)

    def peer(k):
        return me - member + (member ^ k)

    width = out_ref.shape[-1]
    loads = [[pltpu.make_async_copy(feat_hbm, feat, load_sem.at[0, 0])]]
    for i, (src, dst) in enumerate(
        ((w1_hbm, w1), (w2_hbm, w2), (w3_hbm, w3), (w4_hbm, w4))
    ):
        loads.append(
            [
                pltpu.make_async_copy(
                    src.at[dx], dst.at[:, dx * width : (dx + 1) * width], load_sem.at[i + 1, dx]
                )
                for dx in range(3)
            ]
        )
    small = [
        pltpu.make_async_copy(src, dst, small_sem.at[i])
        for i, (src, dst) in enumerate(
            (
                (fine_nbr_hbm, fine_nbr),
                (fine_send_hbm, fine_send),
                (fine_parent_hbm, fine_parent),
                (child_hbm, child_ref),
                (nbr_hbm, nbr_ref),
            )
        )
    ]
    for copy in loads[0]:
        copy.start()
    for copy in small:
        copy.start()
    for copies in loads[1:]:
        for copy in copies:
            copy.start()

    def loaded(i):
        for copy in loads[i]:
            copy.wait()

    has_prev, has_next = me > 0, me < n - 1
    has_down, has_up = me >= LANES, me < n - LANES
    barrier = pltpu.get_barrier_semaphore()

    def greet(other):
        pl.semaphore_signal(barrier, inc=1, device_id={"gx": other}, device_id_type=MESH)

    sides = (
        (has_prev & (member == 0), me - 1),
        (has_next & (member == LANES - 1), me + 1),
        (has_down, me - LANES),
        (has_up, me + LANES),
    )
    for k in range(1, LANES):
        greet(peer(k))
    peers = LANES - 1
    for there, other in sides:
        pl.when(there)(functools.partial(greet, other))
        peers = peers + jnp.where(there, 1, 0)

    def remote(src, dst, send, recv, other):
        return pltpu.make_async_remote_copy(
            src_ref=src,
            dst_ref=dst,
            send_sem=send,
            recv_sem=recv,
            device_id={"gx": other},
            device_id_type=MESH,
        )

    def face_copies(outgoing, incoming, phase):
        up = remote(
            outgoing.at[0],
            incoming.at[0],
            face_send_sem.at[phase, 0],
            face_recv_sem.at[phase, 0],
            me + 1,
        )
        down = remote(
            outgoing.at[1],
            incoming.at[1],
            face_send_sem.at[phase, 1],
            face_recv_sem.at[phase, 1],
            me - 1,
        )
        return up, down

    def start_pair(up, up_there, down, down_there):
        pl.when(up_there)(up.start)
        pl.when(down_there)(down.start)

    def finish_pair(up, up_there, down, down_there):
        @pl.when(down_there)
        def _():
            up.wait_recv()
            down.wait_send()

        @pl.when(up_there)
        def _():
            down.wait_recv()
            up.wait_send()


    cube = (edge, edge, edge, width)
    face = (edge, edge, width)
    base = edge
    padded = (edge + 2) * edge
    own_taps = range(9, 18)
    far_taps = (*range(9), *range(18, 27))
    zero_brick = jnp.zeros(cube, F32)
    zero_plane = jnp.zeros(face, F32)
    table[slots] = zero_brick
    enc[slots] = zero_brick

    def stage_faces(outgoing, source, last, s):
        up_from = jnp.where(fine_send[0, s] >= 0, s, slots)
        down_from = jnp.where(fine_send[1, s] >= 0, s, slots)
        rows = outgoing.shape[2]
        outgoing[0, s] = source[up_from, last].reshape(rows, width).astype(BF16)
        outgoing[1, s] = source[down_from, 0].reshape(rows, width).astype(BF16)

    for copy in small:
        copy.wait()
    meta[member, 0:per, 0 : child_ref.shape[1]] = child_ref[...]
    meta[member, per : 2 * per, 0 : nbr_ref.shape[1]] = nbr_ref[...]
    loaded(0)
    for s in range(slots):
        table[s] = feat[s].astype(F32).reshape(cube)
    for s in range(slots):
        stage_faces(face_out, table, edge - 1, s)
    halo1 = face_copies(face_out, face_in, 0)
    halo2 = face_copies(face_out2, face_in2, 1)
    halo3 = face_copies(face_out3, face_in3, 2)
    meta_copies = [
        remote(
            meta.at[member],
            meta.at[member],
            meta_send_sem.at[k - 1],
            meta_recv_sem.at[k - 1],
            peer(k),
        )
        for k in range(1, LANES)
    ]

    below[slots] = zero_plane
    above[slots] = zero_plane
    coarse[bricks] = zero_brick
    coarse2[bricks] = zero_brick
    low_x[3 * bricks] = zero_plane
    high_x[3 * bricks] = zero_plane
    children[LANES * slots] = jnp.zeros((block, width), F32)
    utab[slots] = jnp.zeros((half, half, edge, width), F32)
    ubelow[slots] = jnp.zeros((half, edge, width), F32)
    uabove[slots] = jnp.zeros((half, edge, width), F32)

    def assemble(target, side, centre, lower, upper, index, taps):
        for t in taps:
            dx, dy, dz = t // 9 - 1, t // 3 % 3 - 1, t % 3 - 1
            at = index(t)
            ys, zs = pick(dy, side), pick(dz, edge)
            if dx == 0:
                piece = centre[at, :, ys, zs, :]
            elif dx < 0:
                piece = lower[at, ys, zs, :][None]
            else:
                piece = upper[at, ys, zs, :][None]
            target[place(dx, side, 1), place(dy, side, 1), place(dz, edge, base), :] = piece

    def shift(store, row, source, x, y, count):
        rows = count * edge
        for dz in range(3):
            first = base + dz - 1
            piece = source[x, y, first : first + edge, :]
            store[dz, pl.ds(row, rows), :] = piece.reshape(rows, width).astype(BF16)

    def columns(store, starts, rows, offsets=(0, 1, 2)):
        return jnp.concatenate(
            [
                jnp.concatenate(
                    [store[dz, r + dy * edge : r + dy * edge + rows, :] for r in starts], axis=0
                )
                for dy in offsets
                for dz in range(3)
            ],
            axis=1,
        )

    def dot(a, b):
        return jnp.dot(a, b, preferred_element_type=F32)

    def local_product(centre, index, weights):
        assemble(pad, edge, centre, None, None, index, own_taps)
        starts = [x * padded for x in range(edge)]
        for x in range(edge):
            shift(zs, x * padded, pad, x + 1, slice(None), edge + 2)
        two = dot(columns(zs, starts, plane), weights[:, 0 : 2 * width])
        third = dot(columns(zs, starts[1:], plane), weights[:, 2 * width : 3 * width])
        totals = []
        for x in range(edge):
            total = two[x * plane : (x + 1) * plane, width : 2 * width]
            if x > 0:
                total = total + two[(x - 1) * plane : x * plane, 0:width]
            if x < edge - 1:
                total = total + third[x * plane : (x + 1) * plane]
            totals.append(total)
        return totals

    def outer_planes(count, lower, upper, index_of, weights, store):
        @pl.loop(0, count)
        def _(j):
            assemble(pad, edge, None, lower, upper, index_of(j), far_taps)
            for side in range(2):
                row = pl.multiple_of((side * count + j) * padded, edge)
                shift(zfar, row, pad, side * (edge + 1), slice(None), edge + 2)

        for side in range(2):
            starts = [(side * count + j) * padded for j in range(count)]
            added = dot(
                columns(zfar, starts, plane),
                weights[:, 2 * side * width : (2 * side + 1) * width],
            )
            for j in range(count):
                store(j, side, added[j * plane : (j + 1) * plane])

    def rounded(value):
        return jnp.maximum(value, 0.0).astype(BF16).astype(F32)

    def fine_index(b):
        def index(t):
            at = fine_nbr[b, t]
            return jnp.where(at >= 0, at, slots)

        return index

    def take_faces(incoming, low, high):
        shape = low.shape[1:]
        for s in range(slots):
            low[s] = incoming[0, s].astype(F32).reshape(shape)
            high[s] = incoming[1, s].astype(F32).reshape(shape)

    cells = half * half

    def pool_copy(k, b):
        if b is None:
            source, at = pooled_out.at[member], slots
        else:
            source, at = pooled.at[member, b], b
        return remote(
            source, source, pool_send_sem.at[k - 1, at], pool_recv_sem.at[k - 1, at], peer(k)
        )

    def pool(value, count):
        pairs = value.reshape(count, 2, half, 2, edge, width)
        summed = (pairs[:, 0, :, 0] + pairs[:, 0, :, 1]) + (pairs[:, 1, :, 0] + pairs[:, 1, :, 1])
        half_z[0 : count * half * edge, :] = summed.reshape(count * half * edge, width)
        even = half_z[pl.ds(0, count * cells, stride=2), :]
        odd = half_z[pl.ds(1, count * cells, stride=2), :]
        return ((even + odd) * 0.125).astype(BF16)

    loaded(1)

    def encode(b):
        totals = local_product(table, fine_index(b), w1)
        opened[b, 0] = totals[0]
        opened[b, 1] = totals[edge - 1]
        value = rounded(jnp.concatenate(totals[1 : edge - 1], axis=0))
        value = value.reshape((edge - 2,) + face)
        enc[b, 1 : edge - 1] = value
        pooled[member, b] = pool(value[1 : edge - 3], half - 2)

    def send_pooled(b):
        for k in range(1, LANES):
            pool_copy(k, b).start()

    encode(0)
    pl.semaphore_wait(barrier, peers)
    start_pair(halo1[0], has_next, halo1[1], has_prev)
    for copy in meta_copies:
        copy.start()
    send_pooled(0)

    @pl.loop(1, slots)
    def _(b):
        encode(b)
        send_pooled(b)

    finish_pair(halo1[0], has_next, halo1[1], has_prev)
    take_faces(face_in, below, above)

    def store_enc(b, side, added):
        enc[b, side * (edge - 1)] = rounded(opened[b, side] + added).reshape(face)

    outer_planes(slots, below, above, fine_index, w1, store_enc)
    for b in range(slots):
        pooled_out[member, b, 0:cells] = pool(enc[b, 0:2], 1)
        pooled_out[member, b, cells : 2 * cells] = pool(enc[b, edge - 2 : edge], 1)
    for k in range(1, LANES):
        pool_copy(k, None).start()
    for s in range(slots):
        stage_faces(face_out2, enc, edge - 1, s)
    start_pair(halo2[0], has_next, halo2[1], has_prev)

    loaded(4)

    def decode_part(b):
        totals = local_product(enc, fine_index(b), w4)
        acc[b] = jnp.concatenate(totals, axis=0)

    def run_decode(first, last):
        @pl.loop(first, last)
        def _(b):
            decode_part(b)

    strips = 4
    span = width // strips

    @pl.loop(0, 3 * strips)
    def _(i):
        dz, strip_at = lax.div(i, strips), lax.rem(i, strips)
        rows = []
        for dy in range(3):
            start = pl.multiple_of((dy * 3 + dz) * width + strip_at * span, span)
            rows.append(w4[pl.ds(start, span), :].astype(F32))
        for py, parts in enumerate(((rows[0], rows[1] + rows[2]), (rows[0] + rows[1], rows[2]))):
            for q, part_q in enumerate(parts):
                a = part_q[:, 0:width]
                b = part_q[:, width : 2 * width]
                c = part_q[:, 2 * width : 3 * width]
                start = pl.multiple_of((q * 3 + dz) * width + strip_at * span, span)
                wup[py, pl.ds(start, span), :] = jnp.concatenate(
                    [b + c, a + b, a, c], axis=1
                ).astype(BF16)

    run_decode(0, SPLIT)

    for copy in meta_copies:
        copy.wait()
    to_smem = pltpu.make_async_copy(meta, meta_s, meta_sem)
    to_smem.start()
    for k in range(1, LANES):
        for b in (*range(slots), None):
            pool_copy(k, b).wait()
    to_smem.wait()
    for lane in range(LANES):
        for s in range(slots):
            at = lane * slots + s
            children[at, cells : block - cells] = pooled[lane, s].astype(F32)
            children[at, 0:cells] = pooled_out[lane, s, 0:cells].astype(F32)
            children[at, block - cells : block] = pooled_out[lane, s, cells : 2 * cells].astype(F32)

    def owner_of(value):
        value = jnp.maximum(value, 0)
        return lax.div(value, per), lax.rem(value, per)

    @pl.loop(0, bricks)
    def _(j):
        lane, slot = lax.div(j, per), lax.rem(j, per)
        for o in range(8):
            child = meta_s[lane, slot, o]
            safe = jnp.maximum(child, 0)
            at = lax.rem(lax.div(safe, slots), LANES) * slots + lax.rem(safe, slots)
            at = jnp.where(child >= 0, at, LANES * slots)
            ox, oy, oz = o // 4 * half, o // 2 % 2 * half, o % 2 * half
            for x in range(half):
                for y in range(half):
                    row = (x * half + y) * half
                    coarse[j, ox + x, oy + y, oz : oz + half, :] = children[
                        at, row : row + half, :
                    ]

    def side_copies(outgoing, incoming, phase):
        up = remote(
            outgoing,
            incoming.at[0],
            side_send_sem.at[phase, 0],
            side_recv_sem.at[phase, 0],
            me + LANES,
        )
        down = remote(
            outgoing,
            incoming.at[1],
            side_send_sem.at[phase, 1],
            side_recv_sem.at[phase, 1],
            me - LANES,
        )
        return up, down

    def coarse_index(lane, slot, live):
        def index(t):
            value = meta_s[lane, per + slot, t]
            there = (value >= 0) & live
            device, at = owner_of(value)
            at = lax.rem(device, LANES) * per + at
            if t // 9 == 1:
                return jnp.where(there, at, bricks)
            at = at + (lax.div(device, LANES) - group + 1) * bricks
            at = jnp.minimum(jnp.maximum(at, 0), 3 * bricks)
            return jnp.where(there, at, 3 * bricks)

        return index

    def send_sides(source, outgoing, incoming, phase):
        for j in range(bricks):
            first, last = source[j, 0], source[j, edge - 1]
            low_x[bricks + j] = first
            high_x[bricks + j] = last
            outgoing[j, 0] = first.reshape(plane, width).astype(BF16)
            outgoing[j, 1] = last.reshape(plane, width).astype(BF16)
        up, down = side_copies(outgoing, incoming, phase)
        start_pair(up, has_up, down, has_down)
        return up, down

    def take_sides(copies, incoming):
        finish_pair(copies[0], has_up, copies[1], has_down)
        for side, start in ((0, 0), (1, 2 * bricks)):
            for j in range(bricks):
                low_x[start + j] = incoming[side, j, 0].astype(F32).reshape(face)
                high_x[start + j] = incoming[side, j, 1].astype(F32).reshape(face)

    def group_index(j):
        return coarse_index(lax.div(j, per), lax.rem(j, per), True)

    copies = send_sides(coarse, side_out, side_in, 0)
    loaded(2)

    @pl.loop(0, bricks)
    def _(j):
        totals = local_product(coarse, group_index(j), w2)
        opened[j, 0] = totals[0]
        opened[j, 1] = totals[edge - 1]
        value = rounded(jnp.concatenate(totals[1 : edge - 1], axis=0))
        coarse2[j, 1 : edge - 1] = value.reshape((edge - 2,) + face)

    take_sides(copies, side_in)

    def store_coarse(j, side, added):
        coarse2[j, side * (edge - 1)] = rounded(opened[j, side] + added).reshape(face)

    outer_planes(bricks, high_x, low_x, group_index, w2, store_coarse)
    copies = send_sides(coarse2, side_out2, side_in2, 1)
    loaded(3)

    part = half * edge
    strip = slots * part
    tall = half + 2
    column = tall * edge

    def parent_of(s):
        parent = fine_parent[s]
        safe = jnp.maximum(parent, 0)
        device, slot = owner_of(lax.div(safe, 8))
        octant = lax.rem(safe, 8)
        ox, oy = lax.div(octant, 4), lax.rem(lax.div(octant, 2), 2)
        return coarse_index(lax.rem(device, LANES), slot, parent >= 0), ox, oy * half

    pad[0] = jnp.zeros(pad.shape[1:], F32)
    pad[edge + 1] = jnp.zeros(pad.shape[1:], F32)

    @pl.loop(0, slots)
    def _(s):
        index, ox, oy = parent_of(s)
        assemble(pad, edge, coarse2, None, None, index, own_taps)
        for x in range(tall):
            row = pl.multiple_of((s * tall + x) * column, edge)
            shift(zq, row, pad, ox * half + x, pl.ds(oy, tall), tall)

    def starts_of(planes):
        return [(s * tall + x) * column for x in planes for s in range(slots)]

    two = dot(columns(zq, starts_of(range(half + 1)), part), w3[:, 0 : 2 * width])
    third = dot(columns(zq, starts_of(range(2, tall)), part), w3[:, 2 * width : 3 * width])
    dacc[...] = third + two[0 : half * strip, 0:width] + two[strip:, width : 2 * width]

    run_decode(SPLIT, slots)
    finish_pair(halo2[0], has_next, halo2[1], has_prev)
    take_faces(face_in2, below, above)

    def store_part(b, side, added):
        at = side * (edge - 1) * plane
        acc[b, at : at + plane] = acc[b, at : at + plane] + added

    outer_planes(slots, below, above, fine_index, w4, store_part)
    take_sides(copies, side_in2)

    @pl.loop(0, slots)
    def _(s):
        index, ox, oy = parent_of(s)
        assemble(pad, edge, None, high_x, low_x, index, far_taps)
        row = pl.multiple_of(s * column, edge)
        shift(zfar, row, pad, ox * (edge + 1), pl.ds(oy, tall), tall)

    far = dot(
        columns(zfar, [s * column for s in range(slots)], part),
        jnp.concatenate([w3[:, 0:width], w3[:, 2 * width : 3 * width]], axis=1),
    )
    picks[0] = far[:, 0:width]
    picks[1] = jnp.zeros((strip, width), F32)
    picks[2] = far[:, width : 2 * width]
    for s in range(slots):
        _, ox, _ = parent_of(s)
        rows = slice(s * part, (s + 1) * part)
        low = picks[ox, rows]
        high = picks[ox + 1, rows]
        pieces = [dacc[x * strip + s * part : x * strip + (s + 1) * part, :] for x in range(half)]
        pieces[0] = pieces[0] + low
        pieces[half - 1] = pieces[half - 1] + high
        piece = rounded(jnp.concatenate(pieces, axis=0))
        oz = lax.rem(jnp.maximum(fine_parent[s], 0), 2)
        spread[s, pl.ds(0, half * part, stride=2), :] = piece
        spread[s, pl.ds(1, half * part, stride=2), :] = piece
        for x in range(half):
            for y in range(half):
                start = ((x * half + y) * 2 + oz) * edge
                utab[s, x, y] = spread[s, pl.ds(start, edge), :]
        stage_faces(face_out3, utab, half - 1, s)
    start_pair(halo3[0], has_next, halo3[1], has_prev)

    brick_rows = tall * column

    @pl.loop(0, slots)
    def _(b):
        assemble(upad, half, utab, None, None, fine_index(b), own_taps)
        for x in range(half):
            row = pl.multiple_of(b * brick_rows + (x + 1) * column, edge)
            shift(zu, row, upad, x + 1, slice(None), tall)

    def woven(zero, one):
        pair = jnp.stack(
            [zero.reshape(half, edge, width), one.reshape(half, edge, width)], axis=1
        )
        return pair.reshape(plane, width)

    inner = [b * brick_rows + (x + 1) * column for b in range(slots) for x in range(half)]
    direct, across = [], []
    for py in range(2):
        lhs = columns(zu, inner, part, (py, py + 1))
        direct.append(dot(lhs, wup[py, :, 0 : 2 * width]))
        across.append(dot(columns(zu, inner, part, (py, py + 1)), wup[py, :, 2 * width :]))

    for b in range(slots):
        for x in range(edge):
            i, px = x // 2, x % 2
            lanes = slice(px * width, (px + 1) * width)
            other = i - 1 + 2 * px
            sums = []
            for py in range(2):
                at = (b * half + i) * part
                value = direct[py][at : at + part, lanes]
                if 0 <= other < half:
                    at = (b * half + other) * part
                    value = value + across[py][at : at + part, lanes]
                sums.append(value)
            rows = slice(x * plane, (x + 1) * plane)
            total = acc[b, rows] + woven(*sums)
            if 0 <= other < half:
                out_ref[b, rows, :] = jnp.maximum(total, 0.0).astype(BF16)
            else:
                acc[b, rows] = total

    finish_pair(halo3[0], has_next, halo3[1], has_prev)
    take_faces(face_in3, ubelow, uabove)

    @pl.loop(0, slots)
    def _(b):
        assemble(upad, half, None, ubelow, uabove, fine_index(b), far_taps)
        for x in (0, half + 1):
            row = pl.multiple_of(b * brick_rows + x * column, edge)
            shift(zu, row, upad, x, slice(None), tall)

    for side in range(2):
        starts = [b * brick_rows + side * (half + 1) * column for b in range(slots)]
        lanes = slice((2 + side) * width, (3 + side) * width)
        sums = [dot(columns(zu, starts, part, (py, py + 1)), wup[py, :, lanes]) for py in range(2)]
        for b in range(slots):
            at = side * (edge - 1) * plane
            rows = slice(b * part, (b + 1) * part)
            total = acc[b, at : at + plane] + woven(sums[0][rows], sums[1][rows])
            out_ref[b, at : at + plane, :] = jnp.maximum(total, 0.0).astype(BF16)


def per_device(
    n,
    features,
    fine_nbr,
    fine_send,
    fine_parent,
    coarse_child,
    coarse_nbr,
    enc_fine_w,
    enc_coarse_w,
    dec_coarse_w,
    dec_fine_w,
):
    slots, edge, width = features.shape[0], features.shape[1], features.shape[-1]
    per = coarse_nbr.shape[0]
    bricks = LANES * per
    half = edge // 2
    plane = edge * edge
    voxels = edge**3
    padded = (edge + 2) * edge
    tall = half + 2
    rows = -(-2 * per // 8) * 8
    kernels = [
        w.reshape(3, 9 * width, width)
        for w in (enc_fine_w, enc_coarse_w, dec_coarse_w, dec_fine_w)
    ]
    vmem = pltpu.VMEM
    vmem_spec = pl.BlockSpec(memory_space=pltpu.VMEM)
    any_spec = pl.BlockSpec(memory_space=pl.ANY)
    cube = (edge, edge, edge, width)
    face = (edge, edge, width)
    dma = pltpu.SemaphoreType.DMA
    out = pl.pallas_call(
        functools.partial(kernel, n),
        out_shape=pltpu.VMEM((slots, voxels, width), BF16),
        in_specs=[any_spec] * 10,
        out_specs=vmem_spec,
        scratch_shapes=[
            pltpu.SMEM(fine_nbr.shape, jnp.int32),
            pltpu.SMEM(fine_send.shape[1:], jnp.int32),
            pltpu.SMEM(fine_parent.shape, jnp.int32),
            vmem(coarse_child.shape, jnp.int32),
            vmem(coarse_nbr.shape, jnp.int32),
            vmem((slots, voxels, width), BF16),
            *[vmem((9 * width, 3 * width), BF16)] * 4,
            vmem((2, 6 * width, 4 * width), BF16),
            vmem((edge + 2, edge + 2, 3 * edge, width), F32),
            vmem((half + 2, half + 2, 3 * edge, width), F32),
            vmem((3, edge * padded, width), BF16),
            vmem((3, 2 * max(slots, bricks) * padded, width), BF16),
            vmem((3, slots * tall * tall * edge, width), BF16),
            vmem((3, slots * tall * tall * edge, width), BF16),
            vmem((max(slots, bricks), 2, plane, width), F32),
            vmem((slots, voxels, width), F32),
            vmem((half * slots * half * edge, width), F32),
            vmem((3, slots * half * edge, width), F32),
            vmem((slots + 1, half, half, edge, width), F32),
            vmem((slots + 1, half, edge, width), F32),
            vmem((slots + 1, half, edge, width), F32),
            vmem((slots + 1,) + cube, F32),
            vmem((slots + 1,) + cube, F32),
            vmem((slots + 1,) + face, F32),
            vmem((slots + 1,) + face, F32),
            vmem((2, slots, plane, width), BF16),
            vmem((2, slots, plane, width), BF16),
            vmem((2, slots, plane, width), BF16),
            vmem((2, slots, plane, width), BF16),
            vmem((2, slots, half * edge, width), BF16),
            vmem((2, slots, half * edge, width), BF16),
            vmem((half * half * edge, width), F32),
            vmem((LANES, slots, (half - 2) * half**2, width), BF16),
            vmem((LANES, slots, 2 * half**2, width), BF16),
            vmem((LANES * slots + 1, half**3, width), F32),
            vmem((LANES, rows, 128), jnp.int32),
            pltpu.SMEM((LANES, rows, 128), jnp.int32),
            vmem((bricks + 1,) + cube, F32),
            vmem((bricks + 1,) + cube, F32),
            vmem((3 * bricks + 1,) + face, F32),
            vmem((3 * bricks + 1,) + face, F32),
            vmem((bricks, 2, plane, width), BF16),
            vmem((2, bricks, 2, plane, width), BF16),
            vmem((bricks, 2, plane, width), BF16),
            vmem((2, bricks, 2, plane, width), BF16),
            vmem((slots, half * half * 2 * edge, width), F32),
            dma((5, 3)),
            dma((5,)),
            dma((3, 2)),
            dma((3, 2)),
            dma((LANES - 1, slots + 1)),
            dma((LANES - 1, slots + 1)),
            dma((LANES - 1,)),
            dma((LANES - 1,)),
            dma((2, 2)),
            dma((2, 2)),
            dma(()),
        ],
        compiler_params=pltpu.CompilerParams(
            collective_id=0, has_side_effects=True, vmem_limit_bytes=60 * 1024 * 1024
        ),
    )(
        fine_nbr,
        fine_send[0],
        fine_parent,
        coarse_child,
        coarse_nbr,
        features.reshape(slots, voxels, width),
        *kernels,
    )
    return out.reshape(features.shape)


def solution(mesh):
    lead = ("groups", "gx")
    placed = (
        P(lead, None, None, None, None),
        P(lead, None),
        P(lead, None, None),
        P(lead),
        P(lead, None),
        P(lead, None),
        P(),
        P(),
        P(),
        P(),
    )
    return jax.shard_map(
        functools.partial(per_device, mesh.shape["gx"]),
        mesh=mesh,
        in_specs=placed,
        out_specs=P(lead, None, None, None, None),
        check_vma=False,
    )
```

```python
import functools

import jax
import jax.numpy as jnp
from jax import lax
from jax.experimental import pallas as pl
from jax.experimental.pallas import tpu as pltpu
from jax.sharding import PartitionSpec as P

F32 = jnp.float32
BF16 = jnp.bfloat16
LANES = 4
SPLIT = 2
MESH = pl.DeviceIdType.MESH


def pick(offset, edge):
    if offset < 0:
        return slice(edge - 1, edge)
    if offset == 0:
        return slice(0, edge)
    return slice(0, 1)


def place(offset, edge, base):
    if offset < 0:
        return slice(base - 1, base)
    if offset == 0:
        return slice(base, base + edge)
    return slice(base + edge, base + edge + 1)


def kernel(
    n,
    fine_nbr_hbm,
    fine_send_hbm,
    fine_parent_hbm,
    child_hbm,
    nbr_hbm,
    parent_row_hbm,
    feat_hbm,
    w1_hbm,
    w2_hbm,
    w3_hbm,
    w4_hbm,
    out_ref,
    fine_nbr,
    fine_send,
    fine_parent,
    child_ref,
    nbr_ref,
    parent_row,
    feat,
    w1,
    w2,
    w3,
    w4,
    wup,
    pad,
    upad,
    zs,
    zfar,
    zq,
    zu,
    opened,
    acc,
    dacc,
    picks,
    utab,
    ubelow,
    uabove,
    table,
    enc,
    below,
    above,
    face_out,
    face_in,
    face_out2,
    face_in2,
    face_out3,
    face_in3,
    half_z,
    pooled,
    pooled_out,
    children,
    meta,
    meta_s,
    meta_far,
    meta_far_s,
    far_children,
    coarse,
    coarse2,
    low_x,
    high_x,
    side_out,
    side_in,
    side_out2,
    side_in2,
    spread,
    load_sem,
    small_sem,
    face_send_sem,
    face_recv_sem,
    pool_send_sem,
    pool_recv_sem,
    meta_send_sem,
    meta_recv_sem,
    side_send_sem,
    side_recv_sem,
    meta_sem,
    far_sem,
):
    slots, edge = out_ref.shape[0], enc.shape[1]
    plane = edge * edge
    width = out_ref.shape[-1]
    half = edge // 2
    block = half**3
    per = child_ref.shape[0]
    bricks = LANES * per
    me = lax.axis_index("gx")
    member = lax.rem(me, LANES)
    group = lax.div(me, LANES)

    def peer(k):
        return me - member + (member ^ k)

    width = out_ref.shape[-1]
    loads = [[pltpu.make_async_copy(feat_hbm, feat, load_sem.at[0])]]
    for i, (src, dst) in enumerate(
        ((w1_hbm, w1), (w2_hbm, w2), (w3_hbm, w3), (w4_hbm, w4))
    ):
        loads.append([pltpu.make_async_copy(src, dst, load_sem.at[i + 1])])
    small = [
        pltpu.make_async_copy(src, dst, small_sem.at[i])
        for i, (src, dst) in enumerate(
            (
                (fine_nbr_hbm, fine_nbr),
                (fine_send_hbm, fine_send),
                (fine_parent_hbm, fine_parent),
                (child_hbm, child_ref),
                (nbr_hbm, nbr_ref),
                (parent_row_hbm, parent_row),
            )
        )
    ]
    for copy in loads[0]:
        copy.start()
    for copy in small:
        copy.start()
    for copies in loads[1:]:
        for copy in copies:
            copy.start()

    def loaded(i):
        for copy in loads[i]:
            copy.wait()

    has_prev, has_next = me > 0, me < n - 1
    has_down, has_up = me >= LANES, me < n - LANES
    barrier = pltpu.get_barrier_semaphore()

    def greet(other):
        pl.semaphore_signal(barrier, inc=1, device_id={"gx": other}, device_id_type=MESH)

    sides = (
        (has_prev & (member == 0), me - 1),
        (has_next & (member == LANES - 1), me + 1),
        (has_down, me - LANES),
        (has_up, me + LANES),
    )
    for k in range(1, LANES):
        greet(peer(k))
    peers = LANES - 1
    for there, other in sides:
        pl.when(there)(functools.partial(greet, other))
        peers = peers + jnp.where(there, 1, 0)

    def remote(src, dst, send, recv, other):
        return pltpu.make_async_remote_copy(
            src_ref=src,
            dst_ref=dst,
            send_sem=send,
            recv_sem=recv,
            device_id={"gx": other},
            device_id_type=MESH,
        )

    def face_copies(outgoing, incoming, phase):
        up = remote(
            outgoing.at[0],
            incoming.at[0],
            face_send_sem.at[phase, 0],
            face_recv_sem.at[phase, 0],
            me + 1,
        )
        down = remote(
            outgoing.at[1],
            incoming.at[1],
            face_send_sem.at[phase, 1],
            face_recv_sem.at[phase, 1],
            me - 1,
        )
        return up, down

    def start_pair(up, up_there, down, down_there):
        pl.when(up_there)(up.start)
        pl.when(down_there)(down.start)

    def finish_pair(up, up_there, down, down_there):
        @pl.when(down_there)
        def _():
            up.wait_recv()
            down.wait_send()

        @pl.when(up_there)
        def _():
            down.wait_recv()
            up.wait_send()


    cube = (edge, edge, edge, width)
    face = (edge, edge, width)
    base = edge
    padded = (edge + 2) * edge
    own_taps = range(9, 18)
    far_taps = (*range(9), *range(18, 27))
    zero_brick = jnp.zeros(cube, F32)
    zero_plane = jnp.zeros(face, F32)
    table[slots] = zero_brick
    enc[slots] = zero_brick

    def stage_faces(outgoing, source, last, s):
        up_from = jnp.where(fine_send[0, s] >= 0, s, slots)
        down_from = jnp.where(fine_send[1, s] >= 0, s, slots)
        rows = outgoing.shape[2]
        outgoing[0, s] = source[up_from, last].reshape(rows, width).astype(BF16)
        outgoing[1, s] = source[down_from, 0].reshape(rows, width).astype(BF16)

    loaded(0)
    for s in range(slots):
        table[s] = feat[s].astype(F32).reshape(cube)
    for copy in small:
        copy.wait()
    meta[member, 0:per, 0 : child_ref.shape[1]] = child_ref[...]
    meta[member, per : 2 * per, 0 : nbr_ref.shape[1]] = nbr_ref[...]
    meta[member, 2 * per : 2 * per + 1, 0:slots] = parent_row[...]
    for s in range(slots):
        stage_faces(face_out, table, edge - 1, s)
    halo1 = face_copies(face_out, face_in, 0)
    halo2 = face_copies(face_out2, face_in2, 1)
    halo3 = face_copies(face_out3, face_in3, 2)
    meta_copies = [
        remote(
            meta.at[member],
            meta.at[member],
            meta_send_sem.at[k - 1],
            meta_recv_sem.at[k - 1],
            peer(k),
        )
        for k in range(1, LANES)
    ]

    below[slots] = zero_plane
    above[slots] = zero_plane
    coarse[bricks] = zero_brick
    coarse2[bricks] = zero_brick
    low_x[3 * bricks] = zero_plane
    high_x[3 * bricks] = zero_plane
    children[LANES * slots] = jnp.zeros((block, width), F32)
    utab[slots] = jnp.zeros((half, half, edge, width), F32)
    ubelow[slots] = jnp.zeros((half, edge, width), F32)
    uabove[slots] = jnp.zeros((half, edge, width), F32)

    def assemble(target, side, centre, lower, upper, index, taps):
        for t in taps:
            dx, dy, dz = t // 9 - 1, t // 3 % 3 - 1, t % 3 - 1
            at = index(t)
            ys, zs = pick(dy, side), pick(dz, edge)
            if dx == 0:
                piece = centre[at, :, ys, zs, :]
            elif dx < 0:
                piece = lower[at, ys, zs, :][None]
            else:
                piece = upper[at, ys, zs, :][None]
            target[place(dx, side, 1), place(dy, side, 1), place(dz, edge, base), :] = piece

    def shift(store, row, source, x, y, count):
        rows = count * edge
        for dz in range(3):
            first = base + dz - 1
            piece = source[x, y, first : first + edge, :]
            store[dz, pl.ds(row, rows), :] = piece.reshape(rows, width).astype(BF16)

    def columns(store, starts, rows, offsets=(0, 1, 2)):
        return jnp.concatenate(
            [
                jnp.concatenate(
                    [store[dz, r + dy * edge : r + dy * edge + rows, :] for r in starts], axis=0
                )
                for dy in offsets
                for dz in range(3)
            ],
            axis=1,
        )

    def taps(weights, *sides):
        return jnp.concatenate([weights[dx] for dx in sides], axis=1)

    def dot(a, b):
        return jnp.dot(a, b, preferred_element_type=F32)

    def stepped(store, start, rows, weight):
        third = 3 * width
        first, middle, last = (weight[i * third : (i + 1) * third, :] for i in range(3))
        both = jnp.concatenate(
            [
                jnp.concatenate([first, middle], axis=1),
                jnp.concatenate([jnp.zeros((third, width), BF16), last], axis=1),
            ],
            axis=0,
        )
        return dot(columns(store, [start], rows, (0, 1)), both)

    def tread(value, at):
        row = at * padded
        return value[row : row + plane, 0:width] + value[row + edge : row + edge + plane, width:]

    def local_product(centre, index, weights):
        assemble(pad, edge, centre, None, None, index, own_taps)
        starts = [x * padded for x in range(edge)]
        for x in range(edge):
            shift(zs, x * padded, pad, x + 1, slice(None), edge + 2)
        two = dot(columns(zs, starts, plane), taps(weights, 0, 1))
        third = stepped(zs, padded, (edge - 1) * padded, weights[2])
        totals = []
        for x in range(edge):
            total = two[x * plane : (x + 1) * plane, width : 2 * width]
            if x > 0:
                total = total + two[(x - 1) * plane : x * plane, 0:width]
            if x < edge - 1:
                total = total + tread(third, x)
            totals.append(total)
        return totals

    def outer_planes(count, lower, upper, index_of, weights, store):
        @pl.loop(0, count)
        def _(j):
            assemble(pad, edge, None, lower, upper, index_of(j), far_taps)
            for side in range(2):
                row = pl.multiple_of((side * count + j) * padded, edge)
                shift(zfar, row, pad, side * (edge + 1), slice(None), edge + 2)

        for side in range(2):
            added = stepped(zfar, side * count * padded, count * padded, weights[2 * side])
            for j in range(count):
                store(j, side, tread(added, j))

    def rounded(value):
        return jnp.maximum(value, 0.0).astype(BF16).astype(F32)

    def fine_index(b):
        def index(t):
            at = fine_nbr[b, t]
            return jnp.where(at >= 0, at, slots)

        return index

    def take_faces(incoming, low, high):
        shape = low.shape[1:]
        for s in range(slots):
            low[s] = incoming[0, s].astype(F32).reshape(shape)
            high[s] = incoming[1, s].astype(F32).reshape(shape)

    cells = half * half

    def pool_copy(k, b):
        if b is None:
            source, at = pooled_out.at[member], slots
        else:
            source, at = pooled.at[member, b], b
        return remote(
            source, source, pool_send_sem.at[k - 1, at], pool_recv_sem.at[k - 1, at], peer(k)
        )

    def pool(value, count):
        pairs = value.reshape(count, 2, half, 2, edge, width)
        summed = (pairs[:, 0, :, 0] + pairs[:, 0, :, 1]) + (pairs[:, 1, :, 0] + pairs[:, 1, :, 1])
        half_z[0 : count * half * edge, :] = summed.reshape(count * half * edge, width)
        even = half_z[pl.ds(0, count * cells, stride=2), :]
        odd = half_z[pl.ds(1, count * cells, stride=2), :]
        return ((even + odd) * 0.125).astype(BF16)

    def side_copies(outgoing, incoming, phase):
        up = remote(
            outgoing,
            incoming.at[0],
            side_send_sem.at[phase, 0],
            side_recv_sem.at[phase, 0],
            me + LANES,
        )
        down = remote(
            outgoing,
            incoming.at[1],
            side_send_sem.at[phase, 1],
            side_recv_sem.at[phase, 1],
            me - LANES,
        )
        return up, down

    pl.semaphore_wait(barrier, peers)
    for copy in meta_copies:
        copy.start()
    start_pair(halo1[0], has_next, halo1[1], has_prev)
    loaded(1)

    def encode(b):
        totals = local_product(table, fine_index(b), w1)
        opened[b, 0] = totals[0]
        opened[b, 1] = totals[edge - 1]
        value = rounded(jnp.concatenate(totals[1 : edge - 1], axis=0))
        value = value.reshape((edge - 2,) + face)
        enc[b, 1 : edge - 1] = value
        pooled[member, b] = pool(value[1 : edge - 3], half - 2)

    def send_pooled(b):
        for k in range(1, LANES):
            pool_copy(k, b).start()

    encode(0)
    send_pooled(0)

    @pl.loop(1, slots)
    def _(b):
        encode(b)
        send_pooled(b)

    finish_pair(halo1[0], has_next, halo1[1], has_prev)
    take_faces(face_in, below, above)

    for copy in meta_copies:
        copy.wait()
    to_smem = pltpu.make_async_copy(meta, meta_s, meta_sem)
    to_smem.start()
    hop_meta = side_copies(meta, meta_far, 2)
    start_pair(hop_meta[0], has_up, hop_meta[1], has_down)
    def store_enc(b, side, added):
        enc[b, side * (edge - 1)] = rounded(opened[b, side] + added).reshape(face)

    outer_planes(slots, below, above, fine_index, w1, store_enc)
    for b in range(slots):
        pooled_out[member, b, 0] = pool(enc[b, 0:2], 1)
        pooled_out[member, b, 1] = pool(enc[b, edge - 2 : edge], 1)
    for k in range(1, LANES):
        pool_copy(k, None).start()
    for s in range(slots):
        stage_faces(face_out2, enc, edge - 1, s)

    loaded(4)

    def decode_part(b):
        totals = local_product(enc, fine_index(b), w4)
        acc[b] = jnp.concatenate(totals, axis=0)

    def run_decode(first, last):
        @pl.loop(first, last)
        def _(b):
            decode_part(b)

    strips = 4
    span = width // strips

    @pl.loop(0, 3 * strips)
    def _(i):
        dz, strip_at = lax.div(i, strips), lax.rem(i, strips)
        rows = []
        for dy in range(3):
            start = pl.multiple_of((dy * 3 + dz) * width + strip_at * span, span)
            rows.append([w4[dx, pl.ds(start, span), :].astype(F32) for dx in range(3)])
        late = [r1 + r2 for r1, r2 in zip(rows[1], rows[2])]
        early = [r0 + r1 for r0, r1 in zip(rows[0], rows[1])]
        for py, parts in enumerate(((rows[0], late), (early, rows[2]))):
            for q, (a, b, c) in enumerate(parts):
                start = pl.multiple_of((q * 3 + dz) * width + strip_at * span, span)
                wup[py, pl.ds(start, span), :] = jnp.concatenate(
                    [b + c, a + b, a, c], axis=1
                ).astype(BF16)

    run_decode(0, SPLIT)

    to_smem.wait()
    finish_pair(hop_meta[0], has_up, hop_meta[1], has_down)

    def far_to_smem(side):
        return pltpu.make_async_copy(meta_far.at[side], meta_far_s.at[side], far_sem.at[side])

    pl.when(has_down)(lambda: far_to_smem(0).start())
    pl.when(has_up)(lambda: far_to_smem(1).start())
    for k in range(1, LANES):
        for b in (*range(slots), None):
            pool_copy(k, b).wait()
    for lane in range(LANES):
        for s in range(slots):
            octant = lax.rem(jnp.maximum(meta_s[lane, 2 * per, s], 0), 8)
            side_out[lane * slots + s] = pooled_out[lane, s, lax.div(octant, 4)]
    copies = side_copies(side_out, side_in, 0)
    start_pair(copies[0], has_up, copies[1], has_down)
    start_pair(halo2[0], has_next, halo2[1], has_prev)
    for lane in range(LANES):
        for s in range(slots):
            at = lane * slots + s
            children[at, cells : block - cells] = pooled[lane, s].astype(F32)
            children[at, 0:cells] = pooled_out[lane, s, 0].astype(F32)
            children[at, block - cells : block] = pooled_out[lane, s, 1].astype(F32)

    def child_at(child):
        safe = jnp.maximum(child, 0)
        at = lax.rem(lax.div(safe, slots), LANES) * slots + lax.rem(safe, slots)
        return jnp.where(child >= 0, at, LANES * slots)

    def owner_of(value):
        value = jnp.maximum(value, 0)
        return lax.div(value, per), lax.rem(value, per)

    @pl.loop(0, bricks)
    def _(j):
        lane, slot = lax.div(j, per), lax.rem(j, per)
        for o in range(8):
            at = child_at(meta_s[lane, slot, o])
            ox, oy, oz = o // 4 * half, o // 2 % 2 * half, o % 2 * half
            for x in range(half):
                for y in range(half):
                    row = (x * half + y) * half
                    coarse[j, ox + x, oy + y, oz : oz + half, :] = children[
                        at, row : row + half, :
                    ]

    def coarse_index(lane, slot, live):
        def index(t):
            value = meta_s[lane, per + slot, t]
            there = (value >= 0) & live
            device, at = owner_of(value)
            at = lax.rem(device, LANES) * per + at
            if t // 9 == 1:
                return jnp.where(there, at, bricks)
            at = at + (lax.div(device, LANES) - group + 1) * bricks
            at = jnp.minimum(jnp.maximum(at, 0), 3 * bricks)
            return jnp.where(there, at, 3 * bricks)

        return index

    def keep_sides(source):
        for j in range(bricks):
            low_x[bricks + j] = source[j, 0]
            high_x[bricks + j] = source[j, edge - 1]

    def send_sides(source, outgoing, incoming, phase):
        for j in range(bricks):
            outgoing[j, 0] = source[j, 0].reshape(plane, width).astype(BF16)
            outgoing[j, 1] = source[j, edge - 1].reshape(plane, width).astype(BF16)
        up, down = side_copies(outgoing, incoming, phase)
        start_pair(up, has_up, down, has_down)
        keep_sides(source)
        return up, down

    def place_far(side):
        start = 2 * bricks * side
        for at in range(LANES * slots):
            far_children[side, at] = side_in[side, at].astype(F32)
        far_children[side, LANES * slots] = jnp.zeros((cells, width), F32)

        @pl.loop(0, bricks)
        def _(j):
            lane, slot = lax.div(j, per), lax.rem(j, per)
            for o in range(8):
                at = child_at(meta_far_s[side, lane, slot, o])
                oy, oz = o // 2 % 2 * half, o % 2 * half
                target = high_x if o // 4 else low_x
                for y in range(half):
                    target[start + j, oy + y, oz : oz + half, :] = far_children[
                        side, at, y * half : (y + 1) * half, :
                    ]

    def take_sides(copies, incoming):
        finish_pair(copies[0], has_up, copies[1], has_down)
        for side, start in ((0, 0), (1, 2 * bricks)):
            for j in range(bricks):
                low_x[start + j] = incoming[side, j, 0].astype(F32).reshape(face)
                high_x[start + j] = incoming[side, j, 1].astype(F32).reshape(face)

    def group_index(j):
        return coarse_index(lax.div(j, per), lax.rem(j, per), True)

    keep_sides(coarse)
    loaded(2)

    @pl.loop(0, bricks)
    def _(j):
        totals = local_product(coarse, group_index(j), w2)
        opened[j, 0] = totals[0]
        opened[j, 1] = totals[edge - 1]
        value = rounded(jnp.concatenate(totals[1 : edge - 1], axis=0))
        coarse2[j, 1 : edge - 1] = value.reshape((edge - 2,) + face)

    finish_pair(copies[0], has_up, copies[1], has_down)
    pl.when(has_down)(lambda: far_to_smem(0).wait())
    pl.when(has_up)(lambda: far_to_smem(1).wait())
    pl.when(has_down)(lambda: place_far(0))
    pl.when(has_up)(lambda: place_far(1))

    def store_coarse(j, side, added):
        coarse2[j, side * (edge - 1)] = rounded(opened[j, side] + added).reshape(face)

    outer_planes(bricks, high_x, low_x, group_index, w2, store_coarse)
    copies = send_sides(coarse2, side_out2, side_in2, 1)
    loaded(3)

    part = half * edge
    strip = slots * part
    tall = half + 2
    column = tall * edge

    def parent_of(s):
        parent = fine_parent[s]
        safe = jnp.maximum(parent, 0)
        device, slot = owner_of(lax.div(safe, 8))
        octant = lax.rem(safe, 8)
        ox, oy = lax.div(octant, 4), lax.rem(lax.div(octant, 2), 2)
        return coarse_index(lax.rem(device, LANES), slot, parent >= 0), ox, oy * half

    pad[0] = jnp.zeros(pad.shape[1:], F32)
    pad[edge + 1] = jnp.zeros(pad.shape[1:], F32)

    @pl.loop(0, slots)
    def _(s):
        index, ox, oy = parent_of(s)
        assemble(pad, edge, coarse2, None, None, index, own_taps)
        for x in range(tall):
            row = pl.multiple_of((s * tall + x) * column, edge)
            shift(zq, row, pad, ox * half + x, pl.ds(oy, tall), tall)

    def starts_of(planes):
        return [(s * tall + x) * column for x in planes for s in range(slots)]

    two = dot(columns(zq, starts_of(range(half + 1)), part), taps(w3, 0, 1))
    third = dot(columns(zq, starts_of(range(2, tall)), part), w3[2])
    dacc[...] = third + two[0 : half * strip, 0:width] + two[strip:, width : 2 * width]

    run_decode(SPLIT, slots)
    finish_pair(halo2[0], has_next, halo2[1], has_prev)
    take_faces(face_in2, below, above)

    def store_part(b, side, added):
        at = side * (edge - 1) * plane
        acc[b, at : at + plane] = acc[b, at : at + plane] + added

    outer_planes(slots, below, above, fine_index, w4, store_part)
    take_sides(copies, side_in2)

    @pl.loop(0, slots)
    def _(s):
        index, ox, oy = parent_of(s)
        assemble(pad, edge, None, high_x, low_x, index, far_taps)
        row = pl.multiple_of(s * column, edge)
        shift(zfar, row, pad, ox * (edge + 1), pl.ds(oy, tall), tall)

    far = dot(
        columns(zfar, [s * column for s in range(slots)], part),
        taps(w3, 0, 2),
    )
    picks[0] = far[:, 0:width]
    picks[1] = jnp.zeros((strip, width), F32)
    picks[2] = far[:, width : 2 * width]
    for s in range(slots):
        _, ox, _ = parent_of(s)
        rows = slice(s * part, (s + 1) * part)
        low = picks[ox, rows]
        high = picks[ox + 1, rows]
        pieces = [dacc[x * strip + s * part : x * strip + (s + 1) * part, :] for x in range(half)]
        pieces[0] = pieces[0] + low
        pieces[half - 1] = pieces[half - 1] + high
        piece = rounded(jnp.concatenate(pieces, axis=0))
        oz = lax.rem(jnp.maximum(fine_parent[s], 0), 2)
        spread[s, pl.ds(0, half * part, stride=2), :] = piece
        spread[s, pl.ds(1, half * part, stride=2), :] = piece
        for x in range(half):
            for y in range(half):
                start = ((x * half + y) * 2 + oz) * edge
                utab[s, x, y] = spread[s, pl.ds(start, edge), :]
        stage_faces(face_out3, utab, half - 1, s)
    start_pair(halo3[0], has_next, halo3[1], has_prev)

    brick_rows = tall * column

    @pl.loop(0, slots)
    def _(b):
        assemble(upad, half, utab, None, None, fine_index(b), own_taps)
        for x in range(half):
            row = pl.multiple_of(b * brick_rows + (x + 1) * column, edge)
            shift(zu, row, upad, x + 1, slice(None), tall)

    def woven(zero, one):
        pair = jnp.stack(
            [zero.reshape(half, edge, width), one.reshape(half, edge, width)], axis=1
        )
        return pair.reshape(plane, width)

    inner = [b * brick_rows + (x + 1) * column for b in range(slots) for x in range(half)]
    direct, across = [], []
    for py in range(2):
        lhs = columns(zu, inner, part, (py, py + 1))
        direct.append(dot(lhs, wup[py, :, 0 : 2 * width]))
        across.append(dot(columns(zu, inner, part, (py, py + 1)), wup[py, :, 2 * width :]))

    for b in range(slots):
        for x in range(edge):
            i, px = x // 2, x % 2
            lanes = slice(px * width, (px + 1) * width)
            other = i - 1 + 2 * px
            sums = []
            for py in range(2):
                at = (b * half + i) * part
                value = direct[py][at : at + part, lanes]
                if 0 <= other < half:
                    at = (b * half + other) * part
                    value = value + across[py][at : at + part, lanes]
                sums.append(value)
            rows = slice(x * plane, (x + 1) * plane)
            total = acc[b, rows] + woven(*sums)
            if 0 <= other < half:
                out_ref[b, rows, :] = jnp.maximum(total, 0.0).astype(BF16)
            else:
                acc[b, rows] = total

    finish_pair(halo3[0], has_next, halo3[1], has_prev)
    take_faces(face_in3, ubelow, uabove)

    @pl.loop(0, slots)
    def _(b):
        assemble(upad, half, None, ubelow, uabove, fine_index(b), far_taps)
        for x in (0, half + 1):
            row = pl.multiple_of(b * brick_rows + x * column, edge)
            shift(zu, row, upad, x, slice(None), tall)

    for side in range(2):
        starts = [b * brick_rows + side * (half + 1) * column for b in range(slots)]
        lanes = slice((2 + side) * width, (3 + side) * width)
        sums = [dot(columns(zu, starts, part, (py, py + 1)), wup[py, :, lanes]) for py in range(2)]
        for b in range(slots):
            at = side * (edge - 1) * plane
            rows = slice(b * part, (b + 1) * part)
            total = acc[b, at : at + plane] + woven(sums[0][rows], sums[1][rows])
            out_ref[b, at : at + plane, :] = jnp.maximum(total, 0.0).astype(BF16)


def per_device(
    n,
    features,
    fine_nbr,
    fine_send,
    fine_parent,
    coarse_child,
    coarse_nbr,
    enc_fine_w,
    enc_coarse_w,
    dec_coarse_w,
    dec_fine_w,
):
    slots, edge, width = features.shape[0], features.shape[1], features.shape[-1]
    per = coarse_nbr.shape[0]
    bricks = LANES * per
    half = edge // 2
    plane = edge * edge
    voxels = edge**3
    padded = (edge + 2) * edge
    tall = half + 2
    rows = -(-(2 * per + 1) // 8) * 8
    kernels = [
        w.reshape(3, 9 * width, width)
        for w in (enc_fine_w, enc_coarse_w, dec_coarse_w, dec_fine_w)
    ]
    vmem = pltpu.VMEM
    vmem_spec = pl.BlockSpec(memory_space=pltpu.VMEM)
    any_spec = pl.BlockSpec(memory_space=pl.ANY)
    cube = (edge, edge, edge, width)
    face = (edge, edge, width)
    dma = pltpu.SemaphoreType.DMA
    out = pl.pallas_call(
        functools.partial(kernel, n),
        out_shape=pltpu.VMEM((slots, voxels, width), BF16),
        in_specs=[any_spec] * 11,
        out_specs=vmem_spec,
        scratch_shapes=[
            pltpu.SMEM(fine_nbr.shape, jnp.int32),
            pltpu.SMEM(fine_send.shape[1:], jnp.int32),
            pltpu.SMEM(fine_parent.shape, jnp.int32),
            vmem(coarse_child.shape, jnp.int32),
            vmem(coarse_nbr.shape, jnp.int32),
            vmem((1,) + fine_parent.shape, jnp.int32),
            vmem((slots, voxels, width), BF16),
            *[vmem((3, 9 * width, width), BF16)] * 4,
            vmem((2, 6 * width, 4 * width), BF16),
            vmem((edge + 2, edge + 2, 3 * edge, width), F32),
            vmem((half + 2, half + 2, 3 * edge, width), F32),
            vmem((3, edge * padded + edge, width), BF16),
            vmem((3, 2 * max(slots, bricks) * padded + edge, width), BF16),
            vmem((3, slots * tall * tall * edge, width), BF16),
            vmem((3, slots * tall * tall * edge, width), BF16),
            vmem((max(slots, bricks), 2, plane, width), F32),
            vmem((slots, voxels, width), F32),
            vmem((half * slots * half * edge, width), F32),
            vmem((3, slots * half * edge, width), F32),
            vmem((slots + 1, half, half, edge, width), F32),
            vmem((slots + 1, half, edge, width), F32),
            vmem((slots + 1, half, edge, width), F32),
            vmem((slots + 1,) + cube, F32),
            vmem((slots + 1,) + cube, F32),
            vmem((slots + 1,) + face, F32),
            vmem((slots + 1,) + face, F32),
            vmem((2, slots, plane, width), BF16),
            vmem((2, slots, plane, width), BF16),
            vmem((2, slots, plane, width), BF16),
            vmem((2, slots, plane, width), BF16),
            vmem((2, slots, half * edge, width), BF16),
            vmem((2, slots, half * edge, width), BF16),
            vmem((half * half * edge, width), F32),
            vmem((LANES, slots, (half - 2) * half**2, width), BF16),
            vmem((LANES, slots, 2, half**2, width), BF16),
            vmem((LANES * slots + 1, half**3, width), F32),
            vmem((LANES, rows, 128), jnp.int32),
            pltpu.SMEM((LANES, rows, 128), jnp.int32),
            vmem((2, LANES, rows, 128), jnp.int32),
            pltpu.SMEM((2, LANES, rows, 128), jnp.int32),
            vmem((2, LANES * slots + 1, half**2, width), F32),
            vmem((bricks + 1,) + cube, F32),
            vmem((bricks + 1,) + cube, F32),
            vmem((3 * bricks + 1,) + face, F32),
            vmem((3 * bricks + 1,) + face, F32),
            vmem((LANES * slots, half**2, width), BF16),
            vmem((2, LANES * slots, half**2, width), BF16),
            vmem((bricks, 2, plane, width), BF16),
            vmem((2, bricks, 2, plane, width), BF16),
            vmem((slots, half * half * 2 * edge, width), F32),
            dma((5,)),
            dma((6,)),
            dma((3, 2)),
            dma((3, 2)),
            dma((LANES - 1, slots + 1)),
            dma((LANES - 1, slots + 1)),
            dma((LANES - 1,)),
            dma((LANES - 1,)),
            dma((3, 2)),
            dma((3, 2)),
            dma(()),
            dma((2,)),
        ],
        compiler_params=pltpu.CompilerParams(
            collective_id=0, has_side_effects=True, vmem_limit_bytes=60 * 1024 * 1024
        ),
    )(
        fine_nbr,
        fine_send[0],
        fine_parent,
        coarse_child,
        coarse_nbr,
        fine_parent[None],
        features.reshape(slots, voxels, width),
        *kernels,
    )
    return out.reshape(features.shape)


def solution(mesh):
    lead = ("groups", "gx")
    placed = (
        P(lead, None, None, None, None),
        P(lead, None),
        P(lead, None, None),
        P(lead),
        P(lead, None),
        P(lead, None),
        P(),
        P(),
        P(),
        P(),
    )
    return jax.shard_map(
        functools.partial(per_device, mesh.shape["gx"]),
        mesh=mesh,
        in_specs=placed,
        out_specs=P(lead, None, None, None, None),
        check_vma=False,
    )
```

```python
import functools

import jax
import jax.numpy as jnp
from jax import lax
from jax.experimental import pallas as pl
from jax.experimental.pallas import tpu as pltpu
from jax.sharding import PartitionSpec as P

F32 = jnp.float32
BF16 = jnp.bfloat16
LANES = 4
MESH = pl.DeviceIdType.MESH


def pick(offset, edge):
    if offset < 0:
        return slice(edge - 1, edge)
    if offset == 0:
        return slice(0, edge)
    return slice(0, 1)


def place(offset, edge, base):
    if offset < 0:
        return slice(base - 1, base)
    if offset == 0:
        return slice(base, base + edge)
    return slice(base + edge, base + edge + 1)


def kernel(
    n,
    fine_nbr_hbm,
    fine_send_hbm,
    fine_parent_hbm,
    child_hbm,
    nbr_hbm,
    feat_hbm,
    w1_hbm,
    w2_hbm,
    w3_hbm,
    w4_hbm,
    out_ref,
    fine_nbr,
    fine_send,
    fine_parent,
    child_ref,
    nbr_ref,
    feat,
    w1,
    w2,
    w3,
    w4,
    wup,
    pad,
    upad,
    zs,
    zfar,
    zq,
    zu,
    opened,
    acc,
    dacc,
    picks,
    utab,
    ubelow,
    uabove,
    table,
    enc,
    below,
    above,
    face_out,
    face_in,
    face_out2,
    face_in2,
    face_out3,
    face_in3,
    half_z,
    pooled,
    pooled_out,
    own_out,
    children,
    meta,
    meta_s,
    meta_far,
    meta_far_s,
    far_children,
    coarse,
    coarse2,
    low_x,
    high_x,
    side_out,
    side_in,
    side_out2,
    side_in2,
    outer_in,
    inner_out,
    inner_in,
    spread,
    load_sem,
    small_sem,
    face_send_sem,
    face_recv_sem,
    pool_send_sem,
    pool_recv_sem,
    meta_send_sem,
    meta_recv_sem,
    side_send_sem,
    side_recv_sem,
    pair_send_sem,
    pair_recv_sem,
    ready_sem,
    meta_sem,
    far_sem,
):
    slots, edge = out_ref.shape[0], enc.shape[1]
    plane = edge * edge
    width = out_ref.shape[-1]
    half = edge // 2
    block = half**3
    per = child_ref.shape[0]
    bricks = LANES * per
    me = lax.axis_index("gx")
    member = lax.rem(me, LANES)
    group = lax.div(me, LANES)

    def peer(k):
        return me - member + (member ^ k)

    width = out_ref.shape[-1]
    loads = [[pltpu.make_async_copy(feat_hbm, feat, load_sem.at[0])]]
    for i, (src, dst) in enumerate(
        ((w1_hbm, w1), (w2_hbm, w2), (w3_hbm, w3), (w4_hbm, w4))
    ):
        loads.append([pltpu.make_async_copy(src, dst, load_sem.at[i + 1])])
    small = [
        pltpu.make_async_copy(src, dst, small_sem.at[i])
        for i, (src, dst) in enumerate(
            (
                (fine_nbr_hbm, fine_nbr),
                (fine_send_hbm, fine_send),
                (fine_parent_hbm, fine_parent),
                (child_hbm, child_ref),
                (nbr_hbm, nbr_ref),
            )
        )
    ]
    for copy in loads[0]:
        copy.start()
    for copy in small:
        copy.start()
    for copies in loads[1:]:
        for copy in copies:
            copy.start()

    def loaded(i):
        for copy in loads[i]:
            copy.wait()

    has_prev, has_next = me > 0, me < n - 1
    has_down, has_up = me >= LANES, me < n - LANES
    barrier = pltpu.get_barrier_semaphore()

    def greet(other):
        pl.semaphore_signal(barrier, inc=1, device_id={"gx": other}, device_id_type=MESH)

    for k in range(1, LANES):
        greet(peer(k))
    first = me - member
    sides = (
        (has_prev & (member == 0), me - 1),
        (has_next & (member == LANES - 1), me + 1),
        (has_down, me - LANES),
        (has_up, me + LANES),
    )
    peers = LANES - 1
    for there, other in sides:
        pl.when(there)(functools.partial(greet, other))
        peers = peers + jnp.where(there, 1, 0)

    def remote(src, dst, send, recv, other):
        return pltpu.make_async_remote_copy(
            src_ref=src,
            dst_ref=dst,
            send_sem=send,
            recv_sem=recv,
            device_id={"gx": other},
            device_id_type=MESH,
        )

    def face_copies(outgoing, incoming, phase):
        up = remote(
            outgoing.at[0],
            incoming.at[0],
            face_send_sem.at[phase, 0],
            face_recv_sem.at[phase, 0],
            me + 1,
        )
        down = remote(
            outgoing.at[1],
            incoming.at[1],
            face_send_sem.at[phase, 1],
            face_recv_sem.at[phase, 1],
            me - 1,
        )
        return up, down

    def start_pair(up, up_there, down, down_there):
        pl.when(up_there)(up.start)
        pl.when(down_there)(down.start)

    def finish_pair(up, up_there, down, down_there):
        @pl.when(down_there)
        def _():
            up.wait_recv()
            down.wait_send()

        @pl.when(up_there)
        def _():
            down.wait_recv()
            up.wait_send()


    cube = (edge, edge, edge, width)
    face = (edge, edge, width)
    base = edge
    padded = (edge + 2) * edge
    own_taps = range(9, 18)
    far_taps = (*range(9), *range(18, 27))
    zero_brick = jnp.zeros(cube, F32)
    zero_plane = jnp.zeros(face, F32)
    table[slots] = zero_brick
    enc[slots] = zero_brick

    def stage_faces(outgoing, source, last, s):
        up_from = jnp.where(fine_send[0, s] >= 0, s, slots)
        down_from = jnp.where(fine_send[1, s] >= 0, s, slots)
        rows = outgoing.shape[2]
        outgoing[0, s] = source[up_from, last].reshape(rows, width).astype(BF16)
        outgoing[1, s] = source[down_from, 0].reshape(rows, width).astype(BF16)

    loaded(0)
    for s in range(slots):
        table[s] = feat[s].astype(F32).reshape(cube)
    for copy in small:
        copy.wait()
    meta[member, 0:per, 0 : child_ref.shape[1]] = child_ref[...]
    meta[member, per : 2 * per, 0 : nbr_ref.shape[1]] = nbr_ref[...]
    for s in range(slots):
        stage_faces(face_out, table, edge - 1, s)
    halo1 = face_copies(face_out, face_in, 0)
    halo2 = face_copies(face_out2, face_in2, 1)
    halo3 = face_copies(face_out3, face_in3, 2)
    meta_copies = [
        remote(
            meta.at[member],
            meta.at[member],
            meta_send_sem,
            meta_recv_sem,
            peer(k),
        )
        for k in range(1, LANES)
    ]

    below[slots] = zero_plane
    above[slots] = zero_plane
    coarse[bricks] = zero_brick
    coarse2[bricks] = zero_brick
    low_x[3 * bricks] = zero_plane
    high_x[3 * bricks] = zero_plane
    children[LANES * slots] = jnp.zeros((block, width), F32)
    utab[slots] = jnp.zeros((half, half, edge, width), F32)
    ubelow[slots] = jnp.zeros((half, edge, width), F32)
    uabove[slots] = jnp.zeros((half, edge, width), F32)

    def assemble(target, side, centre, lower, upper, index, taps):
        for t in taps:
            dx, dy, dz = t // 9 - 1, t // 3 % 3 - 1, t % 3 - 1
            at = index(t)
            ys, zs = pick(dy, side), pick(dz, edge)
            if dx == 0:
                piece = centre[at, :, ys, zs, :]
            elif dx < 0:
                piece = lower[at, ys, zs, :][None]
            else:
                piece = upper[at, ys, zs, :][None]
            target[place(dx, side, 1), place(dy, side, 1), place(dz, edge, base), :] = piece

    def shift(store, row, source, x, y, count):
        rows = count * edge
        for dz in range(3):
            first = base + dz - 1
            piece = source[x, y, first : first + edge, :]
            store[dz, pl.ds(row, rows), :] = piece.reshape(rows, width).astype(BF16)

    def columns(store, starts, rows, offsets=(0, 1, 2)):
        return jnp.concatenate(
            [
                jnp.concatenate(
                    [store[dz, r + dy * edge : r + dy * edge + rows, :] for r in starts], axis=0
                )
                for dy in offsets
                for dz in range(3)
            ],
            axis=1,
        )

    def taps(weights, *sides):
        return jnp.concatenate([weights[dx] for dx in sides], axis=1)

    def dot(a, b):
        return jnp.dot(a, b, preferred_element_type=F32)

    def stepped(store, starts, rows, weight):
        third = 3 * width
        first, middle, last = (weight[i * third : (i + 1) * third, :] for i in range(3))
        both = jnp.concatenate(
            [
                jnp.concatenate([first, middle], axis=1),
                jnp.concatenate([jnp.zeros((third, width), BF16), last], axis=1),
            ],
            axis=0,
        )
        return dot(columns(store, starts, rows, (0, 1)), both)

    def tread(value, row, rows):
        return value[row : row + rows, 0:width] + value[row + edge : row + edge + rows, width:]

    def local_product(centre, index, weights):
        assemble(pad, edge, centre, None, None, index, own_taps)
        starts = [x * padded for x in range(edge)]
        for x in range(edge):
            shift(zs, x * padded, pad, x + 1, slice(None), edge + 2)
        two = dot(columns(zs, starts, plane), taps(weights, 0, 1))
        third = stepped(zs, [padded], (edge - 1) * padded, weights[2])
        totals = []
        for x in range(edge):
            total = two[x * plane : (x + 1) * plane, width : 2 * width]
            if x > 0:
                total = total + two[(x - 1) * plane : x * plane, 0:width]
            if x < edge - 1:
                total = total + tread(third, x * padded, plane)
            totals.append(total)
        return totals

    def outer_planes(count, lower, upper, index_of, weights, store):
        @pl.loop(0, count)
        def _(j):
            assemble(pad, edge, None, lower, upper, index_of(j), far_taps)
            for side in range(2):
                row = pl.multiple_of((side * count + j) * padded, edge)
                shift(zfar, row, pad, side * (edge + 1), slice(None), edge + 2)

        for side in range(2):
            added = stepped(zfar, [side * count * padded], count * padded, weights[2 * side])
            for j in range(count):
                store(j, side, tread(added, j * padded, plane))

    def rounded(value):
        return jnp.maximum(value, 0.0).astype(BF16).astype(F32)

    def fine_index(b):
        def index(t):
            at = fine_nbr[b, t]
            return jnp.where(at >= 0, at, slots)

        return index

    def take_faces(incoming, low, high):
        shape = low.shape[1:]
        for s in range(slots):
            low[s] = incoming[0, s].astype(F32).reshape(shape)
            high[s] = incoming[1, s].astype(F32).reshape(shape)

    cells = half * half

    def pool_copy(k, b):
        source = pooled_out.at[member] if b is None else pooled.at[member, b]
        stage = int(b is None)
        return remote(
            source, source, pool_send_sem.at[stage], pool_recv_sem.at[stage], peer(k)
        )

    def all_pooled(stage):
        source = (pooled, pooled_out)[stage].at[0 : LANES - 1]
        return remote(
            source, source, pool_send_sem.at[stage], pool_recv_sem.at[stage], peer(1)
        )

    def pool(value, count):
        pairs = value.reshape(count, 2, half, 2, edge, width)
        summed = (pairs[:, 0, :, 0] + pairs[:, 0, :, 1]) + (pairs[:, 1, :, 0] + pairs[:, 1, :, 1])
        half_z[0 : count * half * edge, :] = summed.reshape(count * half * edge, width)
        even = half_z[pl.ds(0, count * cells, stride=2), :]
        odd = half_z[pl.ds(1, count * cells, stride=2), :]
        return ((even + odd) * 0.125).astype(BF16)

    def side_copies(outgoing, incoming, phase):
        up = remote(
            outgoing,
            incoming.at[0],
            side_send_sem.at[phase, 0],
            side_recv_sem.at[phase, 0],
            me + LANES,
        )
        down = remote(
            outgoing,
            incoming.at[1],
            side_send_sem.at[phase, 1],
            side_recv_sem.at[phase, 1],
            me - LANES,
        )
        return up, down

    pl.semaphore_wait(barrier, peers)
    for k in range(1, LANES):
        pl.semaphore_signal(ready_sem, inc=1, device_id={"gx": peer(k)}, device_id_type=MESH)
    for copy in meta_copies:
        copy.start()
    start_pair(halo1[0], has_next, halo1[1], has_prev)
    loaded(1)

    def encode(b):
        totals = local_product(table, fine_index(b), w1)
        opened[b, 0] = totals[0]
        opened[b, 1] = totals[edge - 1]
        value = rounded(jnp.concatenate(totals[1 : edge - 1], axis=0))
        value = value.reshape((edge - 2,) + face)
        enc[b, 1 : edge - 1] = value
        pooled[member, b] = pool(value[1 : edge - 3], half - 2)

    def send_pooled(b):
        for k in range(1, LANES):
            pool_copy(k, b).start()


    @pl.loop(0, slots)
    def _(b):
        encode(b)
        send_pooled(b)

    finish_pair(halo1[0], has_next, halo1[1], has_prev)
    take_faces(face_in, below, above)

    every_meta = meta.at[0 : LANES - 1]
    remote(every_meta, every_meta, meta_send_sem, meta_recv_sem, peer(1)).wait()
    to_smem = pltpu.make_async_copy(meta, meta_s, meta_sem)
    to_smem.start()
    hop_meta = side_copies(meta, meta_far, 2)
    start_pair(hop_meta[0], has_up, hop_meta[1], has_down)
    def store_enc(b, side, added):
        enc[b, side * (edge - 1)] = rounded(opened[b, side] + added).reshape(face)

    outer_planes(slots, below, above, fine_index, w1, store_enc)
    for b in range(slots):
        for side in range(2):
            start = side * (edge - 2)
            value = pool(enc[b, start : start + 2], 1)
            pooled_out[member, b, side] = value
            own_out[b, side] = value
    for k in range(1, LANES):
        pool_copy(k, None).start()
    for s in range(slots):
        octant = lax.rem(jnp.maximum(fine_parent[s], 0), 8)
        side_out[s] = own_out[s, lax.div(octant, 4)]

    def face_to(side, lane):
        return remote(
            side_out,
            side_in.at[side, member],
            side_send_sem.at[0, side],
            side_recv_sem.at[0, side],
            first + (LANES if side == 0 else -LANES) + lane,
        )

    def faces_to(side):
        for lane in range(LANES):
            face_to(side, lane).start()

    pl.semaphore_wait(ready_sem, LANES - 1)
    pl.when(has_up)(lambda: faces_to(0))
    pl.when(has_down)(lambda: faces_to(1))
    for s in range(slots):
        stage_faces(face_out2, enc, edge - 1, s)

    loaded(4)

    def decode_part(b):
        totals = local_product(enc, fine_index(b), w4)
        acc[b] = jnp.concatenate(totals, axis=0)

    def run_decode(first, last):
        @pl.loop(first, last)
        def _(b):
            decode_part(b)

    strips = 4
    span = width // strips

    @pl.loop(0, 3 * strips)
    def _(i):
        dz, strip_at = lax.div(i, strips), lax.rem(i, strips)
        rows = []
        for dy in range(3):
            start = pl.multiple_of((dy * 3 + dz) * width + strip_at * span, span)
            rows.append([w4[dx, pl.ds(start, span), :].astype(F32) for dx in range(3)])
        late = [r1 + r2 for r1, r2 in zip(rows[1], rows[2])]
        early = [r0 + r1 for r0, r1 in zip(rows[0], rows[1])]
        for py, parts in enumerate(((rows[0], late), (early, rows[2]))):
            for q, (a, b, c) in enumerate(parts):
                start = pl.multiple_of((q * 3 + dz) * width + strip_at * span, span)
                wup[py, pl.ds(start, span), :] = jnp.concatenate(
                    [b + c, a + b, a, c], axis=1
                ).astype(BF16)

    run_decode(0, slots)

    to_smem.wait()
    finish_pair(hop_meta[0], has_up, hop_meta[1], has_down)

    def far_to_smem(side):
        return pltpu.make_async_copy(meta_far.at[side], meta_far_s.at[side], far_sem.at[side])

    pl.when(has_down)(lambda: far_to_smem(0).start())
    pl.when(has_up)(lambda: far_to_smem(1).start())
    for stage in range(2):
        all_pooled(stage).wait()
    start_pair(halo2[0], has_next, halo2[1], has_prev)
    for lane in range(LANES):
        for s in range(slots):
            at = lane * slots + s
            children[at, cells : block - cells] = pooled[lane, s].astype(F32)
            children[at, 0:cells] = pooled_out[lane, s, 0].astype(F32)
            children[at, block - cells : block] = pooled_out[lane, s, 1].astype(F32)

    def child_at(child):
        safe = jnp.maximum(child, 0)
        at = lax.rem(lax.div(safe, slots), LANES) * slots + lax.rem(safe, slots)
        return jnp.where(child >= 0, at, LANES * slots)

    def owner_of(value):
        value = jnp.maximum(value, 0)
        return lax.div(value, per), lax.rem(value, per)

    @pl.loop(0, bricks)
    def _(j):
        lane, slot = lax.div(j, per), lax.rem(j, per)
        for o in range(8):
            at = child_at(meta_s[lane, slot, o])
            ox, oy, oz = o // 4 * half, o // 2 % 2 * half, o % 2 * half
            for x in range(half):
                for y in range(half):
                    row = (x * half + y) * half
                    coarse[j, ox + x, oy + y, oz : oz + half, :] = children[
                        at, row : row + half, :
                    ]

    def coarse_index(lane, slot, live):
        def index(t):
            value = meta_s[lane, per + slot, t]
            there = (value >= 0) & live
            device, at = owner_of(value)
            at = lax.rem(device, LANES) * per + at
            if t // 9 == 1:
                return jnp.where(there, at, bricks)
            at = at + (lax.div(device, LANES) - group + 1) * bricks
            at = jnp.minimum(jnp.maximum(at, 0), 3 * bricks)
            return jnp.where(there, at, 3 * bricks)

        return index

    def keep_sides(source):
        for j in range(bricks):
            low_x[bricks + j] = source[j, 0]
            high_x[bricks + j] = source[j, edge - 1]

    own = bricks // 2
    parity = lax.rem(member, 2)

    def brick_of(i, odd):
        return (2 * lax.div(i, per) + odd) * per + lax.rem(i, per)

    def place_far(side):
        start = 2 * bricks * side
        for lane in range(LANES):
            for s in range(slots):
                far_children[side, lane * slots + s] = side_in[side, lane, s].astype(F32)
        far_children[side, LANES * slots] = jnp.zeros((cells, width), F32)

        @pl.loop(0, bricks)
        def _(j):
            lane, slot = lax.div(j, per), lax.rem(j, per)
            for o in range(8):
                at = child_at(meta_far_s[side, lane, slot, o])
                oy, oz = o // 2 % 2 * half, o % 2 * half
                target = high_x if o // 4 else low_x
                for y in range(half):
                    target[start + j, oy + y, oz : oz + half, :] = far_children[
                        side, at, y * half : (y + 1) * half, :
                    ]

    def group_index(j):
        return coarse_index(lax.div(j, per), lax.rem(j, per), True)

    keep_sides(coarse)
    loaded(2)

    def own_index(i):
        return group_index(brick_of(i, parity))

    def inner_copy(i):
        return remote(
            inner_out.at[i], inner_in.at[i], pair_send_sem.at[0], pair_recv_sem.at[0], peer(1)
        )

    @pl.loop(0, own)
    def _(i):
        totals = local_product(coarse, own_index(i), w2)
        opened[i, 0] = totals[0]
        opened[i, 1] = totals[edge - 1]
        value = jnp.maximum(jnp.concatenate(totals[1 : edge - 1], axis=0), 0.0).astype(BF16)
        inner_out[i] = value
        coarse2[brick_of(i, parity), 1 : edge - 1] = value.astype(F32).reshape(
            (edge - 2,) + face
        )
        inner_copy(i).start()

    def all_faces(side):
        return remote(
            side_in.at[side],
            side_in.at[side],
            side_send_sem.at[0, side],
            side_recv_sem.at[0, side],
            me + (LANES if side == 0 else -LANES),
        )

    @pl.when(has_down)
    def _():
        all_faces(0).wait_recv()
        all_faces(1).wait_send()

    @pl.when(has_up)
    def _():
        all_faces(1).wait_recv()
        all_faces(0).wait_send()

    pl.when(has_down)(lambda: far_to_smem(0).wait())
    pl.when(has_up)(lambda: far_to_smem(1).wait())
    pl.when(has_down)(lambda: place_far(0))
    pl.when(has_up)(lambda: place_far(1))

    def store_coarse(i, side, added):
        value = jnp.maximum(opened[i, side] + added, 0.0).astype(BF16)
        side_out2[i, side] = value
        coarse2[brick_of(i, parity), side * (edge - 1)] = value.astype(F32).reshape(face)

    outer_planes(own, high_x, low_x, own_index, w2, store_coarse)

    def planes_to(side, k):
        return remote(
            side_out2,
            side_in2.at[side, parity],
            side_send_sem.at[1, side],
            side_recv_sem.at[1, side],
            peer(k) + (LANES if side == 0 else -LANES),
        )

    def all_planes(side):
        return remote(
            side_in2.at[side],
            side_in2.at[side],
            side_send_sem.at[1, side],
            side_recv_sem.at[1, side],
            me + (LANES if side == 0 else -LANES),
        )

    def send_planes(side):
        for k in range(2):
            planes_to(side, k).start()

    pl.when(has_up)(lambda: send_planes(0))
    pl.when(has_down)(lambda: send_planes(1))
    outer_copy = remote(
        side_out2, outer_in, pair_send_sem.at[1], pair_recv_sem.at[1], peer(1)
    )
    outer_copy.start()
    loaded(3)

    part = half * edge
    strip = slots * part
    tall = half + 2
    column = tall * edge

    def parent_of(s):
        parent = fine_parent[s]
        safe = jnp.maximum(parent, 0)
        device, slot = owner_of(lax.div(safe, 8))
        octant = lax.rem(safe, 8)
        ox, oy = lax.div(octant, 4), lax.rem(lax.div(octant, 2), 2)
        return coarse_index(lax.rem(device, LANES), slot, parent >= 0), ox, oy * half

    remote(inner_out, inner_in, pair_send_sem.at[0], pair_recv_sem.at[0], peer(1)).wait()
    outer_copy.wait()
    for i in range(own):
        at = brick_of(i, 1 - parity)
        coarse2[at, 1 : edge - 1] = inner_in[i].astype(F32).reshape((edge - 2,) + face)
        coarse2[at, 0] = outer_in[i, 0].astype(F32).reshape(face)
        coarse2[at, edge - 1] = outer_in[i, 1].astype(F32).reshape(face)
    keep_sides(coarse2)
    pad[0] = jnp.zeros(pad.shape[1:], F32)
    pad[edge + 1] = jnp.zeros(pad.shape[1:], F32)

    @pl.loop(0, slots)
    def _(s):
        index, ox, oy = parent_of(s)
        assemble(pad, edge, coarse2, None, None, index, own_taps)
        for x in range(tall):
            row = pl.multiple_of((s * tall + x) * column, edge)
            shift(zq, row, pad, ox * half + x, pl.ds(oy, tall), tall)

    def starts_of(planes):
        return [(s * tall + x) * column for x in planes for s in range(slots)]

    two = dot(columns(zq, starts_of(range(half + 1)), part), taps(w3, 0, 1))
    third = stepped(
        zq, [(s * tall + 2) * column for s in range(slots)], half * column, w3[2]
    )
    for x in range(half):
        for s in range(slots):
            at = x * strip + s * part
            dacc[at : at + part, :] = (
                two[at : at + part, 0:width]
                + two[at + strip : at + strip + part, width : 2 * width]
                + tread(third, (s * half + x) * column, part)
            )

    finish_pair(halo2[0], has_next, halo2[1], has_prev)
    take_faces(face_in2, below, above)

    def store_part(b, side, added):
        at = side * (edge - 1) * plane
        acc[b, at : at + plane] = acc[b, at : at + plane] + added

    outer_planes(slots, below, above, fine_index, w4, store_part)
    @pl.when(has_down)
    def _():
        all_planes(0).wait_recv()
        all_planes(1).wait_send()

    @pl.when(has_up)
    def _():
        all_planes(1).wait_recv()
        all_planes(0).wait_send()

    for side in range(2):
        for odd in range(2):
            for i in range(own):
                at = 2 * bricks * side + (2 * (i // per) + odd) * per + i % per
                low_x[at] = side_in2[side, odd, i, 0].astype(F32).reshape(face)
                high_x[at] = side_in2[side, odd, i, 1].astype(F32).reshape(face)


    @pl.loop(0, slots)
    def _(s):
        index, ox, oy = parent_of(s)
        assemble(pad, edge, None, high_x, low_x, index, far_taps)
        row = pl.multiple_of(s * column, edge)
        shift(zfar, row, pad, ox * (edge + 1), pl.ds(oy, tall), tall)

    far = dot(
        columns(zfar, [s * column for s in range(slots)], part),
        taps(w3, 0, 2),
    )
    picks[0] = far[:, 0:width]
    picks[1] = jnp.zeros((strip, width), F32)
    picks[2] = far[:, width : 2 * width]
    for s in range(slots):
        _, ox, _ = parent_of(s)
        rows = slice(s * part, (s + 1) * part)
        low = picks[ox, rows]
        high = picks[ox + 1, rows]
        pieces = [dacc[x * strip + s * part : x * strip + (s + 1) * part, :] for x in range(half)]
        pieces[0] = pieces[0] + low
        pieces[half - 1] = pieces[half - 1] + high
        piece = rounded(jnp.concatenate(pieces, axis=0))
        oz = lax.rem(jnp.maximum(fine_parent[s], 0), 2)
        spread[s, pl.ds(0, half * part, stride=2), :] = piece
        spread[s, pl.ds(1, half * part, stride=2), :] = piece
        for x in range(half):
            for y in range(half):
                start = ((x * half + y) * 2 + oz) * edge
                utab[s, x, y] = spread[s, pl.ds(start, edge), :]
        stage_faces(face_out3, utab, half - 1, s)
    start_pair(halo3[0], has_next, halo3[1], has_prev)

    brick_rows = tall * column

    @pl.loop(0, slots)
    def _(b):
        assemble(upad, half, utab, None, None, fine_index(b), own_taps)
        for x in range(half):
            row = pl.multiple_of(b * brick_rows + (x + 1) * column, edge)
            shift(zu, row, upad, x + 1, slice(None), tall)

    def woven(zero, one):
        pair = jnp.stack(
            [zero.reshape(half, edge, width), one.reshape(half, edge, width)], axis=1
        )
        return pair.reshape(plane, width)

    inner = [b * brick_rows + (x + 1) * column for b in range(slots) for x in range(half)]
    direct, across = [], []
    for py in range(2):
        lhs = columns(zu, inner, part, (py, py + 1))
        direct.append(dot(lhs, wup[py, :, 0 : 2 * width]))
        across.append(dot(columns(zu, inner, part, (py, py + 1)), wup[py, :, 2 * width :]))

    for b in range(slots):
        for x in range(edge):
            i, px = x // 2, x % 2
            lanes = slice(px * width, (px + 1) * width)
            other = i - 1 + 2 * px
            sums = []
            for py in range(2):
                at = (b * half + i) * part
                value = direct[py][at : at + part, lanes]
                if 0 <= other < half:
                    at = (b * half + other) * part
                    value = value + across[py][at : at + part, lanes]
                sums.append(value)
            rows = slice(x * plane, (x + 1) * plane)
            total = acc[b, rows] + woven(*sums)
            if 0 <= other < half:
                out_ref[b, rows, :] = jnp.maximum(total, 0.0).astype(BF16)
            else:
                acc[b, rows] = total

    finish_pair(halo3[0], has_next, halo3[1], has_prev)
    take_faces(face_in3, ubelow, uabove)

    @pl.loop(0, slots)
    def _(b):
        assemble(upad, half, None, ubelow, uabove, fine_index(b), far_taps)
        for x in (0, half + 1):
            row = pl.multiple_of(b * brick_rows + x * column, edge)
            shift(zu, row, upad, x, slice(None), tall)

    for side in range(2):
        starts = [b * brick_rows + side * (half + 1) * column for b in range(slots)]
        lanes = slice((2 + side) * width, (3 + side) * width)
        sums = [dot(columns(zu, starts, part, (py, py + 1)), wup[py, :, lanes]) for py in range(2)]
        for b in range(slots):
            at = side * (edge - 1) * plane
            rows = slice(b * part, (b + 1) * part)
            total = acc[b, at : at + plane] + woven(sums[0][rows], sums[1][rows])
            out_ref[b, at : at + plane, :] = jnp.maximum(total, 0.0).astype(BF16)


def per_device(
    n,
    features,
    fine_nbr,
    fine_send,
    fine_parent,
    coarse_child,
    coarse_nbr,
    enc_fine_w,
    enc_coarse_w,
    dec_coarse_w,
    dec_fine_w,
):
    slots, edge, width = features.shape[0], features.shape[1], features.shape[-1]
    per = coarse_nbr.shape[0]
    bricks = LANES * per
    half = edge // 2
    plane = edge * edge
    voxels = edge**3
    padded = (edge + 2) * edge
    tall = half + 2
    rows = -(-2 * per // 8) * 8
    kernels = [
        w.reshape(3, 9 * width, width)
        for w in (enc_fine_w, enc_coarse_w, dec_coarse_w, dec_fine_w)
    ]
    vmem = pltpu.VMEM
    vmem_spec = pl.BlockSpec(memory_space=pltpu.VMEM)
    any_spec = pl.BlockSpec(memory_space=pl.ANY)
    cube = (edge, edge, edge, width)
    face = (edge, edge, width)
    dma = pltpu.SemaphoreType.DMA
    out = pl.pallas_call(
        functools.partial(kernel, n),
        out_shape=pltpu.VMEM((slots, voxels, width), BF16),
        in_specs=[any_spec] * 10,
        out_specs=vmem_spec,
        scratch_shapes=[
            pltpu.SMEM(fine_nbr.shape, jnp.int32),
            pltpu.SMEM(fine_send.shape[1:], jnp.int32),
            pltpu.SMEM(fine_parent.shape, jnp.int32),
            vmem(coarse_child.shape, jnp.int32),
            vmem(coarse_nbr.shape, jnp.int32),
            vmem((slots, voxels, width), BF16),
            *[vmem((3, 9 * width, width), BF16)] * 4,
            vmem((2, 6 * width, 4 * width), BF16),
            vmem((edge + 2, edge + 2, 3 * edge, width), F32),
            vmem((half + 2, half + 2, 3 * edge, width), F32),
            vmem((3, edge * padded + edge, width), BF16),
            vmem((3, 2 * max(slots, bricks) * padded + edge, width), BF16),
            vmem((3, slots * tall * tall * edge + edge, width), BF16),
            vmem((3, slots * tall * tall * edge, width), BF16),
            vmem((max(slots, bricks), 2, plane, width), F32),
            vmem((slots, voxels, width), F32),
            vmem((half * slots * half * edge, width), F32),
            vmem((3, slots * half * edge, width), F32),
            vmem((slots + 1, half, half, edge, width), F32),
            vmem((slots + 1, half, edge, width), F32),
            vmem((slots + 1, half, edge, width), F32),
            vmem((slots + 1,) + cube, F32),
            vmem((slots + 1,) + cube, F32),
            vmem((slots + 1,) + face, F32),
            vmem((slots + 1,) + face, F32),
            vmem((2, slots, plane, width), BF16),
            vmem((2, slots, plane, width), BF16),
            vmem((2, slots, plane, width), BF16),
            vmem((2, slots, plane, width), BF16),
            vmem((2, slots, half * edge, width), BF16),
            vmem((2, slots, half * edge, width), BF16),
            vmem((half * half * edge, width), F32),
            vmem((LANES, slots, (half - 2) * half**2, width), BF16),
            vmem((LANES, slots, 2, half**2, width), BF16),
            vmem((slots, 2, half**2, width), BF16),
            vmem((LANES * slots + 1, half**3, width), F32),
            vmem((LANES, rows, 128), jnp.int32),
            pltpu.SMEM((LANES, rows, 128), jnp.int32),
            vmem((2, LANES, rows, 128), jnp.int32),
            pltpu.SMEM((2, LANES, rows, 128), jnp.int32),
            vmem((2, LANES * slots + 1, half**2, width), F32),
            vmem((bricks + 1,) + cube, F32),
            vmem((bricks + 1,) + cube, F32),
            vmem((3 * bricks + 1,) + face, F32),
            vmem((3 * bricks + 1,) + face, F32),
            vmem((slots, half**2, width), BF16),
            vmem((2, LANES, slots, half**2, width), BF16),
            vmem((bricks // 2, 2, plane, width), BF16),
            vmem((2, 2, bricks // 2, 2, plane, width), BF16),
            vmem((bricks // 2, 2, plane, width), BF16),
            vmem((bricks // 2, (edge - 2) * plane, width), BF16),
            vmem((bricks // 2, (edge - 2) * plane, width), BF16),
            vmem((slots, half * half * 2 * edge, width), F32),
            dma((5,)),
            dma((5,)),
            dma((3, 2)),
            dma((3, 2)),
            dma((2,)),
            dma((2,)),
            dma(()),
            dma(()),
            dma((3, 2)),
            dma((3, 2)),
            dma((2,)),
            dma((2,)),
            pltpu.SemaphoreType.REGULAR,
            dma(()),
            dma((2,)),
        ],
        compiler_params=pltpu.CompilerParams(
            collective_id=0, has_side_effects=True, vmem_limit_bytes=60 * 1024 * 1024
        ),
    )(
        fine_nbr,
        fine_send[0],
        fine_parent,
        coarse_child,
        coarse_nbr,
        features.reshape(slots, voxels, width),
        *kernels,
    )
    return out.reshape(features.shape)


def solution(mesh):
    lead = ("groups", "gx")
    placed = (
        P(lead, None, None, None, None),
        P(lead, None),
        P(lead, None, None),
        P(lead),
        P(lead, None),
        P(lead, None),
        P(),
        P(),
        P(),
        P(),
    )
    return jax.shard_map(
        functools.partial(per_device, mesh.shape["gx"]),
        mesh=mesh,
        in_specs=placed,
        out_specs=P(lead, None, None, None, None),
        check_vma=False,
    )
```

```python
import functools

import jax
import jax.numpy as jnp
from jax import lax
from jax.experimental import pallas as pl
from jax.experimental.pallas import tpu as pltpu
from jax.sharding import PartitionSpec as P

F32 = jnp.float32
BF16 = jnp.bfloat16
LANES = 4
MESH = pl.DeviceIdType.MESH


def pick(offset, edge):
    if offset < 0:
        return slice(edge - 1, edge)
    if offset == 0:
        return slice(0, edge)
    return slice(0, 1)


def place(offset, edge, base):
    if offset < 0:
        return slice(base - 1, base)
    if offset == 0:
        return slice(base, base + edge)
    return slice(base + edge, base + edge + 1)


def kernel(
    n,
    fine_nbr_hbm,
    fine_send_hbm,
    fine_parent_hbm,
    child_hbm,
    nbr_hbm,
    feat_hbm,
    w1_hbm,
    w2_hbm,
    w3_hbm,
    w4_hbm,
    out_ref,
    fine_nbr,
    fine_send,
    fine_parent,
    child_ref,
    nbr_ref,
    feat,
    w1,
    w2,
    w3,
    w4,
    wup,
    pad,
    upad,
    zs,
    zfar,
    zq,
    zu,
    opened,
    acc,
    dacc,
    picks,
    utab,
    ubelow,
    uabove,
    table,
    enc,
    below,
    above,
    face_out,
    face_in,
    face_out2,
    face_in2,
    face_out3,
    face_in3,
    half_z,
    pooled,
    pooled_out,
    own_out,
    children,
    meta,
    meta_s,
    meta_far,
    meta_far_s,
    far_children,
    coarse,
    coarse2,
    low_x,
    high_x,
    side_out,
    side_in,
    side_out2,
    side_in2,
    brick_out,
    brick_in,
    spread,
    load_sem,
    small_sem,
    face_send_sem,
    face_recv_sem,
    pool_send_sem,
    pool_recv_sem,
    meta_send_sem,
    meta_recv_sem,
    side_send_sem,
    side_recv_sem,
    pair_send_sem,
    pair_recv_sem,
    ready_sem,
    meta_sem,
    far_sem,
):
    slots, edge = out_ref.shape[0], enc.shape[1]
    plane = edge * edge
    width = out_ref.shape[-1]
    half = edge // 2
    block = half**3
    per = child_ref.shape[0]
    bricks = LANES * per
    me = lax.axis_index("gx")
    member = lax.rem(me, LANES)
    group = lax.div(me, LANES)

    def peer(k):
        return me - member + (member ^ k)

    width = out_ref.shape[-1]
    loads = [[pltpu.make_async_copy(feat_hbm, feat, load_sem.at[0])]]
    for i, (src, dst) in enumerate(
        ((w1_hbm, w1), (w2_hbm, w2), (w3_hbm, w3), (w4_hbm, w4))
    ):
        loads.append([pltpu.make_async_copy(src, dst, load_sem.at[i + 1])])
    small = [
        pltpu.make_async_copy(src, dst, small_sem.at[i])
        for i, (src, dst) in enumerate(
            (
                (fine_nbr_hbm, fine_nbr),
                (fine_send_hbm, fine_send),
                (fine_parent_hbm, fine_parent),
                (child_hbm, child_ref),
                (nbr_hbm, nbr_ref),
            )
        )
    ]
    for copy in loads[0]:
        copy.start()
    for copy in small:
        copy.start()
    for copies in loads[1:]:
        for copy in copies:
            copy.start()

    def loaded(i):
        for copy in loads[i]:
            copy.wait()

    has_prev, has_next = me > 0, me < n - 1
    has_down, has_up = me >= LANES, me < n - LANES
    barrier = pltpu.get_barrier_semaphore()

    def greet(other):
        pl.semaphore_signal(barrier, inc=1, device_id={"gx": other}, device_id_type=MESH)

    for k in range(1, LANES):
        greet(peer(k))
    first = me - member
    sides = (
        (has_prev & (member == 0), me - 1),
        (has_next & (member == LANES - 1), me + 1),
        (has_down, me - LANES),
        (has_up, me + LANES),
    )
    peers = LANES - 1
    for there, other in sides:
        pl.when(there)(functools.partial(greet, other))
        peers = peers + jnp.where(there, 1, 0)

    def remote(src, dst, send, recv, other):
        return pltpu.make_async_remote_copy(
            src_ref=src,
            dst_ref=dst,
            send_sem=send,
            recv_sem=recv,
            device_id={"gx": other},
            device_id_type=MESH,
        )

    def face_copies(outgoing, incoming, phase):
        up = remote(
            outgoing.at[0],
            incoming.at[0],
            face_send_sem.at[phase, 0],
            face_recv_sem.at[phase, 0],
            me + 1,
        )
        down = remote(
            outgoing.at[1],
            incoming.at[1],
            face_send_sem.at[phase, 1],
            face_recv_sem.at[phase, 1],
            me - 1,
        )
        return up, down

    def start_pair(up, up_there, down, down_there):
        pl.when(up_there)(up.start)
        pl.when(down_there)(down.start)

    def finish_pair(up, up_there, down, down_there):
        @pl.when(down_there)
        def _():
            up.wait_recv()
            down.wait_send()

        @pl.when(up_there)
        def _():
            down.wait_recv()
            up.wait_send()


    cube = (edge, edge, edge, width)
    face = (edge, edge, width)
    base = edge
    padded = (edge + 2) * edge
    own_taps = range(9, 18)
    far_taps = (*range(9), *range(18, 27))
    zero_brick = jnp.zeros(cube, F32)
    zero_plane = jnp.zeros(face, F32)
    table[slots] = zero_brick
    enc[slots] = zero_brick

    def stage_faces(outgoing, source, last, s):
        up_from = jnp.where(fine_send[0, s] >= 0, s, slots)
        down_from = jnp.where(fine_send[1, s] >= 0, s, slots)
        rows = outgoing.shape[2]
        outgoing[0, s] = source[up_from, last].reshape(rows, width).astype(BF16)
        outgoing[1, s] = source[down_from, 0].reshape(rows, width).astype(BF16)

    loaded(0)
    for s in range(slots):
        table[s] = feat[s].astype(F32).reshape(cube)
    for copy in small:
        copy.wait()
    meta[member, 0:per, 0 : child_ref.shape[1]] = child_ref[...]
    meta[member, per : 2 * per, 0 : nbr_ref.shape[1]] = nbr_ref[...]
    for s in range(slots):
        stage_faces(face_out, table, edge - 1, s)
    halo1 = face_copies(face_out, face_in, 0)
    halo2 = face_copies(face_out2, face_in2, 1)
    halo3 = face_copies(face_out3, face_in3, 2)
    meta_copies = [
        remote(
            meta.at[member],
            meta.at[member],
            meta_send_sem,
            meta_recv_sem,
            peer(k),
        )
        for k in range(1, LANES)
    ]

    below[slots] = zero_plane
    above[slots] = zero_plane
    coarse[bricks] = zero_brick
    coarse2[bricks] = zero_brick
    low_x[3 * bricks] = zero_plane
    high_x[3 * bricks] = zero_plane
    children[LANES * slots] = jnp.zeros((block, width), F32)
    utab[slots] = jnp.zeros((half, half, edge, width), F32)
    ubelow[slots] = jnp.zeros((half, edge, width), F32)
    uabove[slots] = jnp.zeros((half, edge, width), F32)

    def assemble(target, side, centre, lower, upper, index, taps):
        for t in taps:
            dx, dy, dz = t // 9 - 1, t // 3 % 3 - 1, t % 3 - 1
            at = index(t)
            ys, zs = pick(dy, side), pick(dz, edge)
            if dx == 0:
                piece = centre[at, :, ys, zs, :]
            elif dx < 0:
                piece = lower[at, ys, zs, :][None]
            else:
                piece = upper[at, ys, zs, :][None]
            target[place(dx, side, 1), place(dy, side, 1), place(dz, edge, base), :] = piece

    def shift(store, row, source, x, y, count):
        rows = count * edge
        for dz in range(3):
            first = base + dz - 1
            piece = source[x, y, first : first + edge, :]
            store[dz, pl.ds(row, rows), :] = piece.reshape(rows, width).astype(BF16)

    def columns(store, starts, rows, offsets=(0, 1, 2)):
        return jnp.concatenate(
            [
                jnp.concatenate(
                    [store[dz, r + dy * edge : r + dy * edge + rows, :] for r in starts], axis=0
                )
                for dy in offsets
                for dz in range(3)
            ],
            axis=1,
        )

    def taps(weights, *sides):
        return jnp.concatenate([weights[dx] for dx in sides], axis=1)

    def dot(a, b):
        return jnp.dot(a, b, preferred_element_type=F32)

    def stepped(store, starts, rows, weight):
        third = 3 * width
        first, middle, last = (weight[i * third : (i + 1) * third, :] for i in range(3))
        both = jnp.concatenate(
            [
                jnp.concatenate([first, middle], axis=1),
                jnp.concatenate([jnp.zeros((third, width), BF16), last], axis=1),
            ],
            axis=0,
        )
        return dot(columns(store, starts, rows, (0, 1)), both)

    def tread(value, row, rows):
        return value[row : row + rows, 0:width] + value[row + edge : row + edge + rows, width:]

    def local_product(centre, index, weights):
        assemble(pad, edge, centre, None, None, index, own_taps)
        starts = [x * padded for x in range(edge)]
        for x in range(edge):
            shift(zs, x * padded, pad, x + 1, slice(None), edge + 2)
        two = dot(columns(zs, starts, plane), taps(weights, 0, 1))
        third = stepped(zs, [padded], (edge - 1) * padded, weights[2])
        totals = []
        for x in range(edge):
            total = two[x * plane : (x + 1) * plane, width : 2 * width]
            if x > 0:
                total = total + two[(x - 1) * plane : x * plane, 0:width]
            if x < edge - 1:
                total = total + tread(third, x * padded, plane)
            totals.append(total)
        return totals

    def outer_planes(count, lower, upper, index_of, weights, store):
        @pl.loop(0, count)
        def _(j):
            assemble(pad, edge, None, lower, upper, index_of(j), far_taps)
            for side in range(2):
                row = pl.multiple_of((side * count + j) * padded, edge)
                shift(zfar, row, pad, side * (edge + 1), slice(None), edge + 2)

        for side in range(2):
            added = stepped(zfar, [side * count * padded], count * padded, weights[2 * side])
            for j in range(count):
                store(j, side, tread(added, j * padded, plane))

    def rounded(value):
        return jnp.maximum(value, 0.0).astype(BF16).astype(F32)

    def fine_index(b):
        def index(t):
            at = fine_nbr[b, t]
            return jnp.where(at >= 0, at, slots)

        return index

    def take_faces(incoming, low, high):
        shape = low.shape[1:]
        for s in range(slots):
            low[s] = incoming[0, s].astype(F32).reshape(shape)
            high[s] = incoming[1, s].astype(F32).reshape(shape)

    cells = half * half

    def pool_copy(k, b):
        source = pooled_out.at[member] if b is None else pooled.at[member, b]
        stage = int(b is None)
        return remote(
            source, source, pool_send_sem.at[stage], pool_recv_sem.at[stage], peer(k)
        )

    def all_pooled(stage):
        source = (pooled, pooled_out)[stage].at[0 : LANES - 1]
        return remote(
            source, source, pool_send_sem.at[stage], pool_recv_sem.at[stage], peer(1)
        )

    def pool(value, count):
        pairs = value.reshape(count, 2, half, 2, edge, width)
        summed = (pairs[:, 0, :, 0] + pairs[:, 0, :, 1]) + (pairs[:, 1, :, 0] + pairs[:, 1, :, 1])
        half_z[0 : count * half * edge, :] = summed.reshape(count * half * edge, width)
        even = half_z[pl.ds(0, count * cells, stride=2), :]
        odd = half_z[pl.ds(1, count * cells, stride=2), :]
        return ((even + odd) * 0.125).astype(BF16)

    def side_copies(outgoing, incoming, phase):
        up = remote(
            outgoing,
            incoming.at[0],
            side_send_sem.at[phase, 0],
            side_recv_sem.at[phase, 0],
            me + LANES,
        )
        down = remote(
            outgoing,
            incoming.at[1],
            side_send_sem.at[phase, 1],
            side_recv_sem.at[phase, 1],
            me - LANES,
        )
        return up, down

    pl.semaphore_wait(barrier, peers)
    for k in range(1, LANES):
        pl.semaphore_signal(ready_sem, inc=1, device_id={"gx": peer(k)}, device_id_type=MESH)
    for copy in meta_copies:
        copy.start()
    start_pair(halo1[0], has_next, halo1[1], has_prev)
    loaded(1)

    def encode(b):
        totals = local_product(table, fine_index(b), w1)
        opened[b, 0] = totals[0]
        opened[b, 1] = totals[edge - 1]
        value = rounded(jnp.concatenate(totals[1 : edge - 1], axis=0))
        value = value.reshape((edge - 2,) + face)
        enc[b, 1 : edge - 1] = value
        pooled[member, b] = pool(value[1 : edge - 3], half - 2)

    def send_pooled(b):
        for k in range(1, LANES):
            pool_copy(k, b).start()


    @pl.loop(0, slots)
    def _(b):
        encode(b)
        send_pooled(b)

    finish_pair(halo1[0], has_next, halo1[1], has_prev)
    take_faces(face_in, below, above)

    every_meta = meta.at[0 : LANES - 1]
    remote(every_meta, every_meta, meta_send_sem, meta_recv_sem, peer(1)).wait()
    to_smem = pltpu.make_async_copy(meta, meta_s, meta_sem)
    to_smem.start()
    hop_meta = side_copies(meta, meta_far, 2)
    start_pair(hop_meta[0], has_up, hop_meta[1], has_down)
    def store_enc(b, side, added):
        enc[b, side * (edge - 1)] = rounded(opened[b, side] + added).reshape(face)

    outer_planes(slots, below, above, fine_index, w1, store_enc)
    for b in range(slots):
        for side in range(2):
            start = side * (edge - 2)
            value = pool(enc[b, start : start + 2], 1)
            pooled_out[member, b, side] = value
            own_out[b, side] = value
    for k in range(1, LANES):
        pool_copy(k, None).start()
    for s in range(slots):
        octant = lax.rem(jnp.maximum(fine_parent[s], 0), 8)
        side_out[s] = own_out[s, lax.div(octant, 4)]

    def face_to(side, lane):
        return remote(
            side_out,
            side_in.at[side, member],
            side_send_sem.at[0, side],
            side_recv_sem.at[0, side],
            first + (LANES if side == 0 else -LANES) + lane,
        )

    def faces_to(side):
        for lane in range(LANES):
            face_to(side, lane).start()

    pl.semaphore_wait(ready_sem, LANES - 1)
    for s in range(slots):
        stage_faces(face_out2, enc, edge - 1, s)

    loaded(4)

    def decode_part(b):
        totals = local_product(enc, fine_index(b), w4)
        acc[b] = jnp.concatenate(totals, axis=0)

    def run_decode(first, last):
        @pl.loop(first, last)
        def _(b):
            decode_part(b)

            @pl.when(b == 0)
            def _():
                pl.when(has_up)(lambda: faces_to(0))
                pl.when(has_down)(lambda: faces_to(1))

    run_decode(0, slots)

    to_smem.wait()
    finish_pair(hop_meta[0], has_up, hop_meta[1], has_down)

    def far_to_smem(side):
        return pltpu.make_async_copy(meta_far.at[side], meta_far_s.at[side], far_sem.at[side])

    pl.when(has_down)(lambda: far_to_smem(0).start())
    pl.when(has_up)(lambda: far_to_smem(1).start())
    for stage in range(2):
        all_pooled(stage).wait()
    start_pair(halo2[0], has_next, halo2[1], has_prev)
    for lane in range(LANES):
        for s in range(slots):
            at = lane * slots + s
            children[at, cells : block - cells] = pooled[lane, s].astype(F32)
            children[at, 0:cells] = pooled_out[lane, s, 0].astype(F32)
            children[at, block - cells : block] = pooled_out[lane, s, 1].astype(F32)

    def child_at(child, start):
        at = jnp.clip(child - start * LANES * slots, 0, LANES * slots - 1)
        return jnp.where(child >= 0, at, LANES * slots)

    def halves(value, size):
        if size == 1:
            return value, 0
        return lax.div(value, size), lax.rem(value, size)

    @pl.loop(0, bricks)
    def _(j):
        lane, slot = halves(j, per)
        for o in range(8):
            at = child_at(meta_s[lane, slot, o], group)
            ox, oy, oz = o // 4 * half, o // 2 % 2 * half, o % 2 * half
            for x in range(half):
                for y in range(half):
                    row = (x * half + y) * half
                    coarse[j, ox + x, oy + y, oz : oz + half, :] = children[
                        at, row : row + half, :
                    ]

    def coarse_index(lane, slot, live):
        def index(t):
            value = meta_s[lane, per + slot, t]
            there = (value >= 0) & live
            if t // 9 == 1:
                return jnp.where(there, jnp.clip(value - group * bricks, 0, bricks - 1), bricks)
            at = jnp.clip(value - (group - 1) * bricks, 0, 3 * bricks - 1)
            return jnp.where(there, at, 3 * bricks)

        return index

    def keep_sides(source):
        for j in range(bricks):
            low_x[bricks + j] = source[j, 0]
            high_x[bricks + j] = source[j, edge - 1]

    own = bricks // 2
    parity = lax.rem(member, 2)

    def brick_of(i, odd):
        lane, slot = halves(i, per)
        return (2 * lane + odd) * per + slot

    def place_far(side):
        start = 2 * bricks * side
        for lane in range(LANES):
            for s in range(slots):
                far_children[side, lane * slots + s] = side_in[side, lane, s].astype(F32)
        far_children[side, LANES * slots] = jnp.zeros((cells, width), F32)

        @pl.loop(0, bricks)
        def _(j):
            lane, slot = halves(j, per)
            for o in range(8):
                at = child_at(meta_far_s[side, lane, slot, o], group - 1 + 2 * side)
                oy, oz = o // 2 % 2 * half, o % 2 * half
                target = high_x if o // 4 else low_x
                for y in range(half):
                    target[start + j, oy + y, oz : oz + half, :] = far_children[
                        side, at, y * half : (y + 1) * half, :
                    ]

    def group_index(j):
        return coarse_index(*halves(j, per), True)

    keep_sides(coarse)
    def all_faces(side):
        return remote(
            side_in.at[side],
            side_in.at[side],
            side_send_sem.at[0, side],
            side_recv_sem.at[0, side],
            me + (LANES if side == 0 else -LANES),
        )

    @pl.when(has_down)
    def _():
        all_faces(0).wait_recv()
        all_faces(1).wait_send()

    @pl.when(has_up)
    def _():
        all_faces(1).wait_recv()
        all_faces(0).wait_send()

    pl.when(has_down)(lambda: far_to_smem(0).wait())
    pl.when(has_up)(lambda: far_to_smem(1).wait())
    pl.when(has_down)(lambda: place_far(0))
    pl.when(has_up)(lambda: place_far(1))

    loaded(2)

    def own_index(i):
        return group_index(brick_of(i, parity))

    def brick_copy(i):
        return remote(brick_out.at[i], brick_in.at[i], pair_send_sem, pair_recv_sem, peer(1))

    def planes_to(side, i, k):
        return remote(
            side_out2.at[i],
            side_in2.at[side, parity, i],
            side_send_sem.at[1, side],
            side_recv_sem.at[1, side],
            peer(k) + (LANES if side == 0 else -LANES),
        )

    def all_planes(side):
        return remote(
            side_in2.at[side],
            side_in2.at[side],
            side_send_sem.at[1, side],
            side_recv_sem.at[1, side],
            me + (LANES if side == 0 else -LANES),
        )

    @pl.loop(0, own)
    def _(i):
        index = own_index(i)
        totals = local_product(coarse, index, w2)
        assemble(pad, edge, None, high_x, low_x, index, far_taps)
        for side in range(2):
            shift(zfar, side * padded, pad, side * (edge + 1), slice(None), edge + 2)
        for side in range(2):
            added = stepped(zfar, [side * padded], padded, w2[2 * side])
            at = side * (edge - 1)
            totals[at] = totals[at] + tread(added, 0, plane)
        value = jnp.maximum(jnp.concatenate(totals, axis=0), 0.0).astype(BF16)
        side_out2[i, 0] = value[0:plane]
        side_out2[i, 1] = value[(edge - 1) * plane :]
        brick_out[i] = value
        coarse2[brick_of(i, parity)] = value.astype(F32).reshape(cube)

        def send_planes(side):
            for k in range(2):
                planes_to(side, i, k).start()

        pl.when(has_up)(lambda: send_planes(0))
        pl.when(has_down)(lambda: send_planes(1))
        brick_copy(i).start()

    loaded(3)

    part = half * edge
    strip = slots * part
    tall = half + 2
    column = tall * edge

    def parent_of(s):
        parent = fine_parent[s]
        safe = jnp.maximum(parent, 0)
        lane, slot = halves(jnp.clip(safe // 8 - group * bricks, 0, bricks - 1), per)
        octant = safe % 8
        ox, oy = lax.div(octant, 4), lax.rem(lax.div(octant, 2), 2)
        return coarse_index(lane, slot, parent >= 0), ox, oy * half

    strips = 4
    span = width // strips

    @pl.loop(0, 3 * strips)
    def _(i):
        dz, strip_at = lax.div(i, strips), lax.rem(i, strips)
        rows = []
        for dy in range(3):
            start = pl.multiple_of((dy * 3 + dz) * width + strip_at * span, span)
            rows.append([w4[dx, pl.ds(start, span), :].astype(F32) for dx in range(3)])
        late = [r1 + r2 for r1, r2 in zip(rows[1], rows[2])]
        early = [r0 + r1 for r0, r1 in zip(rows[0], rows[1])]
        for py, parts in enumerate(((rows[0], late), (early, rows[2]))):
            for q, (a, b, c) in enumerate(parts):
                start = pl.multiple_of((q * 3 + dz) * width + strip_at * span, span)
                wup[py, pl.ds(start, span), :] = jnp.concatenate(
                    [b + c, a + b, a, c], axis=1
                ).astype(BF16)

    remote(brick_out, brick_in, pair_send_sem, pair_recv_sem, peer(1)).wait()
    for i in range(own):
        coarse2[brick_of(i, 1 - parity)] = brick_in[i].astype(F32).reshape(cube)
    keep_sides(coarse2)
    pad[0] = jnp.zeros(pad.shape[1:], F32)
    pad[edge + 1] = jnp.zeros(pad.shape[1:], F32)

    @pl.loop(0, slots)
    def _(s):
        index, ox, oy = parent_of(s)
        assemble(pad, edge, coarse2, None, None, index, own_taps)
        for x in range(tall):
            row = pl.multiple_of((s * tall + x) * column, edge)
            shift(zq, row, pad, ox * half + x, pl.ds(oy, tall), tall)

    def starts_of(planes):
        return [(s * tall + x) * column for x in planes for s in range(slots)]

    two = dot(columns(zq, starts_of(range(half + 1)), part), taps(w3, 0, 1))
    third = stepped(
        zq, [(s * tall + 2) * column for s in range(slots)], half * column, w3[2]
    )
    for x in range(half):
        for s in range(slots):
            at = x * strip + s * part
            dacc[at : at + part, :] = (
                two[at : at + part, 0:width]
                + two[at + strip : at + strip + part, width : 2 * width]
                + tread(third, (s * half + x) * column, part)
            )

    finish_pair(halo2[0], has_next, halo2[1], has_prev)
    take_faces(face_in2, below, above)

    def store_part(b, side, added):
        at = side * (edge - 1) * plane
        acc[b, at : at + plane] = acc[b, at : at + plane] + added

    outer_planes(slots, below, above, fine_index, w4, store_part)
    @pl.when(has_down)
    def _():
        all_planes(0).wait_recv()
        all_planes(1).wait_send()

    @pl.when(has_up)
    def _():
        all_planes(1).wait_recv()
        all_planes(0).wait_send()

    for side in range(2):
        for odd in range(2):
            for i in range(own):
                at = 2 * bricks * side + (2 * (i // per) + odd) * per + i % per
                low_x[at] = side_in2[side, odd, i, 0].astype(F32).reshape(face)
                high_x[at] = side_in2[side, odd, i, 1].astype(F32).reshape(face)


    @pl.loop(0, slots)
    def _(s):
        index, ox, oy = parent_of(s)
        assemble(pad, edge, None, high_x, low_x, index, far_taps)
        row = pl.multiple_of(s * column, edge)
        shift(zfar, row, pad, ox * (edge + 1), pl.ds(oy, tall), tall)

    far = dot(
        columns(zfar, [s * column for s in range(slots)], part),
        taps(w3, 0, 2),
    )
    picks[0] = far[:, 0:width]
    picks[1] = jnp.zeros((strip, width), F32)
    picks[2] = far[:, width : 2 * width]
    for s in range(slots):
        _, ox, _ = parent_of(s)
        rows = slice(s * part, (s + 1) * part)
        low = picks[ox, rows]
        high = picks[ox + 1, rows]
        pieces = [dacc[x * strip + s * part : x * strip + (s + 1) * part, :] for x in range(half)]
        pieces[0] = pieces[0] + low
        pieces[half - 1] = pieces[half - 1] + high
        piece = rounded(jnp.concatenate(pieces, axis=0))
        oz = lax.rem(jnp.maximum(fine_parent[s], 0), 2)
        spread[s, pl.ds(0, half * part, stride=2), :] = piece
        spread[s, pl.ds(1, half * part, stride=2), :] = piece
        for x in range(half):
            for y in range(half):
                start = ((x * half + y) * 2 + oz) * edge
                utab[s, x, y] = spread[s, pl.ds(start, edge), :]
        stage_faces(face_out3, utab, half - 1, s)
    start_pair(halo3[0], has_next, halo3[1], has_prev)

    brick_rows = tall * column

    @pl.loop(0, slots)
    def _(b):
        assemble(upad, half, utab, None, None, fine_index(b), own_taps)
        for x in range(half):
            row = pl.multiple_of(b * brick_rows + (x + 1) * column, edge)
            shift(zu, row, upad, x + 1, slice(None), tall)

    def woven(zero, one):
        pair = jnp.stack(
            [zero.reshape(half, edge, width), one.reshape(half, edge, width)], axis=1
        )
        return pair.reshape(plane, width)

    inner = [b * brick_rows + (x + 1) * column for b in range(slots) for x in range(half)]
    direct, across = [], []
    for py in range(2):
        lhs = columns(zu, inner, part, (py, py + 1))
        direct.append(dot(lhs, wup[py, :, 0 : 2 * width]))
        across.append(dot(columns(zu, inner, part, (py, py + 1)), wup[py, :, 2 * width :]))

    for b in range(slots):
        for x in range(edge):
            i, px = x // 2, x % 2
            lanes = slice(px * width, (px + 1) * width)
            other = i - 1 + 2 * px
            sums = []
            for py in range(2):
                at = (b * half + i) * part
                value = direct[py][at : at + part, lanes]
                if 0 <= other < half:
                    at = (b * half + other) * part
                    value = value + across[py][at : at + part, lanes]
                sums.append(value)
            rows = slice(x * plane, (x + 1) * plane)
            total = acc[b, rows] + woven(*sums)
            if 0 <= other < half:
                out_ref[b, rows, :] = jnp.maximum(total, 0.0).astype(BF16)
            else:
                acc[b, rows] = total

    finish_pair(halo3[0], has_next, halo3[1], has_prev)
    take_faces(face_in3, ubelow, uabove)

    @pl.loop(0, slots)
    def _(b):
        assemble(upad, half, None, ubelow, uabove, fine_index(b), far_taps)
        for x in (0, half + 1):
            row = pl.multiple_of(b * brick_rows + x * column, edge)
            shift(zu, row, upad, x, slice(None), tall)

    for side in range(2):
        starts = [b * brick_rows + side * (half + 1) * column for b in range(slots)]
        lanes = slice((2 + side) * width, (3 + side) * width)
        sums = [dot(columns(zu, starts, part, (py, py + 1)), wup[py, :, lanes]) for py in range(2)]
        for b in range(slots):
            at = side * (edge - 1) * plane
            rows = slice(b * part, (b + 1) * part)
            total = acc[b, at : at + plane] + woven(sums[0][rows], sums[1][rows])
            out_ref[b, at : at + plane, :] = jnp.maximum(total, 0.0).astype(BF16)


def per_device(
    n,
    features,
    fine_nbr,
    fine_send,
    fine_parent,
    coarse_child,
    coarse_nbr,
    enc_fine_w,
    enc_coarse_w,
    dec_coarse_w,
    dec_fine_w,
):
    slots, edge, width = features.shape[0], features.shape[1], features.shape[-1]
    per = coarse_nbr.shape[0]
    bricks = LANES * per
    half = edge // 2
    plane = edge * edge
    voxels = edge**3
    padded = (edge + 2) * edge
    tall = half + 2
    rows = -(-2 * per // 8) * 8
    kernels = [
        w.reshape(3, 9 * width, width)
        for w in (enc_fine_w, enc_coarse_w, dec_coarse_w, dec_fine_w)
    ]
    vmem = pltpu.VMEM
    vmem_spec = pl.BlockSpec(memory_space=pltpu.VMEM)
    any_spec = pl.BlockSpec(memory_space=pl.ANY)
    cube = (edge, edge, edge, width)
    face = (edge, edge, width)
    dma = pltpu.SemaphoreType.DMA
    out = pl.pallas_call(
        functools.partial(kernel, n),
        out_shape=pltpu.VMEM((slots, voxels, width), BF16),
        in_specs=[any_spec] * 10,
        out_specs=vmem_spec,
        scratch_shapes=[
            pltpu.SMEM(fine_nbr.shape, jnp.int32),
            pltpu.SMEM(fine_send.shape[1:], jnp.int32),
            pltpu.SMEM(fine_parent.shape, jnp.int32),
            vmem(coarse_child.shape, jnp.int32),
            vmem(coarse_nbr.shape, jnp.int32),
            vmem((slots, voxels, width), BF16),
            *[vmem((3, 9 * width, width), BF16)] * 4,
            vmem((2, 6 * width, 4 * width), BF16),
            vmem((edge + 2, edge + 2, 3 * edge, width), F32),
            vmem((half + 2, half + 2, 3 * edge, width), F32),
            vmem((3, edge * padded + edge, width), BF16),
            vmem((3, 2 * max(slots, bricks) * padded + edge, width), BF16),
            vmem((3, slots * tall * tall * edge + edge, width), BF16),
            vmem((3, slots * tall * tall * edge, width), BF16),
            vmem((max(slots, bricks), 2, plane, width), F32),
            vmem((slots, voxels, width), F32),
            vmem((half * slots * half * edge, width), F32),
            vmem((3, slots * half * edge, width), F32),
            vmem((slots + 1, half, half, edge, width), F32),
            vmem((slots + 1, half, edge, width), F32),
            vmem((slots + 1, half, edge, width), F32),
            vmem((slots + 1,) + cube, F32),
            vmem((slots + 1,) + cube, F32),
            vmem((slots + 1,) + face, F32),
            vmem((slots + 1,) + face, F32),
            vmem((2, slots, plane, width), BF16),
            vmem((2, slots, plane, width), BF16),
            vmem((2, slots, plane, width), BF16),
            vmem((2, slots, plane, width), BF16),
            vmem((2, slots, half * edge, width), BF16),
            vmem((2, slots, half * edge, width), BF16),
            vmem((half * half * edge, width), F32),
            vmem((LANES, slots, (half - 2) * half**2, width), BF16),
            vmem((LANES, slots, 2, half**2, width), BF16),
            vmem((slots, 2, half**2, width), BF16),
            vmem((LANES * slots + 1, half**3, width), F32),
            vmem((LANES, rows, 128), jnp.int32),
            pltpu.SMEM((LANES, rows, 128), jnp.int32),
            vmem((2, LANES, rows, 128), jnp.int32),
            pltpu.SMEM((2, LANES, rows, 128), jnp.int32),
            vmem((2, LANES * slots + 1, half**2, width), F32),
            vmem((bricks + 1,) + cube, F32),
            vmem((bricks + 1,) + cube, F32),
            vmem((3 * bricks + 1,) + face, F32),
            vmem((3 * bricks + 1,) + face, F32),
            vmem((slots, half**2, width), BF16),
            vmem((2, LANES, slots, half**2, width), BF16),
            vmem((bricks // 2, 2, plane, width), BF16),
            vmem((2, 2, bricks // 2, 2, plane, width), BF16),
            vmem((bricks // 2, voxels, width), BF16),
            vmem((bricks // 2, voxels, width), BF16),
            vmem((slots, half * half * 2 * edge, width), F32),
            dma((5,)),
            dma((5,)),
            dma((3, 2)),
            dma((3, 2)),
            dma((2,)),
            dma((2,)),
            dma(()),
            dma(()),
            dma((3, 2)),
            dma((3, 2)),
            dma(()),
            dma(()),
            pltpu.SemaphoreType.REGULAR,
            dma(()),
            dma((2,)),
        ],
        compiler_params=pltpu.CompilerParams(
            collective_id=0, has_side_effects=True, vmem_limit_bytes=60 * 1024 * 1024
        ),
    )(
        fine_nbr,
        fine_send[0],
        fine_parent,
        coarse_child,
        coarse_nbr,
        features.reshape(slots, voxels, width),
        *kernels,
    )
    return out.reshape(features.shape)


def solution(mesh):
    lead = ("groups", "gx")
    placed = (
        P(lead, None, None, None, None),
        P(lead, None),
        P(lead, None, None),
        P(lead),
        P(lead, None),
        P(lead, None),
        P(),
        P(),
        P(),
        P(),
    )
    return jax.shard_map(
        functools.partial(per_device, mesh.shape["gx"]),
        mesh=mesh,
        in_specs=placed,
        out_specs=P(lead, None, None, None, None),
        check_vma=False,
    )
```

```python
import functools

import jax
import jax.numpy as jnp
from jax import lax
from jax.experimental import pallas as pl
from jax.experimental.pallas import tpu as pltpu
from jax.sharding import PartitionSpec as P

F32 = jnp.float32
BF16 = jnp.bfloat16
LANES = 4
GROUP = 2
MESH = pl.DeviceIdType.MESH


def pick(offset, edge):
    if offset < 0:
        return slice(edge - 1, edge)
    if offset == 0:
        return slice(0, edge)
    return slice(0, 1)


def place(offset, edge, base):
    if offset < 0:
        return slice(base - 1, base)
    if offset == 0:
        return slice(base, base + edge)
    return slice(base + edge, base + edge + 1)


def kernel(
    n,
    fine_nbr_hbm,
    fine_send_hbm,
    fine_parent_hbm,
    child_hbm,
    nbr_hbm,
    feat_hbm,
    w1_hbm,
    w2_hbm,
    w3_hbm,
    w4_hbm,
    out_ref,
    fine_nbr,
    fine_send,
    fine_parent,
    child_ref,
    nbr_ref,
    feat,
    w1,
    w2,
    w3,
    w4,
    wup,
    pad,
    upad,
    zs,
    zfar,
    zq,
    zu,
    opened,
    acc,
    dacc,
    picks,
    utab,
    ubelow,
    uabove,
    table,
    enc,
    below,
    above,
    face_out,
    face_in,
    face_out2,
    face_in2,
    face_out3,
    face_in3,
    half_z,
    pooled,
    pooled_out,
    own_out,
    children,
    meta,
    meta_s,
    meta_far,
    meta_far_s,
    far_children,
    coarse,
    coarse2,
    ends,
    side_out,
    side_in,
    side_out2,
    side_in2,
    brick_out,
    brick_in,
    spread,
    load_sem,
    small_sem,
    face_send_sem,
    face_recv_sem,
    pool_send_sem,
    pool_recv_sem,
    meta_send_sem,
    meta_recv_sem,
    side_send_sem,
    side_recv_sem,
    pair_send_sem,
    pair_recv_sem,
    hand_send_sem,
    hand_recv_sem,
    ready_sem,
    meta_sem,
    far_sem,
):
    slots, edge = out_ref.shape[0], enc.shape[1]
    plane = edge * edge
    width = out_ref.shape[-1]
    half = edge // 2
    block = half**3
    per = child_ref.shape[0]
    bricks = LANES * per
    me = lax.axis_index("gx")
    member = lax.rem(me, LANES)
    group = lax.div(me, LANES)

    def peer(k):
        return me - member + (member ^ k)

    width = out_ref.shape[-1]
    loads = [[pltpu.make_async_copy(feat_hbm, feat, load_sem.at[0])]]
    for i, (src, dst) in enumerate(
        ((w1_hbm, w1), (w2_hbm, w2), (w3_hbm, w3), (w4_hbm, w4))
    ):
        loads.append([pltpu.make_async_copy(src, dst, load_sem.at[i + 1])])
    small = [
        pltpu.make_async_copy(src, dst, small_sem.at[i])
        for i, (src, dst) in enumerate(
            (
                (fine_nbr_hbm, fine_nbr),
                (fine_send_hbm, fine_send),
                (fine_parent_hbm, fine_parent),
                (child_hbm, child_ref),
                (nbr_hbm, nbr_ref),
            )
        )
    ]
    for copy in loads[0]:
        copy.start()
    for copy in small:
        copy.start()
    for copies in loads[1:]:
        for copy in copies:
            copy.start()

    def loaded(i):
        for copy in loads[i]:
            copy.wait()

    has_prev, has_next = me > 0, me < n - 1
    has_down, has_up = me >= LANES, me < n - LANES
    barrier = pltpu.get_barrier_semaphore()

    def greet(other):
        pl.semaphore_signal(barrier, inc=1, device_id={"gx": other}, device_id_type=MESH)

    for k in range(1, LANES):
        greet(peer(k))
    first = me - member
    sides = (
        (has_prev & (member == 0), me - 1),
        (has_next & (member == LANES - 1), me + 1),
        (has_down, me - LANES),
        (has_up, me + LANES),
    )
    peers = LANES - 1
    for there, other in sides:
        pl.when(there)(functools.partial(greet, other))
        peers = peers + jnp.where(there, 1, 0)

    def remote(src, dst, send, recv, other):
        return pltpu.make_async_remote_copy(
            src_ref=src,
            dst_ref=dst,
            send_sem=send,
            recv_sem=recv,
            device_id={"gx": other},
            device_id_type=MESH,
        )

    def face_copies(outgoing, incoming, phase):
        up = remote(
            outgoing.at[0],
            incoming.at[0],
            face_send_sem.at[phase, 0],
            face_recv_sem.at[phase, 0],
            me + 1,
        )
        down = remote(
            outgoing.at[1],
            incoming.at[1],
            face_send_sem.at[phase, 1],
            face_recv_sem.at[phase, 1],
            me - 1,
        )
        return up, down

    def start_pair(up, up_there, down, down_there):
        pl.when(up_there)(up.start)
        pl.when(down_there)(down.start)

    def finish_pair(up, up_there, down, down_there):
        @pl.when(down_there)
        def _():
            up.wait_recv()
            down.wait_send()

        @pl.when(up_there)
        def _():
            down.wait_recv()
            up.wait_send()


    cube = (edge, edge, edge, width)
    face = (edge, edge, width)
    base = edge
    high_x, low_x = ends.at[0], ends.at[1]
    padded = (edge + 2) * edge
    own_taps = range(9, 18)
    far_taps = (*range(9), *range(18, 27))
    zero_brick = jnp.zeros(cube, F32)
    zero_plane = jnp.zeros(face, F32)
    table[slots] = zero_brick
    enc[slots] = zero_brick

    def stage_faces(outgoing, source, last, s):
        up_from = jnp.where(fine_send[0, s] >= 0, s, slots)
        down_from = jnp.where(fine_send[1, s] >= 0, s, slots)
        rows = outgoing.shape[2]
        outgoing[0, s] = source[up_from, last].reshape(rows, width).astype(BF16)
        outgoing[1, s] = source[down_from, 0].reshape(rows, width).astype(BF16)

    loaded(0)
    for s in range(slots):
        table[s] = feat[s].astype(F32).reshape(cube)
    for copy in small:
        copy.wait()
    meta[member, 0:per, 0 : child_ref.shape[1]] = child_ref[...]
    meta[member, per : 2 * per, 0 : nbr_ref.shape[1]] = nbr_ref[...]
    for s in range(slots):
        stage_faces(face_out, table, edge - 1, s)
    halo1 = face_copies(face_out, face_in, 0)
    halo2 = face_copies(face_out2, face_in2, 1)
    halo3 = face_copies(face_out3, face_in3, 2)
    meta_copies = [
        remote(
            meta.at[member],
            meta.at[member],
            meta_send_sem,
            meta_recv_sem,
            peer(k),
        )
        for k in range(1, LANES)
    ]

    below[slots] = zero_plane
    above[slots] = zero_plane
    coarse[bricks] = zero_brick
    coarse2[bricks] = zero_brick
    low_x[3 * bricks] = zero_plane
    high_x[3 * bricks] = zero_plane
    children[LANES * slots] = jnp.zeros((block, width), F32)
    utab[slots] = jnp.zeros((half, half, edge, width), F32)
    ubelow[slots] = jnp.zeros((half, edge, width), F32)
    uabove[slots] = jnp.zeros((half, edge, width), F32)

    def assemble(target, side, centre, lower, upper, index, taps):
        for t in taps:
            dx, dy, dz = t // 9 - 1, t // 3 % 3 - 1, t % 3 - 1
            at = index(t)
            ys, zs = pick(dy, side), pick(dz, edge)
            if dx == 0:
                piece = centre[at, :, ys, zs, :]
            elif dx < 0:
                piece = lower[at, ys, zs, :][None]
            else:
                piece = upper[at, ys, zs, :][None]
            target[place(dx, side, 1), place(dy, side, 1), place(dz, edge, base), :] = piece

    def shift(store, row, source, x, y, count):
        rows = count * edge
        for dz in range(3):
            first = base + dz - 1
            piece = source[x, y, first : first + edge, :]
            store[dz, pl.ds(row, rows), :] = piece.reshape(rows, width).astype(BF16)

    def columns(store, starts, rows, offsets=(0, 1, 2)):
        return jnp.concatenate(
            [
                jnp.concatenate(
                    [store[dz, r + dy * edge : r + dy * edge + rows, :] for r in starts], axis=0
                )
                for dy in offsets
                for dz in range(3)
            ],
            axis=1,
        )

    def taps(weights, *sides):
        return jnp.concatenate([weights[dx] for dx in sides], axis=1)

    def dot(a, b):
        return jnp.dot(a, b, preferred_element_type=F32)

    def stepped(store, starts, rows, weight):
        third = 3 * width
        first, middle, last = (weight[i * third : (i + 1) * third, :] for i in range(3))
        both = jnp.concatenate(
            [
                jnp.concatenate([first, middle], axis=1),
                jnp.concatenate([jnp.zeros((third, width), BF16), last], axis=1),
            ],
            axis=0,
        )
        return dot(columns(store, starts, rows, (0, 1)), both)

    def tread(value, row, rows):
        return value[row : row + rows, 0:width] + value[row + edge : row + edge + rows, width:]

    def local_product(centre, indices, weights):
        rows = edge * padded
        for i, index in enumerate(indices):
            assemble(pad, edge, centre, None, None, index, own_taps)
            for x in range(edge):
                shift(zs, i * rows + x * padded, pad, x + 1, slice(None), edge + 2)
        count = len(indices)
        starts = [i * rows + x * padded for i in range(count) for x in range(edge)]
        two = dot(columns(zs, starts, plane), taps(weights, 0, 1))
        inner = [i * rows + padded for i in range(count)]
        third = stepped(zs, inner, (edge - 1) * padded, weights[2])
        results = []
        for i in range(count):
            totals = []
            for x in range(edge):
                at = (i * edge + x) * plane
                total = two[at : at + plane, width : 2 * width]
                if x > 0:
                    total = total + two[at - plane : at, 0:width]
                if x < edge - 1:
                    total = total + tread(third, (i * (edge - 1) + x) * padded, plane)
                totals.append(total)
            results.append(totals)
        return results

    def outer_planes(count, lower, upper, index_of, weights, store):
        @pl.loop(0, count)
        def _(j):
            assemble(pad, edge, None, lower, upper, index_of(j), far_taps)
            for side in range(2):
                row = pl.multiple_of((side * count + j) * padded, edge)
                shift(zfar, row, pad, side * (edge + 1), slice(None), edge + 2)

        for side in range(2):
            added = stepped(zfar, [side * count * padded], count * padded, weights[2 * side])
            for j in range(count):
                store(j, side, tread(added, j * padded, plane))

    def rounded(value):
        return jnp.maximum(value, 0.0).astype(BF16).astype(F32)

    def fine_index(b):
        def index(t):
            at = fine_nbr[b, t]
            return jnp.where(at >= 0, at, slots)

        return index

    def take_faces(incoming, low, high):
        shape = low.shape[1:]
        for s in range(slots):
            low[s] = incoming[0, s].astype(F32).reshape(shape)
            high[s] = incoming[1, s].astype(F32).reshape(shape)

    cells = half * half

    def pool_copy(k, b):
        source = pooled_out.at[member] if b is None else pooled.at[member, b]
        stage = int(b is None)
        return remote(
            source, source, pool_send_sem.at[stage], pool_recv_sem.at[stage], peer(k)
        )

    def all_pooled(stage):
        source = (pooled, pooled_out)[stage].at[0 : LANES - 1]
        return remote(
            source, source, pool_send_sem.at[stage], pool_recv_sem.at[stage], peer(1)
        )

    def pool(value, count):
        pairs = value.reshape(count, 2, half, 2, edge, width)
        summed = (pairs[:, 0, :, 0] + pairs[:, 0, :, 1]) + (pairs[:, 1, :, 0] + pairs[:, 1, :, 1])
        half_z[0 : count * half * edge, :] = summed.reshape(count * half * edge, width)
        even = half_z[pl.ds(0, count * cells, stride=2), :]
        odd = half_z[pl.ds(1, count * cells, stride=2), :]
        return ((even + odd) * 0.125).astype(BF16)

    def side_copies(outgoing, incoming, phase):
        up = remote(
            outgoing,
            incoming.at[0],
            side_send_sem.at[phase, 0],
            side_recv_sem.at[phase, 0],
            me + LANES,
        )
        down = remote(
            outgoing,
            incoming.at[1],
            side_send_sem.at[phase, 1],
            side_recv_sem.at[phase, 1],
            me - LANES,
        )
        return up, down

    pl.semaphore_wait(barrier, peers)
    for k in range(1, LANES):
        pl.semaphore_signal(ready_sem, inc=1, device_id={"gx": peer(k)}, device_id_type=MESH)
    for copy in meta_copies:
        copy.start()
    start_pair(halo1[0], has_next, halo1[1], has_prev)
    loaded(1)

    at_once = GROUP if slots % GROUP == 0 else 1

    def encode(h):
        bricks_of = [at_once * h + i for i in range(at_once)]
        results = local_product(table, [fine_index(b) for b in bricks_of], w1)
        for b, totals in zip(bricks_of, results):
            opened[b, 0] = totals[0]
            opened[b, 1] = totals[edge - 1]
            value = rounded(jnp.concatenate(totals[1 : edge - 1], axis=0))
            value = value.reshape((edge - 2,) + face)
            enc[b, 1 : edge - 1] = value
            pooled[member, b] = pool(value[1 : edge - 3], half - 2)
        for b in bricks_of:
            send_pooled(b)

    def send_pooled(b):
        for k in range(1, LANES):
            pool_copy(k, b).start()


    @pl.loop(0, slots // at_once)
    def _(h):
        encode(h)

    finish_pair(halo1[0], has_next, halo1[1], has_prev)
    take_faces(face_in, below, above)

    every_meta = meta.at[0 : LANES - 1]
    remote(every_meta, every_meta, meta_send_sem, meta_recv_sem, peer(1)).wait()
    to_smem = pltpu.make_async_copy(meta, meta_s, meta_sem)
    to_smem.start()
    hop_meta = side_copies(meta, meta_far, 2)
    start_pair(hop_meta[0], has_up, hop_meta[1], has_down)
    def store_enc(b, side, added):
        enc[b, side * (edge - 1)] = rounded(opened[b, side] + added).reshape(face)

    outer_planes(slots, below, above, fine_index, w1, store_enc)
    for b in range(slots):
        for side in range(2):
            start = side * (edge - 2)
            value = pool(enc[b, start : start + 2], 1)
            pooled_out[member, b, side] = value
            own_out[b, side] = value
    for k in range(1, LANES):
        pool_copy(k, None).start()
    for s in range(slots):
        octant = lax.rem(jnp.maximum(fine_parent[s], 0), 8)
        side_out[s] = own_out[s, lax.div(octant, 4)]

    parity = lax.rem(member, 2)

    def face_to(side, h):
        return remote(
            side_out,
            side_in.at[side, parity, lax.div(member, 2)],
            side_send_sem.at[0, side],
            side_recv_sem.at[0, side],
            first + (LANES if side == 0 else -LANES) + 2 * h + parity,
        )

    def faces_to(side):
        for h in range(LANES // 2):
            face_to(side, h).start()

    def all_faces(side):
        return remote(
            side_in.at[side, 0],
            side_in.at[side, 0],
            side_send_sem.at[0, side],
            side_recv_sem.at[0, side],
            me + (LANES if side == 0 else -LANES),
        )

    def hand_over(side):
        block_of = side_in.at[side, parity]
        return remote(block_of, block_of, hand_send_sem.at[side], hand_recv_sem.at[side], peer(1))

    pl.semaphore_wait(ready_sem, LANES - 1)
    pl.when(has_up)(lambda: faces_to(0))
    pl.when(has_down)(lambda: faces_to(1))
    for s in range(slots):
        stage_faces(face_out2, enc, edge - 1, s)

    loaded(4)

    def decode_part(b):
        (totals,) = local_product(enc, [fine_index(b)], w4)
        acc[b] = jnp.concatenate(totals, axis=0)

    def run_decode(first, last):
        @pl.loop(first, last)
        def _(b):
            decode_part(b)

    run_decode(0, slots)

    to_smem.wait()
    finish_pair(hop_meta[0], has_up, hop_meta[1], has_down)

    def far_to_smem(side):
        return pltpu.make_async_copy(meta_far.at[side], meta_far_s.at[side], far_sem.at[side])

    pl.when(has_down)(lambda: far_to_smem(0).start())
    pl.when(has_up)(lambda: far_to_smem(1).start())
    for stage in range(2):
        all_pooled(stage).wait()

    @pl.when(has_down)
    def _():
        all_faces(0).wait_recv()
        all_faces(1).wait_send()
        hand_over(0).start()

    @pl.when(has_up)
    def _():
        all_faces(1).wait_recv()
        all_faces(0).wait_send()
        hand_over(1).start()

    start_pair(halo2[0], has_next, halo2[1], has_prev)
    for lane in range(LANES):
        for s in range(slots):
            at = lane * slots + s
            children[at, cells : block - cells] = pooled[lane, s].astype(F32)
            children[at, 0:cells] = pooled_out[lane, s, 0].astype(F32)
            children[at, block - cells : block] = pooled_out[lane, s, 1].astype(F32)

    def child_at(child, start):
        at = jnp.clip(child - start * LANES * slots, 0, LANES * slots - 1)
        return jnp.where(child >= 0, at, LANES * slots)

    def halves(value, size):
        if size == 1:
            return value, 0
        return lax.div(value, size), lax.rem(value, size)

    @pl.loop(0, bricks)
    def _(j):
        lane, slot = halves(j, per)
        for o in range(8):
            at = child_at(meta_s[lane, slot, o], group)
            ox, oy, oz = o // 4 * half, o // 2 % 2 * half, o % 2 * half
            for x in range(half):
                for y in range(half):
                    row = (x * half + y) * half
                    coarse[j, ox + x, oy + y, oz : oz + half, :] = children[
                        at, row : row + half, :
                    ]

    def coarse_index(lane, slot, live):
        def index(t):
            value = meta_s[lane, per + slot, t]
            there = (value >= 0) & live
            if t // 9 == 1:
                return jnp.where(there, jnp.clip(value - group * bricks, 0, bricks - 1), bricks)
            at = jnp.clip(value - (group - 1) * bricks, 0, 3 * bricks - 1)
            return jnp.where(there, at, 3 * bricks)

        return index

    def keep_sides(source):
        for j in range(bricks):
            low_x[bricks + j] = source[j, 0]
            high_x[bricks + j] = source[j, edge - 1]

    own = bricks // 2
    def brick_of(i, odd):
        lane, slot = halves(i, per)
        return (2 * lane + odd) * per + slot

    def place_far(side):
        start = 2 * bricks * side
        for lane in range(LANES):
            for s in range(slots):
                far_children[side, lane * slots + s] = side_in[side, lane % 2, lane // 2, s].astype(F32)
        far_children[side, LANES * slots] = jnp.zeros((cells, width), F32)

        @pl.loop(0, bricks)
        def _(j):
            lane, slot = halves(j, per)
            for o in range(8):
                at = child_at(meta_far_s[side, lane, slot, o], group - 1 + 2 * side)
                oy, oz = o // 2 % 2 * half, o % 2 * half
                target = high_x if o // 4 else low_x
                for y in range(half):
                    target[start + j, oy + y, oz : oz + half, :] = far_children[
                        side, at, y * half : (y + 1) * half, :
                    ]

    def group_index(j):
        return coarse_index(*halves(j, per), True)

    keep_sides(coarse)
    def far_planes():
        pl.when(has_down)(lambda: hand_over(0).wait())
        pl.when(has_up)(lambda: hand_over(1).wait())
        pl.when(has_down)(lambda: far_to_smem(0).wait())
        pl.when(has_up)(lambda: far_to_smem(1).wait())
        pl.when(has_down)(lambda: place_far(0))
        pl.when(has_up)(lambda: place_far(1))


    loaded(2)

    def own_index(i):
        return group_index(brick_of(i, parity))

    def brick_copy(i):
        return remote(brick_out.at[i], brick_in.at[i], pair_send_sem, pair_recv_sem, peer(1))

    def planes_to(side, i, k):
        return remote(
            side_out2.at[i],
            side_in2.at[side, parity, i],
            side_send_sem.at[1, side],
            side_recv_sem.at[1, side],
            peer(k) + (LANES if side == 0 else -LANES),
        )

    def all_planes(side):
        return remote(
            side_in2.at[side],
            side_in2.at[side],
            side_send_sem.at[1, side],
            side_recv_sem.at[1, side],
            me + (LANES if side == 0 else -LANES),
        )

    @pl.loop(0, own)
    def _(i):
        index = own_index(i)
        (totals,) = local_product(coarse, [index], w2)
        opened[i, 0] = totals[0]
        opened[i, 1] = totals[edge - 1]
        value = jnp.maximum(jnp.concatenate(totals[1 : edge - 1], axis=0), 0.0).astype(BF16)
        brick_out[i, plane : (edge - 1) * plane] = value
        coarse2[brick_of(i, parity), 1 : edge - 1] = value.astype(F32).reshape(
            (edge - 2,) + face
        )
        pl.when(i == 0)(far_planes)
        assemble(pad, edge, None, high_x, low_x, index, far_taps)
        for side in range(2):
            shift(zfar, side * padded, pad, side * (edge + 1), slice(None), edge + 2)
        for side in range(2):
            added = stepped(zfar, [side * padded], padded, w2[2 * side])
            at = side * (edge - 1)
            value = jnp.maximum(opened[i, side] + tread(added, 0, plane), 0.0).astype(BF16)
            side_out2[i, side] = value
            brick_out[i, at * plane : (at + 1) * plane] = value
            coarse2[brick_of(i, parity), at] = value.astype(F32).reshape(face)

        def send_planes(side):
            for k in range(2):
                planes_to(side, i, k).start()

        pl.when(has_up)(lambda: send_planes(0))
        pl.when(has_down)(lambda: send_planes(1))
        brick_copy(i).start()

    loaded(3)

    part = half * edge
    strip = slots * part
    tall = half + 2
    column = tall * edge

    def parent_of(s):
        parent = fine_parent[s]
        safe = jnp.maximum(parent, 0)
        lane, slot = halves(jnp.clip(safe // 8 - group * bricks, 0, bricks - 1), per)
        octant = safe % 8
        ox, oy = lax.div(octant, 4), lax.rem(lax.div(octant, 2), 2)
        return lane, slot, ox, oy * half

    strips = 4
    span = width // strips

    @pl.loop(0, 3 * strips)
    def _(i):
        dz, strip_at = lax.div(i, strips), lax.rem(i, strips)
        rows = []
        for dy in range(3):
            start = pl.multiple_of((dy * 3 + dz) * width + strip_at * span, span)
            rows.append([w4[dx, pl.ds(start, span), :].astype(F32) for dx in range(3)])
        late = [r1 + r2 for r1, r2 in zip(rows[1], rows[2])]
        early = [r0 + r1 for r0, r1 in zip(rows[0], rows[1])]
        for py, parts in enumerate(((rows[0], late), (early, rows[2]))):
            for q, (a, b, c) in enumerate(parts):
                start = pl.multiple_of((q * 3 + dz) * width + strip_at * span, span)
                wup[py, pl.ds(start, span), :] = jnp.concatenate(
                    [b + c, a + b, a, c], axis=1
                ).astype(BF16)

    remote(brick_out, brick_in, pair_send_sem, pair_recv_sem, peer(1)).wait()
    for i in range(own):
        coarse2[brick_of(i, 1 - parity)] = brick_in[i].astype(F32).reshape(cube)
    keep_sides(coarse2)
    pad[0] = jnp.zeros(pad.shape[1:], F32)
    pad[edge + 1] = jnp.zeros(pad.shape[1:], F32)

    @pl.loop(0, slots)
    def _(s):
        lane, slot, ox, oy = parent_of(s)
        index = coarse_index(lane, slot, fine_parent[s] >= 0)
        assemble(pad, edge, coarse2, None, None, index, own_taps)
        for x in range(tall):
            row = pl.multiple_of((s * tall + x) * column, edge)
            shift(zq, row, pad, ox * half + x, pl.ds(oy, tall), tall)

    def starts_of(planes):
        return [(s * tall + x) * column for x in planes for s in range(slots)]

    two = dot(columns(zq, starts_of(range(half + 1)), part), taps(w3, 0, 1))
    third = stepped(
        zq, [(s * tall + 2) * column for s in range(slots)], half * column, w3[2]
    )
    for x in range(half):
        for s in range(slots):
            at = x * strip + s * part
            dacc[at : at + part, :] = (
                two[at : at + part, 0:width]
                + two[at + strip : at + strip + part, width : 2 * width]
                + tread(third, (s * half + x) * column, part)
            )

    def lift(s, x, value):
        piece = rounded(value)
        oz = lax.rem(jnp.maximum(fine_parent[s], 0), 2)
        start = x * 2 * part
        spread[s, pl.ds(start, part, stride=2), :] = piece
        spread[s, pl.ds(start + 1, part, stride=2), :] = piece
        for y in range(half):
            utab[s, x, y] = spread[s, pl.ds(start + (2 * y + oz) * edge, edge), :]

    for s in range(slots):
        for x in range(1, half - 1):
            lift(s, x, dacc[x * strip + s * part : x * strip + (s + 1) * part, :])
    @pl.when(has_down)
    def _():
        all_planes(0).wait_recv()
        all_planes(1).wait_send()

    @pl.when(has_up)
    def _():
        all_planes(1).wait_recv()
        all_planes(0).wait_send()

    for side in range(2):
        for odd in range(2):
            for i in range(own):
                at = 2 * bricks * side + (2 * (i // per) + odd) * per + i % per
                low_x[at] = side_in2[side, odd, i, 0].astype(F32).reshape(face)
                high_x[at] = side_in2[side, odd, i, 1].astype(F32).reshape(face)


    @pl.loop(0, slots)
    def _(s):
        lane, slot, ox, oy = parent_of(s)
        live = fine_parent[s] >= 0
        for k in range(9):
            value = meta_s[lane, per + slot, ox * 18 + k]
            at = jnp.clip(value - (group - 1) * bricks, 0, 3 * bricks - 1)
            at = jnp.where((value >= 0) & live, at, 3 * bricks)
            dy, dz = k // 3 - 1, k % 3 - 1
            piece = ends[ox, at, pick(dy, edge), pick(dz, edge), :]
            pad[0, place(dy, edge, 1), place(dz, edge, base), :] = piece
        row = pl.multiple_of(s * column, edge)
        shift(zfar, row, pad, 0, pl.ds(oy, tall), tall)

    far = dot(
        columns(zfar, [s * column for s in range(slots)], part),
        taps(w3, 0, 2),
    )
    picks[0] = far[:, 0:width]
    picks[1] = jnp.zeros((strip, width), F32)
    picks[2] = far[:, width : 2 * width]
    for s in range(slots):
        ox = parent_of(s)[2]
        rows = slice(s * part, (s + 1) * part)
        lift(s, 0, dacc[rows, :] + picks[ox, rows])
        last = (half - 1) * strip + s * part
        lift(s, half - 1, dacc[last : last + part, :] + picks[ox + 1, rows])
        stage_faces(face_out3, utab, half - 1, s)
    start_pair(halo3[0], has_next, halo3[1], has_prev)

    brick_rows = tall * column

    @pl.loop(0, slots)
    def _(b):
        assemble(upad, half, utab, None, None, fine_index(b), own_taps)
        for x in range(half):
            row = pl.multiple_of(b * brick_rows + (x + 1) * column, edge)
            shift(zu, row, upad, x + 1, slice(None), tall)

    def woven(zero, one):
        pair = jnp.stack(
            [zero.reshape(half, edge, width), one.reshape(half, edge, width)], axis=1
        )
        return pair.reshape(plane, width)

    inner = [b * brick_rows + (x + 1) * column for b in range(slots) for x in range(half)]
    direct, across = [], []
    for py in range(2):
        lhs = columns(zu, inner, part, (py, py + 1))
        direct.append(dot(lhs, wup[py, :, 0 : 2 * width]))
        across.append(dot(columns(zu, inner, part, (py, py + 1)), wup[py, :, 2 * width :]))

    for b in range(slots):
        for x in range(edge):
            i, px = x // 2, x % 2
            lanes = slice(px * width, (px + 1) * width)
            other = i - 1 + 2 * px
            sums = []
            for py in range(2):
                at = (b * half + i) * part
                value = direct[py][at : at + part, lanes]
                if 0 <= other < half:
                    at = (b * half + other) * part
                    value = value + across[py][at : at + part, lanes]
                sums.append(value)
            rows = slice(x * plane, (x + 1) * plane)
            total = acc[b, rows] + woven(*sums)
            if 0 <= other < half:
                out_ref[b, rows, :] = jnp.maximum(total, 0.0).astype(BF16)
            else:
                acc[b, rows] = total

    finish_pair(halo2[0], has_next, halo2[1], has_prev)
    take_faces(face_in2, below, above)

    def store_part(b, side, added):
        at = side * (edge - 1) * plane
        acc[b, at : at + plane] = acc[b, at : at + plane] + added

    outer_planes(slots, below, above, fine_index, w4, store_part)
    finish_pair(halo3[0], has_next, halo3[1], has_prev)
    take_faces(face_in3, ubelow, uabove)

    @pl.loop(0, slots)
    def _(b):
        assemble(upad, half, None, ubelow, uabove, fine_index(b), far_taps)
        for x in (0, half + 1):
            row = pl.multiple_of(b * brick_rows + x * column, edge)
            shift(zu, row, upad, x, slice(None), tall)

    for side in range(2):
        starts = [b * brick_rows + side * (half + 1) * column for b in range(slots)]
        lanes = slice((2 + side) * width, (3 + side) * width)
        sums = [dot(columns(zu, starts, part, (py, py + 1)), wup[py, :, lanes]) for py in range(2)]
        for b in range(slots):
            at = side * (edge - 1) * plane
            rows = slice(b * part, (b + 1) * part)
            total = acc[b, at : at + plane] + woven(sums[0][rows], sums[1][rows])
            out_ref[b, at : at + plane, :] = jnp.maximum(total, 0.0).astype(BF16)


def per_device(
    n,
    features,
    fine_nbr,
    fine_send,
    fine_parent,
    coarse_child,
    coarse_nbr,
    enc_fine_w,
    enc_coarse_w,
    dec_coarse_w,
    dec_fine_w,
):
    slots, edge, width = features.shape[0], features.shape[1], features.shape[-1]
    per = coarse_nbr.shape[0]
    bricks = LANES * per
    half = edge // 2
    plane = edge * edge
    voxels = edge**3
    padded = (edge + 2) * edge
    tall = half + 2
    rows = -(-2 * per // 8) * 8
    kernels = [
        w.reshape(3, 9 * width, width)
        for w in (enc_fine_w, enc_coarse_w, dec_coarse_w, dec_fine_w)
    ]
    vmem = pltpu.VMEM
    vmem_spec = pl.BlockSpec(memory_space=pltpu.VMEM)
    any_spec = pl.BlockSpec(memory_space=pl.ANY)
    cube = (edge, edge, edge, width)
    face = (edge, edge, width)
    dma = pltpu.SemaphoreType.DMA
    out = pl.pallas_call(
        functools.partial(kernel, n),
        out_shape=pltpu.VMEM((slots, voxels, width), BF16),
        in_specs=[any_spec] * 10,
        out_specs=vmem_spec,
        scratch_shapes=[
            pltpu.SMEM(fine_nbr.shape, jnp.int32),
            pltpu.SMEM(fine_send.shape[1:], jnp.int32),
            pltpu.SMEM(fine_parent.shape, jnp.int32),
            vmem(coarse_child.shape, jnp.int32),
            vmem(coarse_nbr.shape, jnp.int32),
            vmem((slots, voxels, width), BF16),
            *[vmem((3, 9 * width, width), BF16)] * 4,
            vmem((2, 6 * width, 4 * width), BF16),
            vmem((edge + 2, edge + 2, 3 * edge, width), F32),
            vmem((half + 2, half + 2, 3 * edge, width), F32),
            vmem((3, GROUP * edge * padded + edge, width), BF16),
            vmem((3, 2 * max(slots, bricks) * padded + edge, width), BF16),
            vmem((3, slots * tall * tall * edge + edge, width), BF16),
            vmem((3, slots * tall * tall * edge, width), BF16),
            vmem((max(slots, bricks), 2, plane, width), F32),
            vmem((slots, voxels, width), F32),
            vmem((half * slots * half * edge, width), F32),
            vmem((3, slots * half * edge, width), F32),
            vmem((slots + 1, half, half, edge, width), F32),
            vmem((slots + 1, half, edge, width), F32),
            vmem((slots + 1, half, edge, width), F32),
            vmem((slots + 1,) + cube, F32),
            vmem((slots + 1,) + cube, F32),
            vmem((slots + 1,) + face, F32),
            vmem((slots + 1,) + face, F32),
            vmem((2, slots, plane, width), BF16),
            vmem((2, slots, plane, width), BF16),
            vmem((2, slots, plane, width), BF16),
            vmem((2, slots, plane, width), BF16),
            vmem((2, slots, half * edge, width), BF16),
            vmem((2, slots, half * edge, width), BF16),
            vmem((half * half * edge, width), F32),
            vmem((LANES, slots, (half - 2) * half**2, width), BF16),
            vmem((LANES, slots, 2, half**2, width), BF16),
            vmem((slots, 2, half**2, width), BF16),
            vmem((LANES * slots + 1, half**3, width), F32),
            vmem((LANES, rows, 128), jnp.int32),
            pltpu.SMEM((LANES, rows, 128), jnp.int32),
            vmem((2, LANES, rows, 128), jnp.int32),
            pltpu.SMEM((2, LANES, rows, 128), jnp.int32),
            vmem((2, LANES * slots + 1, half**2, width), F32),
            vmem((bricks + 1,) + cube, F32),
            vmem((bricks + 1,) + cube, F32),
            vmem((2, 3 * bricks + 1) + face, F32),
            vmem((slots, half**2, width), BF16),
            vmem((2, 2, LANES // 2, slots, half**2, width), BF16),
            vmem((bricks // 2, 2, plane, width), BF16),
            vmem((2, 2, bricks // 2, 2, plane, width), BF16),
            vmem((bricks // 2, voxels, width), BF16),
            vmem((bricks // 2, voxels, width), BF16),
            vmem((slots, half * half * 2 * edge, width), F32),
            dma((5,)),
            dma((5,)),
            dma((3, 2)),
            dma((3, 2)),
            dma((2,)),
            dma((2,)),
            dma(()),
            dma(()),
            dma((3, 2)),
            dma((3, 2)),
            dma(()),
            dma(()),
            dma((2,)),
            dma((2,)),
            pltpu.SemaphoreType.REGULAR,
            dma(()),
            dma((2,)),
        ],
        compiler_params=pltpu.CompilerParams(
            collective_id=0, has_side_effects=True, vmem_limit_bytes=60 * 1024 * 1024
        ),
    )(
        fine_nbr,
        fine_send[0],
        fine_parent,
        coarse_child,
        coarse_nbr,
        features.reshape(slots, voxels, width),
        *kernels,
    )
    return out.reshape(features.shape)


def solution(mesh):
    lead = ("groups", "gx")
    placed = (
        P(lead, None, None, None, None),
        P(lead, None),
        P(lead, None, None),
        P(lead),
        P(lead, None),
        P(lead, None),
        P(),
        P(),
        P(),
        P(),
    )
    return jax.shard_map(
        functools.partial(per_device, mesh.shape["gx"]),
        mesh=mesh,
        in_specs=placed,
        out_specs=P(lead, None, None, None, None),
        check_vma=False,
    )
```

```python
import functools

import jax
import jax.numpy as jnp
from jax import lax
from jax.experimental import pallas as pl
from jax.experimental.pallas import tpu as pltpu
from jax.sharding import PartitionSpec as P

F32 = jnp.float32
BF16 = jnp.bfloat16
LANES = 4
GROUP = 2
MESH = pl.DeviceIdType.MESH


def pick(offset, edge):
    if offset < 0:
        return slice(edge - 1, edge)
    if offset == 0:
        return slice(0, edge)
    return slice(0, 1)


def place(offset, edge, base):
    if offset < 0:
        return slice(base - 1, base)
    if offset == 0:
        return slice(base, base + edge)
    return slice(base + edge, base + edge + 1)


def kernel(
    n,
    fine_nbr_hbm,
    fine_send_hbm,
    fine_parent_hbm,
    child_hbm,
    nbr_hbm,
    feat_hbm,
    w1_hbm,
    w2_hbm,
    w3_hbm,
    w4_hbm,
    out_ref,
    fine_nbr,
    fine_send,
    fine_parent,
    child_ref,
    nbr_ref,
    feat,
    w1,
    w2,
    w3,
    w4,
    wup,
    pad,
    upad,
    zs,
    zfar,
    zq,
    zu,
    opened,
    acc,
    dacc,
    picks,
    utab,
    ubelow,
    uabove,
    table,
    enc,
    below,
    above,
    face_out,
    face_in,
    face_out2,
    face_in2,
    face_out3,
    face_in3,
    half_z,
    pooled,
    pooled_out,
    own_out,
    children,
    meta,
    meta_s,
    meta_far,
    meta_far_s,
    far_children,
    coarse,
    coarse2,
    ends,
    side_out,
    side_in,
    side_out2,
    side_in2,
    brick_out,
    brick_in,
    spread,
    load_sem,
    small_sem,
    face_send_sem,
    face_recv_sem,
    pool_send_sem,
    pool_recv_sem,
    meta_send_sem,
    meta_recv_sem,
    side_send_sem,
    side_recv_sem,
    pair_send_sem,
    pair_recv_sem,
    hand_send_sem,
    hand_recv_sem,
    ready_sem,
):
    slots, edge = out_ref.shape[0], enc.shape[1]
    plane = edge * edge
    width = out_ref.shape[-1]
    half = edge // 2
    block = half**3
    per = child_ref.shape[0]
    bricks = LANES * per
    me = lax.axis_index("gx")
    member = lax.rem(me, LANES)
    group = lax.div(me, LANES)

    def peer(k):
        return me - member + (member ^ k)

    width = out_ref.shape[-1]
    loads = [[pltpu.make_async_copy(feat_hbm, feat, load_sem.at[0])]]
    for i, (src, dst) in enumerate(
        ((w1_hbm, w1), (w2_hbm, w2), (w3_hbm, w3), (w4_hbm, w4))
    ):
        loads.append([pltpu.make_async_copy(src, dst, load_sem.at[i + 1])])
    small = [
        pltpu.make_async_copy(src, dst, small_sem.at[i])
        for i, (src, dst) in enumerate(
            (
                (fine_nbr_hbm, fine_nbr),
                (fine_send_hbm, fine_send),
                (fine_parent_hbm, fine_parent),
                (child_hbm, child_ref),
                (nbr_hbm, nbr_ref),
            )
        )
    ]
    for copy in loads[0]:
        copy.start()
    for copy in small:
        copy.start()
    for copies in loads[1:]:
        for copy in copies:
            copy.start()

    def loaded(i):
        for copy in loads[i]:
            copy.wait()

    has_prev, has_next = me > 0, me < n - 1
    has_down, has_up = me >= LANES, me < n - LANES
    barrier = pltpu.get_barrier_semaphore()

    def greet(other):
        pl.semaphore_signal(barrier, inc=1, device_id={"gx": other}, device_id_type=MESH)

    for k in range(1, LANES):
        greet(peer(k))
    first = me - member
    sides = (
        (has_prev & (member == 0), me - 1),
        (has_next & (member == LANES - 1), me + 1),
        (has_down, me - LANES),
        (has_up, me + LANES),
    )
    peers = LANES - 1
    for there, other in sides:
        pl.when(there)(functools.partial(greet, other))
        peers = peers + jnp.where(there, 1, 0)

    def remote(src, dst, send, recv, other):
        return pltpu.make_async_remote_copy(
            src_ref=src,
            dst_ref=dst,
            send_sem=send,
            recv_sem=recv,
            device_id={"gx": other},
            device_id_type=MESH,
        )

    def face_copies(outgoing, incoming, phase):
        up = remote(
            outgoing.at[0],
            incoming.at[0],
            face_send_sem.at[0],
            face_recv_sem.at[phase, 0],
            me + 1,
        )
        down = remote(
            outgoing.at[1],
            incoming.at[1],
            face_send_sem.at[1],
            face_recv_sem.at[phase, 1],
            me - 1,
        )
        return up, down

    def start_pair(up, up_there, down, down_there):
        pl.when(up_there)(up.start)
        pl.when(down_there)(down.start)

    def finish_pair(up, up_there, down, down_there):
        @pl.when(down_there)
        def _():
            up.wait_recv()
            down.wait_send()

        @pl.when(up_there)
        def _():
            down.wait_recv()
            up.wait_send()


    cube = (edge, edge, edge, width)
    face = (edge, edge, width)
    base = edge
    high_x, low_x = ends.at[0], ends.at[1]
    padded = (edge + 2) * edge
    own_taps = range(9, 18)
    far_taps = (*range(9), *range(18, 27))
    zero_brick = jnp.zeros(cube, F32)
    zero_plane = jnp.zeros(face, F32)
    table[slots] = zero_brick
    enc[slots] = zero_brick

    def stage_faces(outgoing, source, last, s):
        up_from = jnp.where(fine_send[0, s] >= 0, s, slots)
        down_from = jnp.where(fine_send[1, s] >= 0, s, slots)
        rows = outgoing.shape[2]
        outgoing[0, s] = source[up_from, last].reshape(rows, width).astype(BF16)
        outgoing[1, s] = source[down_from, 0].reshape(rows, width).astype(BF16)

    loaded(0)
    for s in range(slots):
        table[s] = feat[s].astype(F32).reshape(cube)
    for copy in small:
        copy.wait()
    meta[member, 0:per, 0 : child_ref.shape[1]] = child_ref[...]
    meta[member, per : 2 * per, 0 : nbr_ref.shape[1]] = nbr_ref[...]
    for s in range(slots):
        stage_faces(face_out, table, edge - 1, s)
    halo1 = face_copies(face_out, face_in, 0)
    halo2 = face_copies(face_out2, face_in2, 1)
    halo3 = face_copies(face_out3, face_in3, 2)
    meta_copies = [
        remote(
            meta.at[member],
            meta.at[member],
            meta_send_sem,
            meta_recv_sem,
            peer(k),
        )
        for k in range(1, LANES)
    ]

    below[slots] = zero_plane
    above[slots] = zero_plane
    coarse[bricks] = zero_brick
    coarse2[bricks] = zero_brick
    low_x[3 * bricks] = zero_plane
    high_x[3 * bricks] = zero_plane
    children[LANES * slots] = jnp.zeros((block, width), F32)
    utab[slots] = jnp.zeros((half, half, edge, width), F32)
    ubelow[slots] = jnp.zeros((half, edge, width), F32)
    uabove[slots] = jnp.zeros((half, edge, width), F32)

    def assemble(target, side, centre, lower, upper, index, taps):
        for t in taps:
            dx, dy, dz = t // 9 - 1, t // 3 % 3 - 1, t % 3 - 1
            at = index(t)
            ys, zs = pick(dy, side), pick(dz, edge)
            if dx == 0:
                piece = centre[at, :, ys, zs, :]
            elif dx < 0:
                piece = lower[at, ys, zs, :][None]
            else:
                piece = upper[at, ys, zs, :][None]
            target[place(dx, side, 1), place(dy, side, 1), place(dz, edge, base), :] = piece

    def shift(store, row, source, x, y, count):
        rows = count * edge
        for dz in range(3):
            first = base + dz - 1
            piece = source[x, y, first : first + edge, :]
            store[dz, pl.ds(row, rows), :] = piece.reshape(rows, width).astype(BF16)

    def columns(store, starts, rows, offsets=(0, 1, 2)):
        return jnp.concatenate(
            [
                jnp.concatenate(
                    [store[dz, r + dy * edge : r + dy * edge + rows, :] for r in starts], axis=0
                )
                for dy in offsets
                for dz in range(3)
            ],
            axis=1,
        )

    def taps(weights, *sides):
        return jnp.concatenate([weights[dx] for dx in sides], axis=1)

    def dot(a, b):
        return jnp.dot(a, b, preferred_element_type=F32)

    def stepped(store, starts, rows, weight):
        third = 3 * width
        first, middle, last = (weight[i * third : (i + 1) * third, :] for i in range(3))
        both = jnp.concatenate(
            [
                jnp.concatenate([first, middle], axis=1),
                jnp.concatenate([jnp.zeros((third, width), BF16), last], axis=1),
            ],
            axis=0,
        )
        return dot(columns(store, starts, rows, (0, 1)), both)

    def tread(value, row, rows):
        return value[row : row + rows, 0:width] + value[row + edge : row + edge + rows, width:]

    def local_product(centre, indices, weights):
        rows = edge * padded
        for i, index in enumerate(indices):
            assemble(pad, edge, centre, None, None, index, own_taps)
            for x in range(edge):
                shift(zs, i * rows + x * padded, pad, x + 1, slice(None), edge + 2)
        count = len(indices)
        starts = [i * rows + x * padded for i in range(count) for x in range(edge)]
        two = dot(columns(zs, starts, plane), taps(weights, 0, 1))
        inner = [i * rows + padded for i in range(count)]
        third = stepped(zs, inner, (edge - 1) * padded, weights[2])
        results = []
        for i in range(count):
            totals = []
            for x in range(edge):
                at = (i * edge + x) * plane
                total = two[at : at + plane, width : 2 * width]
                if x > 0:
                    total = total + two[at - plane : at, 0:width]
                if x < edge - 1:
                    total = total + tread(third, (i * (edge - 1) + x) * padded, plane)
                totals.append(total)
            results.append(totals)
        return results

    def outer_planes(count, lower, upper, index_of, weights, store):
        @pl.loop(0, count)
        def _(j):
            assemble(pad, edge, None, lower, upper, index_of(j), far_taps)
            for side in range(2):
                row = pl.multiple_of((side * count + j) * padded, edge)
                shift(zfar, row, pad, side * (edge + 1), slice(None), edge + 2)

        for side in range(2):
            added = stepped(zfar, [side * count * padded], count * padded, weights[2 * side])
            for j in range(count):
                store(j, side, tread(added, j * padded, plane))

    def rounded(value):
        return jnp.maximum(value, 0.0).astype(BF16).astype(F32)

    def fine_index(b):
        def index(t):
            at = fine_nbr[b, t]
            return jnp.where(at >= 0, at, slots)

        return index

    def take_faces(incoming, low, high):
        shape = low.shape[1:]
        for s in range(slots):
            low[s] = incoming[0, s].astype(F32).reshape(shape)
            high[s] = incoming[1, s].astype(F32).reshape(shape)

    cells = half * half

    def pool_copy(k, b):
        source = pooled_out.at[member] if b is None else pooled.at[member, b]
        stage = 1 if b is None else 2 * (k - 1)
        return remote(
            source, source, pool_send_sem.at[stage], pool_recv_sem.at[stage], peer(k)
        )

    def all_pooled(stage):
        source = (pooled.at[0:2], pooled_out.at[0 : LANES - 1], pooled.at[0])[stage]
        return remote(
            source, source, pool_send_sem.at[stage], pool_recv_sem.at[stage], peer(1)
        )

    def pass_pooled():
        source = pooled.at[member ^ 2]
        return remote(source, source, pool_send_sem.at[0], pool_recv_sem.at[0], peer(1))

    def pool(value, count):
        pairs = value.reshape(count, 2, half, 2, edge, width)
        summed = (pairs[:, 0, :, 0] + pairs[:, 0, :, 1]) + (pairs[:, 1, :, 0] + pairs[:, 1, :, 1])
        half_z[0 : count * half * edge, :] = summed.reshape(count * half * edge, width)
        even = half_z[pl.ds(0, count * cells, stride=2), :]
        odd = half_z[pl.ds(1, count * cells, stride=2), :]
        return ((even + odd) * 0.125).astype(BF16)

    def side_copies(outgoing, incoming, phase):
        up = remote(
            outgoing,
            incoming.at[0],
            side_send_sem.at[min(phase, 1), 0],
            side_recv_sem.at[phase, 0],
            me + LANES,
        )
        down = remote(
            outgoing,
            incoming.at[1],
            side_send_sem.at[min(phase, 1), 1],
            side_recv_sem.at[phase, 1],
            me - LANES,
        )
        return up, down

    pl.semaphore_wait(barrier, peers)
    for k in range(1, LANES):
        pl.semaphore_signal(ready_sem, inc=1, device_id={"gx": peer(k)}, device_id_type=MESH)
    for copy in meta_copies:
        copy.start()
    start_pair(halo1[0], has_next, halo1[1], has_prev)
    loaded(1)

    at_once = GROUP if slots % GROUP == 0 else 1

    def encode(h):
        bricks_of = [at_once * h + i for i in range(at_once)]
        results = local_product(table, [fine_index(b) for b in bricks_of], w1)
        for b, totals in zip(bricks_of, results):
            opened[b, 0] = totals[0]
            opened[b, 1] = totals[edge - 1]
            value = rounded(jnp.concatenate(totals[1 : edge - 1], axis=0))
            value = value.reshape((edge - 2,) + face)
            enc[b, 1 : edge - 1] = value
            pooled[member, b] = pool(value[1 : edge - 3], half - 2)
        for b in bricks_of:
            send_pooled(b)

    def send_pooled(b):
        for k in (2, 1):
            pool_copy(k, b).start()


    @pl.loop(0, slots // at_once)
    def _(h):
        encode(h)

    finish_pair(halo1[0], has_next, halo1[1], has_prev)
    take_faces(face_in, below, above)

    every_meta = meta.at[0 : LANES - 1]
    remote(every_meta, every_meta, meta_send_sem, meta_recv_sem, peer(1)).wait()
    to_smem = pltpu.make_async_copy(meta, meta_s, small_sem.at[0])
    to_smem.start()
    hop_meta = side_copies(meta, meta_far, 2)
    start_pair(hop_meta[0], has_up, hop_meta[1], has_down)
    def store_enc(b, side, added):
        enc[b, side * (edge - 1)] = rounded(opened[b, side] + added).reshape(face)

    outer_planes(slots, below, above, fine_index, w1, store_enc)
    for b in range(slots):
        for side in range(2):
            start = side * (edge - 2)
            value = pool(enc[b, start : start + 2], 1)
            pooled_out[member, b, side] = value
            own_out[b, side] = value
    for k in range(1, LANES):
        pool_copy(k, None).start()
    for s in range(slots):
        octant = lax.rem(jnp.maximum(fine_parent[s], 0), 8)
        side_out[s] = own_out[s, lax.div(octant, 4)]

    parity = lax.rem(member, 2)

    def face_to(side, h):
        return remote(
            side_out,
            side_in.at[side, parity, lax.div(member, 2)],
            side_send_sem.at[0, side],
            side_recv_sem.at[0, side],
            first + (LANES if side == 0 else -LANES) + 2 * h + parity,
        )

    def faces_to(side):
        for h in range(LANES // 2):
            face_to(side, h).start()

    def all_faces(side):
        return remote(
            side_in.at[side, 0],
            side_in.at[side, 0],
            side_send_sem.at[0, side],
            side_recv_sem.at[0, side],
            me + (LANES if side == 0 else -LANES),
        )

    def hand_over(side):
        block_of = side_in.at[side, parity]
        return remote(block_of, block_of, hand_send_sem.at[side], hand_recv_sem.at[side], peer(1))

    pl.semaphore_wait(ready_sem, LANES - 1)
    pl.when(has_up)(lambda: faces_to(0))
    pl.when(has_down)(lambda: faces_to(1))
    for s in range(slots):
        stage_faces(face_out2, enc, edge - 1, s)

    loaded(4)

    def decode_part(b):
        (totals,) = local_product(enc, [fine_index(b)], w4)
        acc[b] = jnp.concatenate(totals, axis=0)

    def run_decode(first, last):
        @pl.loop(first, last)
        def _(b):
            decode_part(b)

            @pl.when(b == max(slots - 2, 0))
            def _():
                all_pooled(2).wait_recv()
                pass_pooled().start()

    run_decode(0, slots)

    to_smem.wait()
    finish_pair(hop_meta[0], has_up, hop_meta[1], has_down)

    def far_to_smem(side):
        return pltpu.make_async_copy(meta_far.at[side], meta_far_s.at[side], small_sem.at[1 + side])

    pl.when(has_down)(lambda: far_to_smem(0).start())
    pl.when(has_up)(lambda: far_to_smem(1).start())
    for stage in range(2):
        all_pooled(stage).wait()
    all_pooled(2).wait_send()

    @pl.when(has_down)
    def _():
        all_faces(0).wait_recv()
        all_faces(1).wait_send()
        hand_over(0).start()

    @pl.when(has_up)
    def _():
        all_faces(1).wait_recv()
        all_faces(0).wait_send()
        hand_over(1).start()

    start_pair(halo2[0], has_next, halo2[1], has_prev)
    for lane in range(LANES):
        for s in range(slots):
            at = lane * slots + s
            children[at, cells : block - cells] = pooled[lane, s].astype(F32)
            children[at, 0:cells] = pooled_out[lane, s, 0].astype(F32)
            children[at, block - cells : block] = pooled_out[lane, s, 1].astype(F32)

    def child_at(child, start):
        at = jnp.clip(child - start * LANES * slots, 0, LANES * slots - 1)
        return jnp.where(child >= 0, at, LANES * slots)

    def halves(value, size):
        if size == 1:
            return value, 0
        return lax.div(value, size), lax.rem(value, size)

    @pl.loop(0, bricks)
    def _(j):
        lane, slot = halves(j, per)
        for o in range(8):
            at = child_at(meta_s[lane, slot, o], group)
            ox, oy, oz = o // 4 * half, o // 2 % 2 * half, o % 2 * half
            for x in range(half):
                for y in range(half):
                    row = (x * half + y) * half
                    coarse[j, ox + x, oy + y, oz : oz + half, :] = children[
                        at, row : row + half, :
                    ]

    def coarse_index(lane, slot, live):
        def index(t):
            value = meta_s[lane, per + slot, t]
            there = (value >= 0) & live
            if t // 9 == 1:
                return jnp.where(there, jnp.clip(value - group * bricks, 0, bricks - 1), bricks)
            at = jnp.clip(value - (group - 1) * bricks, 0, 3 * bricks - 1)
            return jnp.where(there, at, 3 * bricks)

        return index

    def keep_sides(source):
        for j in range(bricks):
            low_x[bricks + j] = source[j, 0]
            high_x[bricks + j] = source[j, edge - 1]

    own = bricks // 2
    def brick_of(i, odd):
        lane, slot = halves(i, per)
        return (2 * lane + odd) * per + slot

    def place_far(side):
        start = 2 * bricks * side
        for lane in range(LANES):
            for s in range(slots):
                far_children[side, lane * slots + s] = side_in[side, lane % 2, lane // 2, s].astype(F32)
        far_children[side, LANES * slots] = jnp.zeros((cells, width), F32)

        @pl.loop(0, bricks)
        def _(j):
            lane, slot = halves(j, per)
            for o in range(8):
                at = child_at(meta_far_s[side, lane, slot, o], group - 1 + 2 * side)
                oy, oz = o // 2 % 2 * half, o % 2 * half
                target = high_x if o // 4 else low_x
                for y in range(half):
                    target[start + j, oy + y, oz : oz + half, :] = far_children[
                        side, at, y * half : (y + 1) * half, :
                    ]

    def group_index(j):
        return coarse_index(*halves(j, per), True)

    keep_sides(coarse)
    def far_planes():
        pl.when(has_down)(lambda: hand_over(0).wait())
        pl.when(has_up)(lambda: hand_over(1).wait())
        pl.when(has_down)(lambda: far_to_smem(0).wait())
        pl.when(has_up)(lambda: far_to_smem(1).wait())
        pl.when(has_down)(lambda: place_far(0))
        pl.when(has_up)(lambda: place_far(1))


    loaded(2)

    def own_index(i):
        return group_index(brick_of(i, parity))

    def brick_copy(i):
        return remote(brick_out.at[i], brick_in.at[i], pair_send_sem, pair_recv_sem, peer(1))

    def planes_to(side, i, k):
        return remote(
            side_out2.at[i],
            side_in2.at[side, parity, i],
            side_send_sem.at[0, side],
            side_recv_sem.at[1, side],
            peer(k) + (LANES if side == 0 else -LANES),
        )

    def all_planes(side):
        return remote(
            side_in2.at[side],
            side_in2.at[side],
            side_send_sem.at[0, side],
            side_recv_sem.at[1, side],
            me + (LANES if side == 0 else -LANES),
        )

    @pl.loop(0, own)
    def _(i):
        index = own_index(i)
        (totals,) = local_product(coarse, [index], w2)
        opened[i, 0] = totals[0]
        opened[i, 1] = totals[edge - 1]
        value = jnp.maximum(jnp.concatenate(totals[1 : edge - 1], axis=0), 0.0).astype(BF16)
        brick_out[i, plane : (edge - 1) * plane] = value
        coarse2[brick_of(i, parity), 1 : edge - 1] = value.astype(F32).reshape(
            (edge - 2,) + face
        )
        pl.when(i == 0)(far_planes)
        assemble(pad, edge, None, high_x, low_x, index, far_taps)
        for side in range(2):
            shift(zfar, side * padded, pad, side * (edge + 1), slice(None), edge + 2)
        for side in range(2):
            added = stepped(zfar, [side * padded], padded, w2[2 * side])
            at = side * (edge - 1)
            value = jnp.maximum(opened[i, side] + tread(added, 0, plane), 0.0).astype(BF16)
            side_out2[i, side] = value
            brick_out[i, at * plane : (at + 1) * plane] = value
            coarse2[brick_of(i, parity), at] = value.astype(F32).reshape(face)

        def send_planes(side):
            for k in range(2):
                planes_to(side, i, k).start()

        pl.when(has_up)(lambda: send_planes(0))
        pl.when(has_down)(lambda: send_planes(1))
        brick_copy(i).start()

    loaded(3)

    part = half * edge
    strip = slots * part
    tall = half + 2
    column = tall * edge

    def parent_of(s):
        parent = fine_parent[s]
        safe = jnp.maximum(parent, 0)
        lane, slot = halves(jnp.clip(safe // 8 - group * bricks, 0, bricks - 1), per)
        octant = safe % 8
        ox, oy = lax.div(octant, 4), lax.rem(lax.div(octant, 2), 2)
        return lane, slot, ox, oy * half

    strips = 4
    span = width // strips

    @pl.loop(0, 3 * strips)
    def _(i):
        dz, strip_at = lax.div(i, strips), lax.rem(i, strips)
        rows = []
        for dy in range(3):
            start = pl.multiple_of((dy * 3 + dz) * width + strip_at * span, span)
            rows.append([w4[dx, pl.ds(start, span), :].astype(F32) for dx in range(3)])
        late = [r1 + r2 for r1, r2 in zip(rows[1], rows[2])]
        early = [r0 + r1 for r0, r1 in zip(rows[0], rows[1])]
        for py, parts in enumerate(((rows[0], late), (early, rows[2]))):
            for q, (a, b, c) in enumerate(parts):
                start = pl.multiple_of((q * 3 + dz) * width + strip_at * span, span)
                wup[py, pl.ds(start, span), :] = jnp.concatenate(
                    [b + c, a + b, a, c], axis=1
                ).astype(BF16)

    remote(brick_out, brick_in, pair_send_sem, pair_recv_sem, peer(1)).wait()
    for i in range(own):
        coarse2[brick_of(i, 1 - parity)] = brick_in[i].astype(F32).reshape(cube)
    keep_sides(coarse2)
    pad[0] = jnp.zeros(pad.shape[1:], F32)
    pad[edge + 1] = jnp.zeros(pad.shape[1:], F32)

    @pl.loop(0, slots)
    def _(s):
        lane, slot, ox, oy = parent_of(s)
        index = coarse_index(lane, slot, fine_parent[s] >= 0)
        assemble(pad, edge, coarse2, None, None, index, own_taps)
        for x in range(tall):
            row = pl.multiple_of((s * tall + x) * column, edge)
            shift(zq, row, pad, ox * half + x, pl.ds(oy, tall), tall)

    def starts_of(planes):
        return [(s * tall + x) * column for x in planes for s in range(slots)]

    two = dot(columns(zq, starts_of(range(half + 1)), part), taps(w3, 0, 1))
    third = stepped(
        zq, [(s * tall + 2) * column for s in range(slots)], half * column, w3[2]
    )
    for x in range(half):
        for s in range(slots):
            at = x * strip + s * part
            dacc[at : at + part, :] = (
                two[at : at + part, 0:width]
                + two[at + strip : at + strip + part, width : 2 * width]
                + tread(third, (s * half + x) * column, part)
            )

    def lift(s, x, value):
        piece = rounded(value)
        oz = lax.rem(jnp.maximum(fine_parent[s], 0), 2)
        start = x * 2 * part
        spread[s, pl.ds(start, part, stride=2), :] = piece
        spread[s, pl.ds(start + 1, part, stride=2), :] = piece
        for y in range(half):
            utab[s, x, y] = spread[s, pl.ds(start + (2 * y + oz) * edge, edge), :]

    for s in range(slots):
        for x in range(1, half - 1):
            lift(s, x, dacc[x * strip + s * part : x * strip + (s + 1) * part, :])
    @pl.when(has_down)
    def _():
        all_planes(0).wait_recv()
        all_planes(1).wait_send()

    @pl.when(has_up)
    def _():
        all_planes(1).wait_recv()
        all_planes(0).wait_send()

    for side in range(2):
        for odd in range(2):
            for i in range(own):
                at = 2 * bricks * side + (2 * (i // per) + odd) * per + i % per
                low_x[at] = side_in2[side, odd, i, 0].astype(F32).reshape(face)
                high_x[at] = side_in2[side, odd, i, 1].astype(F32).reshape(face)


    @pl.loop(0, slots)
    def _(s):
        lane, slot, ox, oy = parent_of(s)
        live = fine_parent[s] >= 0
        for k in range(9):
            value = meta_s[lane, per + slot, ox * 18 + k]
            at = jnp.clip(value - (group - 1) * bricks, 0, 3 * bricks - 1)
            at = jnp.where((value >= 0) & live, at, 3 * bricks)
            dy, dz = k // 3 - 1, k % 3 - 1
            piece = ends[ox, at, pick(dy, edge), pick(dz, edge), :]
            pad[0, place(dy, edge, 1), place(dz, edge, base), :] = piece
        row = pl.multiple_of(s * column, edge)
        shift(zfar, row, pad, 0, pl.ds(oy, tall), tall)

    far = dot(
        columns(zfar, [s * column for s in range(slots)], part),
        taps(w3, 0, 2),
    )
    picks[0] = far[:, 0:width]
    picks[1] = jnp.zeros((strip, width), F32)
    picks[2] = far[:, width : 2 * width]
    for s in range(slots):
        ox = parent_of(s)[2]
        rows = slice(s * part, (s + 1) * part)
        lift(s, 0, dacc[rows, :] + picks[ox, rows])
        last = (half - 1) * strip + s * part
        lift(s, half - 1, dacc[last : last + part, :] + picks[ox + 1, rows])
        stage_faces(face_out3, utab, half - 1, s)
    start_pair(halo3[0], has_next, halo3[1], has_prev)

    brick_rows = tall * column

    @pl.loop(0, slots)
    def _(b):
        assemble(upad, half, utab, None, None, fine_index(b), own_taps)
        for x in range(half):
            row = pl.multiple_of(b * brick_rows + (x + 1) * column, edge)
            shift(zu, row, upad, x + 1, slice(None), tall)

    def woven(zero, one):
        pair = jnp.stack(
            [zero.reshape(half, edge, width), one.reshape(half, edge, width)], axis=1
        )
        return pair.reshape(plane, width)

    inner = [b * brick_rows + (x + 1) * column for b in range(slots) for x in range(half)]
    direct, across = [], []
    for py in range(2):
        lhs = columns(zu, inner, part, (py, py + 1))
        direct.append(dot(lhs, wup[py, :, 0 : 2 * width]))
        across.append(dot(columns(zu, inner, part, (py, py + 1)), wup[py, :, 2 * width :]))

    for b in range(slots):
        for x in range(edge):
            i, px = x // 2, x % 2
            lanes = slice(px * width, (px + 1) * width)
            other = i - 1 + 2 * px
            sums = []
            for py in range(2):
                at = (b * half + i) * part
                value = direct[py][at : at + part, lanes]
                if 0 <= other < half:
                    at = (b * half + other) * part
                    value = value + across[py][at : at + part, lanes]
                sums.append(value)
            rows = slice(x * plane, (x + 1) * plane)
            total = acc[b, rows] + woven(*sums)
            if 0 <= other < half:
                out_ref[b, rows, :] = jnp.maximum(total, 0.0).astype(BF16)
            else:
                acc[b, rows] = total

    finish_pair(halo2[0], has_next, halo2[1], has_prev)
    take_faces(face_in2, below, above)

    def store_part(b, side, added):
        at = side * (edge - 1) * plane
        acc[b, at : at + plane] = acc[b, at : at + plane] + added

    outer_planes(slots, below, above, fine_index, w4, store_part)
    finish_pair(halo3[0], has_next, halo3[1], has_prev)
    take_faces(face_in3, ubelow, uabove)

    @pl.loop(0, slots)
    def _(b):
        assemble(upad, half, None, ubelow, uabove, fine_index(b), far_taps)
        for x in (0, half + 1):
            row = pl.multiple_of(b * brick_rows + x * column, edge)
            shift(zu, row, upad, x, slice(None), tall)

    for side in range(2):
        starts = [b * brick_rows + side * (half + 1) * column for b in range(slots)]
        lanes = slice((2 + side) * width, (3 + side) * width)
        sums = [dot(columns(zu, starts, part, (py, py + 1)), wup[py, :, lanes]) for py in range(2)]
        for b in range(slots):
            at = side * (edge - 1) * plane
            rows = slice(b * part, (b + 1) * part)
            total = acc[b, at : at + plane] + woven(sums[0][rows], sums[1][rows])
            out_ref[b, at : at + plane, :] = jnp.maximum(total, 0.0).astype(BF16)


def per_device(
    n,
    features,
    fine_nbr,
    fine_send,
    fine_parent,
    coarse_child,
    coarse_nbr,
    enc_fine_w,
    enc_coarse_w,
    dec_coarse_w,
    dec_fine_w,
):
    slots, edge, width = features.shape[0], features.shape[1], features.shape[-1]
    per = coarse_nbr.shape[0]
    bricks = LANES * per
    half = edge // 2
    plane = edge * edge
    voxels = edge**3
    padded = (edge + 2) * edge
    tall = half + 2
    rows = -(-2 * per // 8) * 8
    kernels = [
        w.reshape(3, 9 * width, width)
        for w in (enc_fine_w, enc_coarse_w, dec_coarse_w, dec_fine_w)
    ]
    vmem = pltpu.VMEM
    vmem_spec = pl.BlockSpec(memory_space=pltpu.VMEM)
    any_spec = pl.BlockSpec(memory_space=pl.ANY)
    cube = (edge, edge, edge, width)
    face = (edge, edge, width)
    dma = pltpu.SemaphoreType.DMA
    out = pl.pallas_call(
        functools.partial(kernel, n),
        out_shape=pltpu.VMEM((slots, voxels, width), BF16),
        in_specs=[any_spec] * 10,
        out_specs=vmem_spec,
        scratch_shapes=[
            pltpu.SMEM(fine_nbr.shape, jnp.int32),
            pltpu.SMEM(fine_send.shape[1:], jnp.int32),
            pltpu.SMEM(fine_parent.shape, jnp.int32),
            vmem(coarse_child.shape, jnp.int32),
            vmem(coarse_nbr.shape, jnp.int32),
            vmem((slots, voxels, width), BF16),
            *[vmem((3, 9 * width, width), BF16)] * 4,
            vmem((2, 6 * width, 4 * width), BF16),
            vmem((edge + 2, edge + 2, 3 * edge, width), F32),
            vmem((half + 2, half + 2, 3 * edge, width), F32),
            vmem((3, GROUP * edge * padded + edge, width), BF16),
            vmem((3, 2 * max(slots, bricks) * padded + edge, width), BF16),
            vmem((3, slots * tall * tall * edge + edge, width), BF16),
            vmem((3, slots * tall * tall * edge, width), BF16),
            vmem((max(slots, bricks), 2, plane, width), F32),
            vmem((slots, voxels, width), F32),
            vmem((half * slots * half * edge, width), F32),
            vmem((3, slots * half * edge, width), F32),
            vmem((slots + 1, half, half, edge, width), F32),
            vmem((slots + 1, half, edge, width), F32),
            vmem((slots + 1, half, edge, width), F32),
            vmem((slots + 1,) + cube, F32),
            vmem((slots + 1,) + cube, F32),
            vmem((slots + 1,) + face, F32),
            vmem((slots + 1,) + face, F32),
            vmem((2, slots, plane, width), BF16),
            vmem((2, slots, plane, width), BF16),
            vmem((2, slots, plane, width), BF16),
            vmem((2, slots, plane, width), BF16),
            vmem((2, slots, half * edge, width), BF16),
            vmem((2, slots, half * edge, width), BF16),
            vmem((half * half * edge, width), F32),
            vmem((LANES, slots, (half - 2) * half**2, width), BF16),
            vmem((LANES, slots, 2, half**2, width), BF16),
            vmem((slots, 2, half**2, width), BF16),
            vmem((LANES * slots + 1, half**3, width), F32),
            vmem((LANES, rows, 128), jnp.int32),
            pltpu.SMEM((LANES, rows, 128), jnp.int32),
            vmem((2, LANES, rows, 128), jnp.int32),
            pltpu.SMEM((2, LANES, rows, 128), jnp.int32),
            vmem((2, LANES * slots + 1, half**2, width), F32),
            vmem((bricks + 1,) + cube, F32),
            vmem((bricks + 1,) + cube, F32),
            vmem((2, 3 * bricks + 1) + face, F32),
            vmem((slots, half**2, width), BF16),
            vmem((2, 2, LANES // 2, slots, half**2, width), BF16),
            vmem((bricks // 2, 2, plane, width), BF16),
            vmem((2, 2, bricks // 2, 2, plane, width), BF16),
            vmem((bricks // 2, voxels, width), BF16),
            vmem((bricks // 2, voxels, width), BF16),
            vmem((slots, half * half * 2 * edge, width), F32),
            dma((5,)),
            dma((5,)),
            dma((2,)),
            dma((3, 2)),
            dma((3,)),
            dma((3,)),
            dma(()),
            dma(()),
            dma((2, 2)),
            dma((3, 2)),
            dma(()),
            dma(()),
            dma((2,)),
            dma((2,)),
            pltpu.SemaphoreType.REGULAR,
        ],
        compiler_params=pltpu.CompilerParams(
            collective_id=0, has_side_effects=True, vmem_limit_bytes=60 * 1024 * 1024
        ),
    )(
        fine_nbr,
        fine_send[0],
        fine_parent,
        coarse_child,
        coarse_nbr,
        features.reshape(slots, voxels, width),
        *kernels,
    )
    return out.reshape(features.shape)


def solution(mesh):
    lead = ("groups", "gx")
    placed = (
        P(lead, None, None, None, None),
        P(lead, None),
        P(lead, None, None),
        P(lead),
        P(lead, None),
        P(lead, None),
        P(),
        P(),
        P(),
        P(),
    )
    return jax.shard_map(
        functools.partial(per_device, mesh.shape["gx"]),
        mesh=mesh,
        in_specs=placed,
        out_specs=P(lead, None, None, None, None),
        check_vma=False,
    )
```

```python
import functools

import jax
import jax.numpy as jnp
from jax import lax
from jax.experimental import pallas as pl
from jax.experimental.pallas import tpu as pltpu
from jax.sharding import PartitionSpec as P

F32 = jnp.float32
BF16 = jnp.bfloat16
LANES = 4
GROUP = 2
MESH = pl.DeviceIdType.MESH


def pick(offset, edge):
    if offset < 0:
        return slice(edge - 1, edge)
    if offset == 0:
        return slice(0, edge)
    return slice(0, 1)


def place(offset, edge, base):
    if offset < 0:
        return slice(base - 1, base)
    if offset == 0:
        return slice(base, base + edge)
    return slice(base + edge, base + edge + 1)


def kernel(
    n,
    fine_nbr_hbm,
    fine_send_hbm,
    fine_parent_hbm,
    child_hbm,
    nbr_hbm,
    feat_hbm,
    w1_hbm,
    w2_hbm,
    w3_hbm,
    w4_hbm,
    out_ref,
    fine_nbr,
    fine_send,
    fine_parent,
    child_ref,
    nbr_ref,
    feat,
    w1,
    w2,
    w3,
    w4,
    wup,
    pad,
    upad,
    zs,
    zfar,
    zq,
    zu,
    opened,
    acc,
    dacc,
    picks,
    utab,
    ubelow,
    uabove,
    table,
    enc,
    below,
    above,
    face_out,
    face_in,
    face_out2,
    face_in2,
    face_out3,
    face_in3,
    half_z,
    pooled,
    pooled_out,
    own_out,
    children,
    meta,
    meta_s,
    meta_far,
    meta_far_s,
    far_children,
    coarse,
    coarse2,
    ends,
    side_out,
    side_in,
    side_out2,
    side_in2,
    brick_out,
    brick_in,
    spread,
    load_sem,
    small_sem,
    face_send_sem,
    face_recv_sem,
    pool_send_sem,
    pool_recv_sem,
    meta_send_sem,
    meta_recv_sem,
    side_send_sem,
    side_recv_sem,
    pair_send_sem,
    pair_recv_sem,
    hand_send_sem,
    hand_recv_sem,
    ready_sem,
):
    slots, edge = out_ref.shape[0], enc.shape[1]
    plane = edge * edge
    width = out_ref.shape[-1]
    half = edge // 2
    block = half**3
    per = child_ref.shape[0]
    bricks = LANES * per
    me = lax.axis_index("gx")
    member = lax.rem(me, LANES)
    group = lax.div(me, LANES)

    def peer(k):
        return me - member + (member ^ k)

    width = out_ref.shape[-1]
    loads = [[pltpu.make_async_copy(feat_hbm, feat, load_sem.at[0])]]
    for i, (src, dst) in enumerate(
        ((w1_hbm, w1), (w2_hbm, w2), (w3_hbm, w3), (w4_hbm, w4))
    ):
        loads.append([pltpu.make_async_copy(src, dst, load_sem.at[i + 1])])
    small = [
        pltpu.make_async_copy(src, dst, small_sem.at[i])
        for i, (src, dst) in enumerate(
            (
                (fine_nbr_hbm, fine_nbr),
                (fine_send_hbm, fine_send),
                (fine_parent_hbm, fine_parent),
                (child_hbm, child_ref),
                (nbr_hbm, nbr_ref),
            )
        )
    ]
    for copy in loads[0]:
        copy.start()
    for copy in small:
        copy.start()
    for copies in loads[1:]:
        for copy in copies:
            copy.start()

    def loaded(i):
        for copy in loads[i]:
            copy.wait()

    has_prev, has_next = me > 0, me < n - 1
    has_down, has_up = me >= LANES, me < n - LANES
    barrier = pltpu.get_barrier_semaphore()

    def greet(other):
        pl.semaphore_signal(barrier, inc=1, device_id={"gx": other}, device_id_type=MESH)

    for k in range(1, LANES):
        greet(peer(k))
    first = me - member
    sides = (
        (has_prev & (member == 0), me - 1),
        (has_next & (member == LANES - 1), me + 1),
        (has_down, me - LANES),
        (has_up, me + LANES),
    )
    peers = LANES - 1
    for there, other in sides:
        pl.when(there)(functools.partial(greet, other))
        peers = peers + jnp.where(there, 1, 0)

    def remote(src, dst, send, recv, other):
        return pltpu.make_async_remote_copy(
            src_ref=src,
            dst_ref=dst,
            send_sem=send,
            recv_sem=recv,
            device_id={"gx": other},
            device_id_type=MESH,
        )

    def face_copies(outgoing, incoming, phase):
        up = remote(
            outgoing.at[0],
            incoming.at[0],
            face_send_sem.at[0],
            face_recv_sem.at[phase, 0],
            me + 1,
        )
        down = remote(
            outgoing.at[1],
            incoming.at[1],
            face_send_sem.at[1],
            face_recv_sem.at[phase, 1],
            me - 1,
        )
        return up, down

    def start_pair(up, up_there, down, down_there):
        pl.when(up_there)(up.start)
        pl.when(down_there)(down.start)

    def finish_pair(up, up_there, down, down_there):
        @pl.when(down_there)
        def _():
            up.wait_recv()
            down.wait_send()

        @pl.when(up_there)
        def _():
            down.wait_recv()
            up.wait_send()


    cube = (edge, edge, edge, width)
    face = (edge, edge, width)
    base = edge
    high_x, low_x = ends.at[0], ends.at[1]
    padded = (edge + 2) * edge
    own_taps = range(9, 18)
    far_taps = (*range(9), *range(18, 27))
    zero_brick = jnp.zeros(cube, F32)
    zero_plane = jnp.zeros(face, F32)
    table[slots] = zero_brick
    enc[slots] = zero_brick

    def stage_faces(outgoing, source, last, s):
        up_from = jnp.where(fine_send[0, s] >= 0, s, slots)
        down_from = jnp.where(fine_send[1, s] >= 0, s, slots)
        rows = outgoing.shape[2]
        outgoing[0, s] = source[up_from, last].reshape(rows, width).astype(BF16)
        outgoing[1, s] = source[down_from, 0].reshape(rows, width).astype(BF16)

    loaded(0)
    for s in range(slots):
        table[s] = feat[s].astype(F32).reshape(cube)
    for copy in small:
        copy.wait()
    meta[member, 0:per, 0 : child_ref.shape[1]] = child_ref[...]
    meta[member, per : 2 * per, 0 : nbr_ref.shape[1]] = nbr_ref[...]
    for s in range(slots):
        stage_faces(face_out, table, edge - 1, s)
    halo1 = face_copies(face_out, face_in, 0)
    halo2 = face_copies(face_out2, face_in2, 1)
    halo3 = face_copies(face_out3, face_in3, 2)
    meta_copies = [
        remote(
            meta.at[member],
            meta.at[member],
            meta_send_sem,
            meta_recv_sem,
            peer(k),
        )
        for k in range(1, LANES)
    ]

    below[slots] = zero_plane
    above[slots] = zero_plane
    coarse[bricks] = zero_brick
    coarse2[bricks] = zero_brick
    low_x[3 * bricks] = zero_plane
    high_x[3 * bricks] = zero_plane
    children[LANES * slots] = jnp.zeros((block, width), F32)
    utab[slots] = jnp.zeros((half, half, edge, width), F32)
    ubelow[slots] = jnp.zeros((half, edge, width), F32)
    uabove[slots] = jnp.zeros((half, edge, width), F32)

    def assemble(target, side, centre, lower, upper, index, taps):
        for t in taps:
            dx, dy, dz = t // 9 - 1, t // 3 % 3 - 1, t % 3 - 1
            at = index(t)
            ys, zs = pick(dy, side), pick(dz, edge)
            if dx == 0:
                piece = centre[at, :, ys, zs, :]
            elif dx < 0:
                piece = lower[at, ys, zs, :][None]
            else:
                piece = upper[at, ys, zs, :][None]
            target[place(dx, side, 1), place(dy, side, 1), place(dz, edge, base), :] = piece

    def shift(store, row, source, x, y, count):
        rows = count * edge
        for dz in range(3):
            first = base + dz - 1
            piece = source[x, y, first : first + edge, :]
            store[dz, pl.ds(row, rows), :] = piece.reshape(rows, width).astype(BF16)

    def columns(store, starts, rows, offsets=(0, 1, 2)):
        return jnp.concatenate(
            [
                jnp.concatenate(
                    [store[dz, r + dy * edge : r + dy * edge + rows, :] for r in starts], axis=0
                )
                for dy in offsets
                for dz in range(3)
            ],
            axis=1,
        )

    def taps(weights, *sides):
        return jnp.concatenate([weights[dx] for dx in sides], axis=1)

    def dot(a, b):
        return jnp.dot(a, b, preferred_element_type=F32)

    def stepped(store, starts, rows, weight):
        third = 3 * width
        first, middle, last = (weight[i * third : (i + 1) * third, :] for i in range(3))
        both = jnp.concatenate(
            [
                jnp.concatenate([first, middle], axis=1),
                jnp.concatenate([jnp.zeros((third, width), BF16), last], axis=1),
            ],
            axis=0,
        )
        return dot(columns(store, starts, rows, (0, 1)), both)

    def tread(value, row, rows):
        return value[row : row + rows, 0:width] + value[row + edge : row + edge + rows, width:]

    def local_product(centre, indices, weights):
        rows = edge * padded
        for i, index in enumerate(indices):
            assemble(pad, edge, centre, None, None, index, own_taps)
            for x in range(edge):
                shift(zs, i * rows + x * padded, pad, x + 1, slice(None), edge + 2)
        count = len(indices)
        starts = [i * rows + x * padded for i in range(count) for x in range(edge)]
        two = dot(columns(zs, starts, plane), taps(weights, 0, 1))
        inner = [i * rows + padded for i in range(count)]
        third = stepped(zs, inner, (edge - 1) * padded, weights[2])
        results = []
        for i in range(count):
            totals = []
            for x in range(edge):
                at = (i * edge + x) * plane
                total = two[at : at + plane, width : 2 * width]
                if x > 0:
                    total = total + two[at - plane : at, 0:width]
                if x < edge - 1:
                    total = total + tread(third, (i * (edge - 1) + x) * padded, plane)
                totals.append(total)
            results.append(totals)
        return results

    def outer_planes(count, lower, upper, index_of, weights, store):
        @pl.loop(0, count)
        def _(j):
            assemble(pad, edge, None, lower, upper, index_of(j), far_taps)
            for side in range(2):
                row = pl.multiple_of((side * count + j) * padded, edge)
                shift(zfar, row, pad, side * (edge + 1), slice(None), edge + 2)

        for side in range(2):
            added = stepped(zfar, [side * count * padded], count * padded, weights[2 * side])
            for j in range(count):
                store(j, side, tread(added, j * padded, plane))

    def rounded(value):
        return jnp.maximum(value, 0.0).astype(BF16).astype(F32)

    def fine_index(b):
        def index(t):
            at = fine_nbr[b, t]
            return jnp.where(at >= 0, at, slots)

        return index

    def take_faces(incoming, low, high):
        shape = low.shape[1:]
        for s in range(slots):
            low[s] = incoming[0, s].astype(F32).reshape(shape)
            high[s] = incoming[1, s].astype(F32).reshape(shape)

    cells = half * half

    def pool_copy(k, b):
        source = pooled_out.at[member] if b is None else pooled.at[member, b]
        stage = 1 if b is None else 2 * (k - 1)
        return remote(
            source, source, pool_send_sem.at[stage], pool_recv_sem.at[stage], peer(k)
        )

    def all_pooled(stage):
        source = (pooled.at[0:2], pooled_out.at[0 : LANES - 1], pooled.at[0])[stage]
        return remote(
            source, source, pool_send_sem.at[stage], pool_recv_sem.at[stage], peer(1)
        )

    def pass_pooled():
        source = pooled.at[member ^ 2]
        return remote(source, source, pool_send_sem.at[0], pool_recv_sem.at[0], peer(1))

    def pool(value, count):
        pairs = value.reshape(count, 2, half, 2, edge, width)
        summed = (pairs[:, 0, :, 0] + pairs[:, 0, :, 1]) + (pairs[:, 1, :, 0] + pairs[:, 1, :, 1])
        half_z[0 : count * half * edge, :] = summed.reshape(count * half * edge, width)
        even = half_z[pl.ds(0, count * cells, stride=2), :]
        odd = half_z[pl.ds(1, count * cells, stride=2), :]
        return ((even + odd) * 0.125).astype(BF16)

    def side_copies(outgoing, incoming, phase):
        up = remote(
            outgoing,
            incoming.at[0],
            side_send_sem.at[min(phase, 1), 0],
            side_recv_sem.at[phase, 0],
            me + LANES,
        )
        down = remote(
            outgoing,
            incoming.at[1],
            side_send_sem.at[min(phase, 1), 1],
            side_recv_sem.at[phase, 1],
            me - LANES,
        )
        return up, down

    pl.semaphore_wait(barrier, peers)
    for k in range(1, LANES):
        pl.semaphore_signal(ready_sem, inc=1, device_id={"gx": peer(k)}, device_id_type=MESH)
    for copy in meta_copies:
        copy.start()
    start_pair(halo1[0], has_next, halo1[1], has_prev)
    loaded(1)

    at_once = GROUP if slots % GROUP == 0 else 1

    def encode(h):
        bricks_of = [at_once * h + i for i in range(at_once)]
        results = local_product(table, [fine_index(b) for b in bricks_of], w1)
        for b, totals in zip(bricks_of, results):
            opened[b, 0] = totals[0]
            opened[b, 1] = totals[edge - 1]
            value = rounded(jnp.concatenate(totals[1 : edge - 1], axis=0))
            value = value.reshape((edge - 2,) + face)
            enc[b, 1 : edge - 1] = value
            pooled[member, b] = pool(value[1 : edge - 3], half - 2)

    def send_pooled(b):
        for k in (2, 1):
            pool_copy(k, b).start()


    @pl.loop(0, slots // at_once)
    def _(h):
        encode(h)

    for b in range(slots):
        send_pooled(b)

    finish_pair(halo1[0], has_next, halo1[1], has_prev)
    take_faces(face_in, below, above)

    every_meta = meta.at[0 : LANES - 1]
    remote(every_meta, every_meta, meta_send_sem, meta_recv_sem, peer(1)).wait()
    to_smem = pltpu.make_async_copy(meta, meta_s, small_sem.at[0])
    to_smem.start()
    hop_meta = side_copies(meta, meta_far, 2)
    start_pair(hop_meta[0], has_up, hop_meta[1], has_down)
    def store_enc(b, side, added):
        enc[b, side * (edge - 1)] = rounded(opened[b, side] + added).reshape(face)

    outer_planes(slots, below, above, fine_index, w1, store_enc)
    for b in range(slots):
        for side in range(2):
            start = side * (edge - 2)
            value = pool(enc[b, start : start + 2], 1)
            pooled_out[member, b, side] = value
            own_out[b, side] = value
    for k in range(1, LANES):
        pool_copy(k, None).start()
    for s in range(slots):
        octant = lax.rem(jnp.maximum(fine_parent[s], 0), 8)
        side_out[s] = own_out[s, lax.div(octant, 4)]

    parity = lax.rem(member, 2)

    def face_to(side, h):
        return remote(
            side_out,
            side_in.at[side, parity, lax.div(member, 2)],
            side_send_sem.at[0, side],
            side_recv_sem.at[0, side],
            first + (LANES if side == 0 else -LANES) + 2 * h + parity,
        )

    def faces_to(side):
        for h in range(LANES // 2):
            face_to(side, h).start()

    def all_faces(side):
        return remote(
            side_in.at[side, 0],
            side_in.at[side, 0],
            side_send_sem.at[0, side],
            side_recv_sem.at[0, side],
            me + (LANES if side == 0 else -LANES),
        )

    def hand_over(side):
        block_of = side_in.at[side, parity]
        return remote(block_of, block_of, hand_send_sem.at[side], hand_recv_sem.at[side], peer(1))

    pl.semaphore_wait(ready_sem, LANES - 1)
    pl.when(has_up)(lambda: faces_to(0))
    pl.when(has_down)(lambda: faces_to(1))
    for s in range(slots):
        stage_faces(face_out2, enc, edge - 1, s)

    loaded(4)

    def decode_part(b):
        (totals,) = local_product(enc, [fine_index(b)], w4)
        acc[b] = jnp.concatenate(totals, axis=0)

    def run_decode(first, last):
        @pl.loop(first, last)
        def _(b):
            decode_part(b)

            @pl.when(b == max(slots - 2, 0))
            def _():
                all_pooled(2).wait_recv()
                pass_pooled().start()

    run_decode(0, slots)

    to_smem.wait()
    finish_pair(hop_meta[0], has_up, hop_meta[1], has_down)

    def far_to_smem(side):
        return pltpu.make_async_copy(meta_far.at[side], meta_far_s.at[side], small_sem.at[1 + side])

    pl.when(has_down)(lambda: far_to_smem(0).start())
    pl.when(has_up)(lambda: far_to_smem(1).start())
    for stage in range(2):
        all_pooled(stage).wait()
    all_pooled(2).wait_send()

    @pl.when(has_down)
    def _():
        all_faces(0).wait_recv()
        all_faces(1).wait_send()
        hand_over(0).start()

    @pl.when(has_up)
    def _():
        all_faces(1).wait_recv()
        all_faces(0).wait_send()
        hand_over(1).start()

    start_pair(halo2[0], has_next, halo2[1], has_prev)
    for lane in range(LANES):
        for s in range(slots):
            at = lane * slots + s
            children[at, cells : block - cells] = pooled[lane, s].astype(F32)
            children[at, 0:cells] = pooled_out[lane, s, 0].astype(F32)
            children[at, block - cells : block] = pooled_out[lane, s, 1].astype(F32)

    def child_at(child, start):
        at = jnp.clip(child - start * LANES * slots, 0, LANES * slots - 1)
        return jnp.where(child >= 0, at, LANES * slots)

    def halves(value, size):
        if size == 1:
            return value, 0
        return lax.div(value, size), lax.rem(value, size)

    @pl.loop(0, bricks)
    def _(j):
        lane, slot = halves(j, per)
        for o in range(8):
            at = child_at(meta_s[lane, slot, o], group)
            ox, oy, oz = o // 4 * half, o // 2 % 2 * half, o % 2 * half
            for x in range(half):
                for y in range(half):
                    row = (x * half + y) * half
                    coarse[j, ox + x, oy + y, oz : oz + half, :] = children[
                        at, row : row + half, :
                    ]

    def coarse_index(lane, slot, live):
        def index(t):
            value = meta_s[lane, per + slot, t]
            there = (value >= 0) & live
            if t // 9 == 1:
                return jnp.where(there, jnp.clip(value - group * bricks, 0, bricks - 1), bricks)
            at = jnp.clip(value - (group - 1) * bricks, 0, 3 * bricks - 1)
            return jnp.where(there, at, 3 * bricks)

        return index

    def keep_sides(source):
        for j in range(bricks):
            low_x[bricks + j] = source[j, 0]
            high_x[bricks + j] = source[j, edge - 1]

    own = bricks // 2
    def brick_of(i, odd):
        lane, slot = halves(i, per)
        return (2 * lane + odd) * per + slot

    def place_far(side):
        start = 2 * bricks * side
        for lane in range(LANES):
            for s in range(slots):
                far_children[side, lane * slots + s] = side_in[side, lane % 2, lane // 2, s].astype(F32)
        far_children[side, LANES * slots] = jnp.zeros((cells, width), F32)

        @pl.loop(0, bricks)
        def _(j):
            lane, slot = halves(j, per)
            for o in range(8):
                at = child_at(meta_far_s[side, lane, slot, o], group - 1 + 2 * side)
                oy, oz = o // 2 % 2 * half, o % 2 * half
                target = high_x if o // 4 else low_x
                for y in range(half):
                    target[start + j, oy + y, oz : oz + half, :] = far_children[
                        side, at, y * half : (y + 1) * half, :
                    ]

    def group_index(j):
        return coarse_index(*halves(j, per), True)

    keep_sides(coarse)
    def far_planes():
        pl.when(has_down)(lambda: hand_over(0).wait())
        pl.when(has_up)(lambda: hand_over(1).wait())
        pl.when(has_down)(lambda: far_to_smem(0).wait())
        pl.when(has_up)(lambda: far_to_smem(1).wait())
        pl.when(has_down)(lambda: place_far(0))
        pl.when(has_up)(lambda: place_far(1))


    loaded(2)

    def own_index(i):
        return group_index(brick_of(i, parity))

    def brick_copy(i):
        return remote(brick_out.at[i], brick_in.at[i], pair_send_sem, pair_recv_sem, peer(1))

    def planes_to(side, i, k):
        return remote(
            side_out2.at[i],
            side_in2.at[side, parity, i],
            side_send_sem.at[0, side],
            side_recv_sem.at[1, side],
            peer(k) + (LANES if side == 0 else -LANES),
        )

    def all_planes(side):
        return remote(
            side_in2.at[side],
            side_in2.at[side],
            side_send_sem.at[0, side],
            side_recv_sem.at[1, side],
            me + (LANES if side == 0 else -LANES),
        )

    @pl.loop(0, own)
    def _(i):
        index = own_index(i)
        (totals,) = local_product(coarse, [index], w2)
        opened[i, 0] = totals[0]
        opened[i, 1] = totals[edge - 1]
        value = jnp.maximum(jnp.concatenate(totals[1 : edge - 1], axis=0), 0.0).astype(BF16)
        brick_out[i, plane : (edge - 1) * plane] = value
        coarse2[brick_of(i, parity), 1 : edge - 1] = value.astype(F32).reshape(
            (edge - 2,) + face
        )
        pl.when(i == 0)(far_planes)
        assemble(pad, edge, None, high_x, low_x, index, far_taps)
        for side in range(2):
            shift(zfar, side * padded, pad, side * (edge + 1), slice(None), edge + 2)
        for side in range(2):
            added = stepped(zfar, [side * padded], padded, w2[2 * side])
            at = side * (edge - 1)
            value = jnp.maximum(opened[i, side] + tread(added, 0, plane), 0.0).astype(BF16)
            side_out2[i, side] = value
            brick_out[i, at * plane : (at + 1) * plane] = value
            coarse2[brick_of(i, parity), at] = value.astype(F32).reshape(face)

        def send_planes(side):
            for k in range(2):
                planes_to(side, i, k).start()

        pl.when(has_up)(lambda: send_planes(0))
        pl.when(has_down)(lambda: send_planes(1))
        brick_copy(i).start()

    loaded(3)

    part = half * edge
    strip = slots * part
    tall = half + 2
    column = tall * edge

    def parent_of(s):
        parent = fine_parent[s]
        safe = jnp.maximum(parent, 0)
        lane, slot = halves(jnp.clip(safe // 8 - group * bricks, 0, bricks - 1), per)
        octant = safe % 8
        ox, oy = lax.div(octant, 4), lax.rem(lax.div(octant, 2), 2)
        return lane, slot, ox, oy * half

    strips = 4
    span = width // strips

    @pl.loop(0, 3 * strips)
    def _(i):
        dz, strip_at = lax.div(i, strips), lax.rem(i, strips)
        rows = []
        for dy in range(3):
            start = pl.multiple_of((dy * 3 + dz) * width + strip_at * span, span)
            rows.append([w4[dx, pl.ds(start, span), :].astype(F32) for dx in range(3)])
        late = [r1 + r2 for r1, r2 in zip(rows[1], rows[2])]
        early = [r0 + r1 for r0, r1 in zip(rows[0], rows[1])]
        for py, parts in enumerate(((rows[0], late), (early, rows[2]))):
            for q, (a, b, c) in enumerate(parts):
                start = pl.multiple_of((q * 3 + dz) * width + strip_at * span, span)
                wup[py, pl.ds(start, span), :] = jnp.concatenate(
                    [b + c, a + b, a, c], axis=1
                ).astype(BF16)

    remote(brick_out, brick_in, pair_send_sem, pair_recv_sem, peer(1)).wait()
    for i in range(own):
        coarse2[brick_of(i, 1 - parity)] = brick_in[i].astype(F32).reshape(cube)
    keep_sides(coarse2)
    pad[0] = jnp.zeros(pad.shape[1:], F32)
    pad[edge + 1] = jnp.zeros(pad.shape[1:], F32)

    @pl.loop(0, slots)
    def _(s):
        lane, slot, ox, oy = parent_of(s)
        index = coarse_index(lane, slot, fine_parent[s] >= 0)
        assemble(pad, edge, coarse2, None, None, index, own_taps)
        for x in range(tall):
            row = pl.multiple_of((s * tall + x) * column, edge)
            shift(zq, row, pad, ox * half + x, pl.ds(oy, tall), tall)

    def starts_of(planes):
        return [(s * tall + x) * column for x in planes for s in range(slots)]

    two = dot(columns(zq, starts_of(range(half + 1)), part), taps(w3, 0, 1))
    third = stepped(
        zq, [(s * tall + 2) * column for s in range(slots)], half * column, w3[2]
    )
    for x in range(half):
        for s in range(slots):
            at = x * strip + s * part
            dacc[at : at + part, :] = (
                two[at : at + part, 0:width]
                + two[at + strip : at + strip + part, width : 2 * width]
                + tread(third, (s * half + x) * column, part)
            )

    def lift(s, x, value):
        piece = rounded(value)
        oz = lax.rem(jnp.maximum(fine_parent[s], 0), 2)
        start = x * 2 * part
        spread[s, pl.ds(start, part, stride=2), :] = piece
        spread[s, pl.ds(start + 1, part, stride=2), :] = piece
        for y in range(half):
            utab[s, x, y] = spread[s, pl.ds(start + (2 * y + oz) * edge, edge), :]

    for s in range(slots):
        for x in range(1, half - 1):
            lift(s, x, dacc[x * strip + s * part : x * strip + (s + 1) * part, :])
    @pl.when(has_down)
    def _():
        all_planes(0).wait_recv()
        all_planes(1).wait_send()

    @pl.when(has_up)
    def _():
        all_planes(1).wait_recv()
        all_planes(0).wait_send()

    for side in range(2):
        for odd in range(2):
            for i in range(own):
                at = 2 * bricks * side + (2 * (i // per) + odd) * per + i % per
                low_x[at] = side_in2[side, odd, i, 0].astype(F32).reshape(face)
                high_x[at] = side_in2[side, odd, i, 1].astype(F32).reshape(face)


    @pl.loop(0, slots)
    def _(s):
        lane, slot, ox, oy = parent_of(s)
        live = fine_parent[s] >= 0
        for k in range(9):
            value = meta_s[lane, per + slot, ox * 18 + k]
            at = jnp.clip(value - (group - 1) * bricks, 0, 3 * bricks - 1)
            at = jnp.where((value >= 0) & live, at, 3 * bricks)
            dy, dz = k // 3 - 1, k % 3 - 1
            piece = ends[ox, at, pick(dy, edge), pick(dz, edge), :]
            pad[0, place(dy, edge, 1), place(dz, edge, base), :] = piece
        row = pl.multiple_of(s * column, edge)
        shift(zfar, row, pad, 0, pl.ds(oy, tall), tall)

    far = dot(
        columns(zfar, [s * column for s in range(slots)], part),
        taps(w3, 0, 2),
    )
    picks[0] = far[:, 0:width]
    picks[1] = jnp.zeros((strip, width), F32)
    picks[2] = far[:, width : 2 * width]
    for s in range(slots):
        ox = parent_of(s)[2]
        rows = slice(s * part, (s + 1) * part)
        lift(s, 0, dacc[rows, :] + picks[ox, rows])
        last = (half - 1) * strip + s * part
        lift(s, half - 1, dacc[last : last + part, :] + picks[ox + 1, rows])
        stage_faces(face_out3, utab, half - 1, s)
    start_pair(halo3[0], has_next, halo3[1], has_prev)

    brick_rows = tall * column

    @pl.loop(0, slots)
    def _(b):
        assemble(upad, half, utab, None, None, fine_index(b), own_taps)
        for x in range(half):
            row = pl.multiple_of(b * brick_rows + (x + 1) * column, edge)
            shift(zu, row, upad, x + 1, slice(None), tall)

    def woven(zero, one):
        pair = jnp.stack(
            [zero.reshape(half, edge, width), one.reshape(half, edge, width)], axis=1
        )
        return pair.reshape(plane, width)

    inner = [b * brick_rows + (x + 1) * column for b in range(slots) for x in range(half)]
    direct, across = [], []
    for py in range(2):
        lhs = columns(zu, inner, part, (py, py + 1))
        direct.append(dot(lhs, wup[py, :, 0 : 2 * width]))
        across.append(dot(columns(zu, inner, part, (py, py + 1)), wup[py, :, 2 * width :]))

    for b in range(slots):
        for x in range(edge):
            i, px = x // 2, x % 2
            lanes = slice(px * width, (px + 1) * width)
            other = i - 1 + 2 * px
            sums = []
            for py in range(2):
                at = (b * half + i) * part
                value = direct[py][at : at + part, lanes]
                if 0 <= other < half:
                    at = (b * half + other) * part
                    value = value + across[py][at : at + part, lanes]
                sums.append(value)
            rows = slice(x * plane, (x + 1) * plane)
            total = acc[b, rows] + woven(*sums)
            if 0 <= other < half:
                out_ref[b, rows, :] = jnp.maximum(total, 0.0).astype(BF16)
            else:
                acc[b, rows] = total

    finish_pair(halo2[0], has_next, halo2[1], has_prev)
    take_faces(face_in2, below, above)

    def store_part(b, side, added):
        at = side * (edge - 1) * plane
        acc[b, at : at + plane] = acc[b, at : at + plane] + added

    outer_planes(slots, below, above, fine_index, w4, store_part)
    finish_pair(halo3[0], has_next, halo3[1], has_prev)
    take_faces(face_in3, ubelow, uabove)

    @pl.loop(0, slots)
    def _(b):
        assemble(upad, half, None, ubelow, uabove, fine_index(b), far_taps)
        for x in (0, half + 1):
            row = pl.multiple_of(b * brick_rows + x * column, edge)
            shift(zu, row, upad, x, slice(None), tall)

    for side in range(2):
        starts = [b * brick_rows + side * (half + 1) * column for b in range(slots)]
        lanes = slice((2 + side) * width, (3 + side) * width)
        sums = [dot(columns(zu, starts, part, (py, py + 1)), wup[py, :, lanes]) for py in range(2)]
        for b in range(slots):
            at = side * (edge - 1) * plane
            rows = slice(b * part, (b + 1) * part)
            total = acc[b, at : at + plane] + woven(sums[0][rows], sums[1][rows])
            out_ref[b, at : at + plane, :] = jnp.maximum(total, 0.0).astype(BF16)


def per_device(
    n,
    features,
    fine_nbr,
    fine_send,
    fine_parent,
    coarse_child,
    coarse_nbr,
    enc_fine_w,
    enc_coarse_w,
    dec_coarse_w,
    dec_fine_w,
):
    slots, edge, width = features.shape[0], features.shape[1], features.shape[-1]
    per = coarse_nbr.shape[0]
    bricks = LANES * per
    half = edge // 2
    plane = edge * edge
    voxels = edge**3
    padded = (edge + 2) * edge
    tall = half + 2
    rows = -(-2 * per // 8) * 8
    kernels = [
        w.reshape(3, 9 * width, width)
        for w in (enc_fine_w, enc_coarse_w, dec_coarse_w, dec_fine_w)
    ]
    vmem = pltpu.VMEM
    vmem_spec = pl.BlockSpec(memory_space=pltpu.VMEM)
    any_spec = pl.BlockSpec(memory_space=pl.ANY)
    cube = (edge, edge, edge, width)
    face = (edge, edge, width)
    dma = pltpu.SemaphoreType.DMA
    out = pl.pallas_call(
        functools.partial(kernel, n),
        out_shape=pltpu.VMEM((slots, voxels, width), BF16),
        in_specs=[any_spec] * 10,
        out_specs=vmem_spec,
        scratch_shapes=[
            pltpu.SMEM(fine_nbr.shape, jnp.int32),
            pltpu.SMEM(fine_send.shape[1:], jnp.int32),
            pltpu.SMEM(fine_parent.shape, jnp.int32),
            vmem(coarse_child.shape, jnp.int32),
            vmem(coarse_nbr.shape, jnp.int32),
            vmem((slots, voxels, width), BF16),
            *[vmem((3, 9 * width, width), BF16)] * 4,
            vmem((2, 6 * width, 4 * width), BF16),
            vmem((edge + 2, edge + 2, 3 * edge, width), F32),
            vmem((half + 2, half + 2, 3 * edge, width), F32),
            vmem((3, GROUP * edge * padded + edge, width), BF16),
            vmem((3, 2 * max(slots, bricks) * padded + edge, width), BF16),
            vmem((3, slots * tall * tall * edge + edge, width), BF16),
            vmem((3, slots * tall * tall * edge, width), BF16),
            vmem((max(slots, bricks), 2, plane, width), F32),
            vmem((slots, voxels, width), F32),
            vmem((half * slots * half * edge, width), F32),
            vmem((3, slots * half * edge, width), F32),
            vmem((slots + 1, half, half, edge, width), F32),
            vmem((slots + 1, half, edge, width), F32),
            vmem((slots + 1, half, edge, width), F32),
            vmem((slots + 1,) + cube, F32),
            vmem((slots + 1,) + cube, F32),
            vmem((slots + 1,) + face, F32),
            vmem((slots + 1,) + face, F32),
            vmem((2, slots, plane, width), BF16),
            vmem((2, slots, plane, width), BF16),
            vmem((2, slots, plane, width), BF16),
            vmem((2, slots, plane, width), BF16),
            vmem((2, slots, half * edge, width), BF16),
            vmem((2, slots, half * edge, width), BF16),
            vmem((half * half * edge, width), F32),
            vmem((LANES, slots, (half - 2) * half**2, width), BF16),
            vmem((LANES, slots, 2, half**2, width), BF16),
            vmem((slots, 2, half**2, width), BF16),
            vmem((LANES * slots + 1, half**3, width), F32),
            vmem((LANES, rows, 128), jnp.int32),
            pltpu.SMEM((LANES, rows, 128), jnp.int32),
            vmem((2, LANES, rows, 128), jnp.int32),
            pltpu.SMEM((2, LANES, rows, 128), jnp.int32),
            vmem((2, LANES * slots + 1, half**2, width), F32),
            vmem((bricks + 1,) + cube, F32),
            vmem((bricks + 1,) + cube, F32),
            vmem((2, 3 * bricks + 1) + face, F32),
            vmem((slots, half**2, width), BF16),
            vmem((2, 2, LANES // 2, slots, half**2, width), BF16),
            vmem((bricks // 2, 2, plane, width), BF16),
            vmem((2, 2, bricks // 2, 2, plane, width), BF16),
            vmem((bricks // 2, voxels, width), BF16),
            vmem((bricks // 2, voxels, width), BF16),
            vmem((slots, half * half * 2 * edge, width), F32),
            dma((5,)),
            dma((5,)),
            dma((2,)),
            dma((3, 2)),
            dma((3,)),
            dma((3,)),
            dma(()),
            dma(()),
            dma((2, 2)),
            dma((3, 2)),
            dma(()),
            dma(()),
            dma((2,)),
            dma((2,)),
            pltpu.SemaphoreType.REGULAR,
        ],
        compiler_params=pltpu.CompilerParams(
            collective_id=0, has_side_effects=True, vmem_limit_bytes=60 * 1024 * 1024
        ),
    )(
        fine_nbr,
        fine_send[0],
        fine_parent,
        coarse_child,
        coarse_nbr,
        features.reshape(slots, voxels, width),
        *kernels,
    )
    return out.reshape(features.shape)


def solution(mesh):
    lead = ("groups", "gx")
    placed = (
        P(lead, None, None, None, None),
        P(lead, None),
        P(lead, None, None),
        P(lead),
        P(lead, None),
        P(lead, None),
        P(),
        P(),
        P(),
        P(),
    )
    return jax.shard_map(
        functools.partial(per_device, mesh.shape["gx"]),
        mesh=mesh,
        in_specs=placed,
        out_specs=P(lead, None, None, None, None),
        check_vma=False,
    )
```

```python
import functools

import jax
import jax.numpy as jnp
from jax import lax
from jax.experimental import pallas as pl
from jax.experimental.pallas import tpu as pltpu
from jax.sharding import PartitionSpec as P

F32 = jnp.float32
BF16 = jnp.bfloat16
LANES = 4
GROUP = 2
MESH = pl.DeviceIdType.MESH


def pick(offset, edge):
    if offset < 0:
        return slice(edge - 1, edge)
    if offset == 0:
        return slice(0, edge)
    return slice(0, 1)


def place(offset, edge, base):
    if offset < 0:
        return slice(base - 1, base)
    if offset == 0:
        return slice(base, base + edge)
    return slice(base + edge, base + edge + 1)


def kernel(
    n,
    fine_nbr_hbm,
    fine_send_hbm,
    fine_parent_hbm,
    child_hbm,
    nbr_hbm,
    feat_hbm,
    w1_hbm,
    w2_hbm,
    w3_hbm,
    w4_hbm,
    out_ref,
    fine_nbr,
    fine_send,
    fine_parent,
    child_ref,
    nbr_ref,
    feat,
    w1,
    w2,
    w3,
    w4,
    wup,
    pad,
    upad,
    zs,
    zfar,
    zq,
    zu,
    opened,
    acc,
    dacc,
    picks,
    utab,
    ubelow,
    uabove,
    table,
    enc,
    below,
    above,
    face_out,
    face_in,
    face_out2,
    face_in2,
    face_out3,
    face_in3,
    half_z,
    pooled,
    pooled_out,
    own_out,
    children,
    meta,
    meta_s,
    meta_far,
    meta_far_s,
    far_children,
    coarse,
    coarse2,
    ends,
    side_out,
    side_in,
    side_out2,
    side_in2,
    brick_out,
    brick_in,
    spread,
    load_sem,
    small_sem,
    face_send_sem,
    face_recv_sem,
    pool_send_sem,
    pool_recv_sem,
    meta_send_sem,
    meta_recv_sem,
    side_send_sem,
    side_recv_sem,
    pair_send_sem,
    pair_recv_sem,
    hand_send_sem,
    hand_recv_sem,
    ready_sem,
):
    slots, edge = out_ref.shape[0], enc.shape[1]
    plane = edge * edge
    width = out_ref.shape[-1]
    half = edge // 2
    block = half**3
    per = child_ref.shape[0]
    bricks = LANES * per
    me = lax.axis_index("gx")
    member = lax.rem(me, LANES)
    group = lax.div(me, LANES)

    def peer(k):
        return me - member + (member ^ k)

    width = out_ref.shape[-1]
    loads = [[pltpu.make_async_copy(feat_hbm, feat, load_sem.at[0])]]
    for i, (src, dst) in enumerate(
        ((w1_hbm, w1), (w2_hbm, w2), (w3_hbm, w3), (w4_hbm, w4))
    ):
        loads.append([pltpu.make_async_copy(src, dst, load_sem.at[i + 1])])
    small = [
        pltpu.make_async_copy(src, dst, small_sem.at[i])
        for i, (src, dst) in enumerate(
            (
                (fine_nbr_hbm, fine_nbr),
                (fine_send_hbm, fine_send),
                (fine_parent_hbm, fine_parent),
                (child_hbm, child_ref),
                (nbr_hbm, nbr_ref),
            )
        )
    ]
    for copy in loads[0]:
        copy.start()
    for copy in small:
        copy.start()
    for copies in loads[1:]:
        for copy in copies:
            copy.start()

    def loaded(i):
        for copy in loads[i]:
            copy.wait()

    has_prev, has_next = me > 0, me < n - 1
    has_down, has_up = me >= LANES, me < n - LANES
    barrier = pltpu.get_barrier_semaphore()

    def greet(other):
        pl.semaphore_signal(barrier, inc=1, device_id={"gx": other}, device_id_type=MESH)

    for k in range(1, LANES):
        greet(peer(k))
    first = me - member
    sides = (
        (has_prev & (member == 0), me - 1),
        (has_next & (member == LANES - 1), me + 1),
        (has_down, me - LANES),
        (has_up, me + LANES),
    )
    peers = LANES - 1
    for there, other in sides:
        pl.when(there)(functools.partial(greet, other))
        peers = peers + jnp.where(there, 1, 0)

    def remote(src, dst, send, recv, other):
        return pltpu.make_async_remote_copy(
            src_ref=src,
            dst_ref=dst,
            send_sem=send,
            recv_sem=recv,
            device_id={"gx": other},
            device_id_type=MESH,
        )

    def face_copies(outgoing, incoming, phase):
        up = remote(
            outgoing.at[0],
            incoming.at[0],
            face_send_sem.at[0],
            face_recv_sem.at[phase, 0],
            me + 1,
        )
        down = remote(
            outgoing.at[1],
            incoming.at[1],
            face_send_sem.at[1],
            face_recv_sem.at[phase, 1],
            me - 1,
        )
        return up, down

    def start_pair(up, up_there, down, down_there):
        pl.when(up_there)(up.start)
        pl.when(down_there)(down.start)

    def finish_pair(up, up_there, down, down_there):
        @pl.when(down_there)
        def _():
            up.wait_recv()
            down.wait_send()

        @pl.when(up_there)
        def _():
            down.wait_recv()
            up.wait_send()


    cube = (edge, edge, edge, width)
    face = (edge, edge, width)
    base = edge
    high_x, low_x = ends.at[0], ends.at[1]
    padded = (edge + 2) * edge
    own_taps = range(9, 18)
    far_taps = (*range(9), *range(18, 27))
    zero_brick = jnp.zeros(cube, F32)
    zero_plane = jnp.zeros(face, F32)
    table[slots] = zero_brick
    enc[slots] = zero_brick

    def stage_faces(outgoing, source, last, s):
        up_from = jnp.where(fine_send[0, s] >= 0, s, slots)
        down_from = jnp.where(fine_send[1, s] >= 0, s, slots)
        rows = outgoing.shape[2]
        outgoing[0, s] = source[up_from, last].reshape(rows, width).astype(BF16)
        outgoing[1, s] = source[down_from, 0].reshape(rows, width).astype(BF16)

    loaded(0)
    for s in range(slots):
        table[s] = feat[s].astype(F32).reshape(cube)
    for copy in small:
        copy.wait()
    meta[member, 0:per, 0 : child_ref.shape[1]] = child_ref[...]
    meta[member, per : 2 * per, 0 : nbr_ref.shape[1]] = nbr_ref[...]
    for s in range(slots):
        stage_faces(face_out, table, edge - 1, s)
    halo1 = face_copies(face_out, face_in, 0)
    halo2 = face_copies(face_out2, face_in2, 1)
    halo3 = face_copies(face_out3, face_in3, 2)
    meta_copies = [
        remote(
            meta.at[member],
            meta.at[member],
            meta_send_sem,
            meta_recv_sem,
            peer(k),
        )
        for k in range(1, LANES)
    ]

    below[slots] = zero_plane
    above[slots] = zero_plane
    coarse[bricks] = zero_brick
    coarse2[bricks] = zero_brick
    low_x[3 * bricks] = zero_plane
    high_x[3 * bricks] = zero_plane
    children[LANES * slots] = jnp.zeros((block, width), F32)
    utab[slots] = jnp.zeros((half, half, edge, width), F32)
    ubelow[slots] = jnp.zeros((half, edge, width), F32)
    uabove[slots] = jnp.zeros((half, edge, width), F32)

    def assemble(target, side, centre, lower, upper, index, taps):
        for t in taps:
            dx, dy, dz = t // 9 - 1, t // 3 % 3 - 1, t % 3 - 1
            at = index(t)
            ys, zs = pick(dy, side), pick(dz, edge)
            if dx == 0:
                piece = centre[at, :, ys, zs, :]
            elif dx < 0:
                piece = lower[at, ys, zs, :][None]
            else:
                piece = upper[at, ys, zs, :][None]
            target[place(dx, side, 1), place(dy, side, 1), place(dz, edge, base), :] = piece

    def shift(store, row, source, x, y, count):
        rows = count * edge
        for dz in range(3):
            first = base + dz - 1
            piece = source[x, y, first : first + edge, :]
            store[dz, pl.ds(row, rows), :] = piece.reshape(rows, width).astype(BF16)

    def columns(store, starts, rows, offsets=(0, 1, 2)):
        return jnp.concatenate(
            [
                jnp.concatenate(
                    [store[dz, r + dy * edge : r + dy * edge + rows, :] for r in starts], axis=0
                )
                for dy in offsets
                for dz in range(3)
            ],
            axis=1,
        )

    def taps(weights, *sides):
        return jnp.concatenate([weights[dx] for dx in sides], axis=1)

    def dot(a, b):
        return jnp.dot(a, b, preferred_element_type=F32)

    def stepped(store, starts, rows, weight):
        third = 3 * width
        first, middle, last = (weight[i * third : (i + 1) * third, :] for i in range(3))
        both = jnp.concatenate(
            [
                jnp.concatenate([first, middle], axis=1),
                jnp.concatenate([jnp.zeros((third, width), BF16), last], axis=1),
            ],
            axis=0,
        )
        return dot(columns(store, starts, rows, (0, 1)), both)

    def tread(value, row, rows):
        return value[row : row + rows, 0:width] + value[row + edge : row + edge + rows, width:]

    def local_product(centre, indices, weights):
        rows = edge * padded
        for i, index in enumerate(indices):
            assemble(pad, edge, centre, None, None, index, own_taps)
            for x in range(edge):
                shift(zs, i * rows + x * padded, pad, x + 1, slice(None), edge + 2)
        count = len(indices)
        starts = [i * rows + x * padded for i in range(count) for x in range(edge)]
        two = dot(columns(zs, starts, plane), taps(weights, 0, 1))
        inner = [i * rows + padded for i in range(count)]
        third = stepped(zs, inner, (edge - 1) * padded, weights[2])
        results = []
        for i in range(count):
            totals = []
            for x in range(edge):
                at = (i * edge + x) * plane
                total = two[at : at + plane, width : 2 * width]
                if x > 0:
                    total = total + two[at - plane : at, 0:width]
                if x < edge - 1:
                    total = total + tread(third, (i * (edge - 1) + x) * padded, plane)
                totals.append(total)
            results.append(totals)
        return results

    def outer_planes(count, lower, upper, index_of, weights, store):
        @pl.loop(0, count)
        def _(j):
            assemble(pad, edge, None, lower, upper, index_of(j), far_taps)
            for side in range(2):
                row = pl.multiple_of((side * count + j) * padded, edge)
                shift(zfar, row, pad, side * (edge + 1), slice(None), edge + 2)

        for side in range(2):
            added = stepped(zfar, [side * count * padded], count * padded, weights[2 * side])
            for j in range(count):
                store(j, side, tread(added, j * padded, plane))

    def rounded(value):
        return jnp.maximum(value, 0.0).astype(BF16).astype(F32)

    def fine_index(b):
        def index(t):
            at = fine_nbr[b, t]
            return jnp.where(at >= 0, at, slots)

        return index

    def take_faces(incoming, low, high):
        shape = low.shape[1:]
        for s in range(slots):
            low[s] = incoming[0, s].astype(F32).reshape(shape)
            high[s] = incoming[1, s].astype(F32).reshape(shape)

    cells = half * half

    def pool_copy(k, b):
        source = pooled_out.at[member] if b is None else pooled.at[member, b]
        stage = 1 if b is None else 2 * (k - 1)
        return remote(
            source, source, pool_send_sem.at[stage], pool_recv_sem.at[stage], peer(k)
        )

    def all_pooled(stage):
        source = (pooled.at[0:2], pooled_out.at[0 : LANES - 1], pooled.at[0])[stage]
        return remote(
            source, source, pool_send_sem.at[stage], pool_recv_sem.at[stage], peer(1)
        )

    def pass_pooled():
        source = pooled.at[member ^ 2]
        return remote(source, source, pool_send_sem.at[0], pool_recv_sem.at[0], peer(1))

    def pool(value, count):
        pairs = value.reshape(count, 2, half, 2, edge, width)
        summed = (pairs[:, 0, :, 0] + pairs[:, 0, :, 1]) + (pairs[:, 1, :, 0] + pairs[:, 1, :, 1])
        half_z[0 : count * half * edge, :] = summed.reshape(count * half * edge, width)
        even = half_z[pl.ds(0, count * cells, stride=2), :]
        odd = half_z[pl.ds(1, count * cells, stride=2), :]
        return ((even + odd) * 0.125).astype(BF16)

    def side_copies(outgoing, incoming, phase):
        up = remote(
            outgoing,
            incoming.at[0],
            side_send_sem.at[min(phase, 1), 0],
            side_recv_sem.at[phase, 0],
            me + LANES,
        )
        down = remote(
            outgoing,
            incoming.at[1],
            side_send_sem.at[min(phase, 1), 1],
            side_recv_sem.at[phase, 1],
            me - LANES,
        )
        return up, down

    pl.semaphore_wait(barrier, peers)
    for k in range(1, LANES):
        pl.semaphore_signal(ready_sem, inc=1, device_id={"gx": peer(k)}, device_id_type=MESH)
    for copy in meta_copies:
        copy.start()
    start_pair(halo1[0], has_next, halo1[1], has_prev)
    loaded(1)

    at_once = GROUP if slots % GROUP == 0 else 1

    def encode(h):
        bricks_of = [at_once * h + i for i in range(at_once)]
        results = local_product(table, [fine_index(b) for b in bricks_of], w1)
        for b, totals in zip(bricks_of, results):
            opened[b, 0] = totals[0]
            opened[b, 1] = totals[edge - 1]
            value = rounded(jnp.concatenate(totals[1 : edge - 1], axis=0))
            value = value.reshape((edge - 2,) + face)
            enc[b, 1 : edge - 1] = value
            pooled[member, b] = pool(value[1 : edge - 3], half - 2)

    def send_pooled(b):
        for k in (2, 1):
            pool_copy(k, b).start()


    @pl.loop(0, slots // at_once)
    def _(h):
        encode(h)

    for b in range(slots):
        send_pooled(b)

    finish_pair(halo1[0], has_next, halo1[1], has_prev)
    take_faces(face_in, below, above)

    every_meta = meta.at[0 : LANES - 1]
    remote(every_meta, every_meta, meta_send_sem, meta_recv_sem, peer(1)).wait()
    to_smem = pltpu.make_async_copy(meta, meta_s, small_sem.at[0])
    to_smem.start()
    hop_meta = side_copies(meta, meta_far, 2)
    start_pair(hop_meta[0], has_up, hop_meta[1], has_down)
    def store_enc(b, side, added):
        enc[b, side * (edge - 1)] = rounded(opened[b, side] + added).reshape(face)

    outer_planes(slots, below, above, fine_index, w1, store_enc)
    for b in range(slots):
        for side in range(2):
            start = side * (edge - 2)
            value = pool(enc[b, start : start + 2], 1)
            pooled_out[member, b, side] = value
            own_out[b, side] = value
    for k in range(1, LANES):
        pool_copy(k, None).start()
    for s in range(slots):
        octant = lax.rem(jnp.maximum(fine_parent[s], 0), 8)
        side_out[s] = own_out[s, lax.div(octant, 4)]

    parity = lax.rem(member, 2)

    def face_to(side, h):
        return remote(
            side_out,
            side_in.at[side, parity, lax.div(member, 2)],
            side_send_sem.at[0, side],
            side_recv_sem.at[0, side],
            first + (LANES if side == 0 else -LANES) + 2 * h + parity,
        )

    def faces_to(side):
        for h in range(LANES // 2):
            face_to(side, h).start()

    def all_faces(side):
        return remote(
            side_in.at[side, 0],
            side_in.at[side, 0],
            side_send_sem.at[0, side],
            side_recv_sem.at[0, side],
            me + (LANES if side == 0 else -LANES),
        )

    def hand_over(side):
        block_of = side_in.at[side, parity]
        return remote(block_of, block_of, hand_send_sem.at[side], hand_recv_sem.at[side], peer(1))

    pl.semaphore_wait(ready_sem, LANES - 1)
    pl.when(has_up)(lambda: faces_to(0))
    pl.when(has_down)(lambda: faces_to(1))
    for s in range(slots):
        stage_faces(face_out2, enc, edge - 1, s)

    loaded(4)

    def decode_part(b):
        (totals,) = local_product(enc, [fine_index(b)], w4)
        acc[b] = jnp.concatenate(totals, axis=0)

    def run_decode(first, last):
        @pl.loop(first, last)
        def _(b):
            decode_part(b)

            @pl.when(b == max(slots - 2, 0))
            def _():
                all_pooled(2).wait_recv()
                pass_pooled().start()

    run_decode(0, slots)

    to_smem.wait()
    finish_pair(hop_meta[0], has_up, hop_meta[1], has_down)

    def far_to_smem(side):
        return pltpu.make_async_copy(meta_far.at[side], meta_far_s.at[side], small_sem.at[1 + side])

    pl.when(has_down)(lambda: far_to_smem(0).start())
    pl.when(has_up)(lambda: far_to_smem(1).start())
    for stage in range(2):
        all_pooled(stage).wait()
    all_pooled(2).wait_send()

    @pl.when(has_down)
    def _():
        all_faces(0).wait_recv()
        all_faces(1).wait_send()
        hand_over(0).start()

    @pl.when(has_up)
    def _():
        all_faces(1).wait_recv()
        all_faces(0).wait_send()
        hand_over(1).start()

    for lane in range(LANES):
        for s in range(slots):
            at = lane * slots + s
            children[at, cells : block - cells] = pooled[lane, s].astype(F32)
            children[at, 0:cells] = pooled_out[lane, s, 0].astype(F32)
            children[at, block - cells : block] = pooled_out[lane, s, 1].astype(F32)

    def child_at(child, start):
        at = jnp.clip(child - start * LANES * slots, 0, LANES * slots - 1)
        return jnp.where(child >= 0, at, LANES * slots)

    def halves(value, size):
        if size == 1:
            return value, 0
        return lax.div(value, size), lax.rem(value, size)

    @pl.loop(0, bricks)
    def _(j):
        lane, slot = halves(j, per)
        for o in range(8):
            at = child_at(meta_s[lane, slot, o], group)
            ox, oy, oz = o // 4 * half, o // 2 % 2 * half, o % 2 * half
            for x in range(half):
                for y in range(half):
                    row = (x * half + y) * half
                    coarse[j, ox + x, oy + y, oz : oz + half, :] = children[
                        at, row : row + half, :
                    ]

    def coarse_index(lane, slot, live):
        def index(t):
            value = meta_s[lane, per + slot, t]
            there = (value >= 0) & live
            if t // 9 == 1:
                return jnp.where(there, jnp.clip(value - group * bricks, 0, bricks - 1), bricks)
            at = jnp.clip(value - (group - 1) * bricks, 0, 3 * bricks - 1)
            return jnp.where(there, at, 3 * bricks)

        return index

    def keep_sides(source):
        for j in range(bricks):
            low_x[bricks + j] = source[j, 0]
            high_x[bricks + j] = source[j, edge - 1]

    own = bricks // 2
    def brick_of(i, odd):
        lane, slot = halves(i, per)
        return (2 * lane + odd) * per + slot

    def place_far(side):
        start = 2 * bricks * side
        for lane in range(LANES):
            for s in range(slots):
                far_children[side, lane * slots + s] = side_in[side, lane % 2, lane // 2, s].astype(F32)
        far_children[side, LANES * slots] = jnp.zeros((cells, width), F32)

        @pl.loop(0, bricks)
        def _(j):
            lane, slot = halves(j, per)
            for o in range(8):
                at = child_at(meta_far_s[side, lane, slot, o], group - 1 + 2 * side)
                oy, oz = o // 2 % 2 * half, o % 2 * half
                target = high_x if o // 4 else low_x
                for y in range(half):
                    target[start + j, oy + y, oz : oz + half, :] = far_children[
                        side, at, y * half : (y + 1) * half, :
                    ]

    def group_index(j):
        return coarse_index(*halves(j, per), True)

    keep_sides(coarse)
    def far_planes():
        pl.when(has_down)(lambda: hand_over(0).wait())
        pl.when(has_up)(lambda: hand_over(1).wait())
        pl.when(has_down)(lambda: far_to_smem(0).wait())
        pl.when(has_up)(lambda: far_to_smem(1).wait())
        pl.when(has_down)(lambda: place_far(0))
        pl.when(has_up)(lambda: place_far(1))


    loaded(2)

    def own_index(i):
        return group_index(brick_of(i, parity))

    def brick_copy(i):
        return remote(brick_out.at[i], brick_in.at[i], pair_send_sem, pair_recv_sem, peer(1))

    def planes_to(side, i, k):
        return remote(
            side_out2.at[i],
            side_in2.at[side, parity, i],
            side_send_sem.at[0, side],
            side_recv_sem.at[1, side],
            peer(k) + (LANES if side == 0 else -LANES),
        )

    def all_planes(side):
        return remote(
            side_in2.at[side],
            side_in2.at[side],
            side_send_sem.at[0, side],
            side_recv_sem.at[1, side],
            me + (LANES if side == 0 else -LANES),
        )

    @pl.loop(0, own)
    def _(i):
        index = own_index(i)
        (totals,) = local_product(coarse, [index], w2)
        opened[i, 0] = totals[0]
        opened[i, 1] = totals[edge - 1]
        value = jnp.maximum(jnp.concatenate(totals[1 : edge - 1], axis=0), 0.0).astype(BF16)
        brick_out[i, plane : (edge - 1) * plane] = value
        coarse2[brick_of(i, parity), 1 : edge - 1] = value.astype(F32).reshape(
            (edge - 2,) + face
        )
        pl.when(i == 0)(far_planes)
        assemble(pad, edge, None, high_x, low_x, index, far_taps)
        for side in range(2):
            shift(zfar, side * padded, pad, side * (edge + 1), slice(None), edge + 2)
        for side in range(2):
            added = stepped(zfar, [side * padded], padded, w2[2 * side])
            at = side * (edge - 1)
            value = jnp.maximum(opened[i, side] + tread(added, 0, plane), 0.0).astype(BF16)
            side_out2[i, side] = value
            brick_out[i, at * plane : (at + 1) * plane] = value
            coarse2[brick_of(i, parity), at] = value.astype(F32).reshape(face)

        def send_planes(side):
            for k in range(2):
                planes_to(side, i, k).start()

        pl.when(has_up)(lambda: send_planes(0))
        pl.when(has_down)(lambda: send_planes(1))
        brick_copy(i).start()

    loaded(3)

    part = half * edge
    strip = slots * part
    tall = half + 2
    column = tall * edge

    def parent_of(s):
        parent = fine_parent[s]
        safe = jnp.maximum(parent, 0)
        lane, slot = halves(jnp.clip(safe // 8 - group * bricks, 0, bricks - 1), per)
        octant = safe % 8
        ox, oy = lax.div(octant, 4), lax.rem(lax.div(octant, 2), 2)
        return lane, slot, ox, oy * half

    strips = 4
    span = width // strips

    @pl.loop(0, 3 * strips)
    def _(i):
        dz, strip_at = lax.div(i, strips), lax.rem(i, strips)
        rows = []
        for dy in range(3):
            start = pl.multiple_of((dy * 3 + dz) * width + strip_at * span, span)
            rows.append([w4[dx, pl.ds(start, span), :].astype(F32) for dx in range(3)])
        late = [r1 + r2 for r1, r2 in zip(rows[1], rows[2])]
        early = [r0 + r1 for r0, r1 in zip(rows[0], rows[1])]
        for py, parts in enumerate(((rows[0], late), (early, rows[2]))):
            for q, (a, b, c) in enumerate(parts):
                start = pl.multiple_of((q * 3 + dz) * width + strip_at * span, span)
                wup[py, pl.ds(start, span), :] = jnp.concatenate(
                    [b + c, a + b, a, c], axis=1
                ).astype(BF16)

    remote(brick_out, brick_in, pair_send_sem, pair_recv_sem, peer(1)).wait()
    for i in range(own):
        coarse2[brick_of(i, 1 - parity)] = brick_in[i].astype(F32).reshape(cube)
    keep_sides(coarse2)
    start_pair(halo2[0], has_next, halo2[1], has_prev)
    pad[0] = jnp.zeros(pad.shape[1:], F32)
    pad[edge + 1] = jnp.zeros(pad.shape[1:], F32)

    @pl.loop(0, slots)
    def _(s):
        lane, slot, ox, oy = parent_of(s)
        index = coarse_index(lane, slot, fine_parent[s] >= 0)
        assemble(pad, edge, coarse2, None, None, index, own_taps)
        for x in range(tall):
            row = pl.multiple_of((s * tall + x) * column, edge)
            shift(zq, row, pad, ox * half + x, pl.ds(oy, tall), tall)

    def starts_of(planes):
        return [(s * tall + x) * column for x in planes for s in range(slots)]

    two = dot(columns(zq, starts_of(range(half + 1)), part), taps(w3, 0, 1))
    third = stepped(
        zq, [(s * tall + 2) * column for s in range(slots)], half * column, w3[2]
    )
    for x in range(half):
        for s in range(slots):
            at = x * strip + s * part
            dacc[at : at + part, :] = (
                two[at : at + part, 0:width]
                + two[at + strip : at + strip + part, width : 2 * width]
                + tread(third, (s * half + x) * column, part)
            )

    def lift(s, x, value):
        piece = rounded(value)
        oz = lax.rem(jnp.maximum(fine_parent[s], 0), 2)
        start = x * 2 * part
        spread[s, pl.ds(start, part, stride=2), :] = piece
        spread[s, pl.ds(start + 1, part, stride=2), :] = piece
        for y in range(half):
            utab[s, x, y] = spread[s, pl.ds(start + (2 * y + oz) * edge, edge), :]

    for s in range(slots):
        for x in range(1, half - 1):
            lift(s, x, dacc[x * strip + s * part : x * strip + (s + 1) * part, :])
    @pl.when(has_down)
    def _():
        all_planes(0).wait_recv()
        all_planes(1).wait_send()

    @pl.when(has_up)
    def _():
        all_planes(1).wait_recv()
        all_planes(0).wait_send()

    for side in range(2):
        for odd in range(2):
            for i in range(own):
                at = 2 * bricks * side + (2 * (i // per) + odd) * per + i % per
                low_x[at] = side_in2[side, odd, i, 0].astype(F32).reshape(face)
                high_x[at] = side_in2[side, odd, i, 1].astype(F32).reshape(face)


    @pl.loop(0, slots)
    def _(s):
        lane, slot, ox, oy = parent_of(s)
        live = fine_parent[s] >= 0
        for k in range(9):
            value = meta_s[lane, per + slot, ox * 18 + k]
            at = jnp.clip(value - (group - 1) * bricks, 0, 3 * bricks - 1)
            at = jnp.where((value >= 0) & live, at, 3 * bricks)
            dy, dz = k // 3 - 1, k % 3 - 1
            piece = ends[ox, at, pick(dy, edge), pick(dz, edge), :]
            pad[0, place(dy, edge, 1), place(dz, edge, base), :] = piece
        row = pl.multiple_of(s * column, edge)
        shift(zfar, row, pad, 0, pl.ds(oy, tall), tall)

    far = dot(
        columns(zfar, [s * column for s in range(slots)], part),
        taps(w3, 0, 2),
    )
    picks[0] = far[:, 0:width]
    picks[1] = jnp.zeros((strip, width), F32)
    picks[2] = far[:, width : 2 * width]
    for s in range(slots):
        ox = parent_of(s)[2]
        rows = slice(s * part, (s + 1) * part)
        lift(s, 0, dacc[rows, :] + picks[ox, rows])
        last = (half - 1) * strip + s * part
        lift(s, half - 1, dacc[last : last + part, :] + picks[ox + 1, rows])
        stage_faces(face_out3, utab, half - 1, s)
    start_pair(halo3[0], has_next, halo3[1], has_prev)

    brick_rows = tall * column

    @pl.loop(0, slots)
    def _(b):
        assemble(upad, half, utab, None, None, fine_index(b), own_taps)
        for x in range(half):
            row = pl.multiple_of(b * brick_rows + (x + 1) * column, edge)
            shift(zu, row, upad, x + 1, slice(None), tall)

    def woven(zero, one):
        pair = jnp.stack(
            [zero.reshape(half, edge, width), one.reshape(half, edge, width)], axis=1
        )
        return pair.reshape(plane, width)

    inner = [b * brick_rows + (x + 1) * column for b in range(slots) for x in range(half)]
    direct, across = [], []
    for py in range(2):
        lhs = columns(zu, inner, part, (py, py + 1))
        direct.append(dot(lhs, wup[py, :, 0 : 2 * width]))
        across.append(dot(columns(zu, inner, part, (py, py + 1)), wup[py, :, 2 * width :]))

    for b in range(slots):
        for x in range(edge):
            i, px = x // 2, x % 2
            lanes = slice(px * width, (px + 1) * width)
            other = i - 1 + 2 * px
            sums = []
            for py in range(2):
                at = (b * half + i) * part
                value = direct[py][at : at + part, lanes]
                if 0 <= other < half:
                    at = (b * half + other) * part
                    value = value + across[py][at : at + part, lanes]
                sums.append(value)
            rows = slice(x * plane, (x + 1) * plane)
            total = acc[b, rows] + woven(*sums)
            if 0 <= other < half:
                out_ref[b, rows, :] = jnp.maximum(total, 0.0).astype(BF16)
            else:
                acc[b, rows] = total

    finish_pair(halo2[0], has_next, halo2[1], has_prev)
    take_faces(face_in2, below, above)

    def store_part(b, side, added):
        at = side * (edge - 1) * plane
        acc[b, at : at + plane] = acc[b, at : at + plane] + added

    outer_planes(slots, below, above, fine_index, w4, store_part)
    finish_pair(halo3[0], has_next, halo3[1], has_prev)
    take_faces(face_in3, ubelow, uabove)

    @pl.loop(0, slots)
    def _(b):
        assemble(upad, half, None, ubelow, uabove, fine_index(b), far_taps)
        for x in (0, half + 1):
            row = pl.multiple_of(b * brick_rows + x * column, edge)
            shift(zu, row, upad, x, slice(None), tall)

    for side in range(2):
        starts = [b * brick_rows + side * (half + 1) * column for b in range(slots)]
        lanes = slice((2 + side) * width, (3 + side) * width)
        sums = [dot(columns(zu, starts, part, (py, py + 1)), wup[py, :, lanes]) for py in range(2)]
        for b in range(slots):
            at = side * (edge - 1) * plane
            rows = slice(b * part, (b + 1) * part)
            total = acc[b, at : at + plane] + woven(sums[0][rows], sums[1][rows])
            out_ref[b, at : at + plane, :] = jnp.maximum(total, 0.0).astype(BF16)


def per_device(
    n,
    features,
    fine_nbr,
    fine_send,
    fine_parent,
    coarse_child,
    coarse_nbr,
    enc_fine_w,
    enc_coarse_w,
    dec_coarse_w,
    dec_fine_w,
):
    slots, edge, width = features.shape[0], features.shape[1], features.shape[-1]
    per = coarse_nbr.shape[0]
    bricks = LANES * per
    half = edge // 2
    plane = edge * edge
    voxels = edge**3
    padded = (edge + 2) * edge
    tall = half + 2
    rows = -(-2 * per // 8) * 8
    kernels = [
        w.reshape(3, 9 * width, width)
        for w in (enc_fine_w, enc_coarse_w, dec_coarse_w, dec_fine_w)
    ]
    vmem = pltpu.VMEM
    vmem_spec = pl.BlockSpec(memory_space=pltpu.VMEM)
    any_spec = pl.BlockSpec(memory_space=pl.ANY)
    cube = (edge, edge, edge, width)
    face = (edge, edge, width)
    dma = pltpu.SemaphoreType.DMA
    out = pl.pallas_call(
        functools.partial(kernel, n),
        out_shape=pltpu.VMEM((slots, voxels, width), BF16),
        in_specs=[any_spec] * 10,
        out_specs=vmem_spec,
        scratch_shapes=[
            pltpu.SMEM(fine_nbr.shape, jnp.int32),
            pltpu.SMEM(fine_send.shape[1:], jnp.int32),
            pltpu.SMEM(fine_parent.shape, jnp.int32),
            vmem(coarse_child.shape, jnp.int32),
            vmem(coarse_nbr.shape, jnp.int32),
            vmem((slots, voxels, width), BF16),
            *[vmem((3, 9 * width, width), BF16)] * 4,
            vmem((2, 6 * width, 4 * width), BF16),
            vmem((edge + 2, edge + 2, 3 * edge, width), F32),
            vmem((half + 2, half + 2, 3 * edge, width), F32),
            vmem((3, GROUP * edge * padded + edge, width), BF16),
            vmem((3, 2 * max(slots, bricks) * padded + edge, width), BF16),
            vmem((3, slots * tall * tall * edge + edge, width), BF16),
            vmem((3, slots * tall * tall * edge, width), BF16),
            vmem((max(slots, bricks), 2, plane, width), F32),
            vmem((slots, voxels, width), F32),
            vmem((half * slots * half * edge, width), F32),
            vmem((3, slots * half * edge, width), F32),
            vmem((slots + 1, half, half, edge, width), F32),
            vmem((slots + 1, half, edge, width), F32),
            vmem((slots + 1, half, edge, width), F32),
            vmem((slots + 1,) + cube, F32),
            vmem((slots + 1,) + cube, F32),
            vmem((slots + 1,) + face, F32),
            vmem((slots + 1,) + face, F32),
            vmem((2, slots, plane, width), BF16),
            vmem((2, slots, plane, width), BF16),
            vmem((2, slots, plane, width), BF16),
            vmem((2, slots, plane, width), BF16),
            vmem((2, slots, half * edge, width), BF16),
            vmem((2, slots, half * edge, width), BF16),
            vmem((half * half * edge, width), F32),
            vmem((LANES, slots, (half - 2) * half**2, width), BF16),
            vmem((LANES, slots, 2, half**2, width), BF16),
            vmem((slots, 2, half**2, width), BF16),
            vmem((LANES * slots + 1, half**3, width), F32),
            vmem((LANES, rows, 128), jnp.int32),
            pltpu.SMEM((LANES, rows, 128), jnp.int32),
            vmem((2, LANES, rows, 128), jnp.int32),
            pltpu.SMEM((2, LANES, rows, 128), jnp.int32),
            vmem((2, LANES * slots + 1, half**2, width), F32),
            vmem((bricks + 1,) + cube, F32),
            vmem((bricks + 1,) + cube, F32),
            vmem((2, 3 * bricks + 1) + face, F32),
            vmem((slots, half**2, width), BF16),
            vmem((2, 2, LANES // 2, slots, half**2, width), BF16),
            vmem((bricks // 2, 2, plane, width), BF16),
            vmem((2, 2, bricks // 2, 2, plane, width), BF16),
            vmem((bricks // 2, voxels, width), BF16),
            vmem((bricks // 2, voxels, width), BF16),
            vmem((slots, half * half * 2 * edge, width), F32),
            dma((5,)),
            dma((5,)),
            dma((2,)),
            dma((3, 2)),
            dma((3,)),
            dma((3,)),
            dma(()),
            dma(()),
            dma((2, 2)),
            dma((3, 2)),
            dma(()),
            dma(()),
            dma((2,)),
            dma((2,)),
            pltpu.SemaphoreType.REGULAR,
        ],
        compiler_params=pltpu.CompilerParams(
            collective_id=0, has_side_effects=True, vmem_limit_bytes=60 * 1024 * 1024
        ),
    )(
        fine_nbr,
        fine_send[0],
        fine_parent,
        coarse_child,
        coarse_nbr,
        features.reshape(slots, voxels, width),
        *kernels,
    )
    return out.reshape(features.shape)


def solution(mesh):
    lead = ("groups", "gx")
    placed = (
        P(lead, None, None, None, None),
        P(lead, None),
        P(lead, None, None),
        P(lead),
        P(lead, None),
        P(lead, None),
        P(),
        P(),
        P(),
        P(),
    )
    return jax.shard_map(
        functools.partial(per_device, mesh.shape["gx"]),
        mesh=mesh,
        in_specs=placed,
        out_specs=P(lead, None, None, None, None),
        check_vma=False,
    )
```
